32 devices in a mesh: ctx: 8 (over y, x, core), wt: 4 (over z).
Axes of the slice: x: 2, y: 2, z: 4, core: 2. Of those that a mesh axis runs over, the one named last changes fastest.
Arguments:
- tokens: bfloat16 [1, 1024, 2048], P(None, 'ctx'), may hold values from -6 to 6
- cotangent: bfloat16 [1, 1024, 2048], P(None, 'ctx'), may hold values from -6 to 6
- routes: int32 [1024, 8], P(('ctx', 'wt')), may hold values from 0 to 31, all different within a row; in each aligned block of 32 rows (0 to 31, 32 to 63, ...) at most 11 rows name the same one
- attn_gain: float32 [2048], replicated, may hold values from 0.5 to 1.5
- query_gain: float32 [128], replicated, may hold values from 0.25 to 1.75
- key_gain: float32 [128], replicated, may hold values from 0.25 to 1.75
- w_query: bfloat16 [2048, 4096], P(None, 'wt'), may hold values from -0.125 to 0.125
- key_weight: bfloat16 [2048, 512], P(None, 'wt'), may hold values from -0.125 to 0.125
- value_weight: bfloat16 [2048, 512], P(None, 'wt'), may hold values from -0.125 to 0.125
- w_output: bfloat16 [4096, 2048], P('wt'), may hold values from -1 to 1
- moe_gain: float32 [2048], replicated, may hold values from 0.5 to 1.5
- w_router: bfloat16 [2048, 32], replicated, may hold values from -0.0625 to 0.0625
- w_gate_up: bfloat16 [32, 2048, 1536], P(('ctx', 'wt')), may hold values from -0.125 to 0.125
- w_down: bfloat16 [32, 768, 2048], P(('ctx', 'wt')), may hold values from -0.875 to 0.875
Outputs:
- block_out: bfloat16 [1, 1024, 2048], P(None, 'ctx')
- tokens_grad: bfloat16 [1, 1024, 2048], P(None, 'ctx')
- attn_gain_grad: float32 [2048], replicated
- query_gain_grad: float32 [128], replicated
- key_gain_grad: float32 [128], replicated
- w_query_grad: float32 [2048, 4096], P('ctx', 'wt')
- w_key_grad: float32 [2048, 512], P('ctx', 'wt')
- w_value_grad: float32 [2048, 512], P('ctx', 'wt')
- w_output_grad: float32 [4096, 2048], P('wt', 'ctx')
- moe_gain_grad: float32 [2048], replicated
- w_router_grad: float32 [2048, 32], replicated
- w_gate_up_grad: float32 [32, 2048, 1536], P(('ctx', 'wt'))
- w_down_grad: float32 [32, 768, 2048], P(('ctx', 'wt'))
The draws below stay inside these ranges and needn't reach their ends.
Inputs may be any that keep to these rules, and one draw needn't show every extreme that they name: `routes`: each row names 8 different experts. In each aligned block of 32 rows (the rows of one device of ctx and wt together) no expert is named by more than 11 rows, and in every draw some block has an expert named by exactly 11 of its rows.
All inputs are finite; a program needn't handle non-finite values.
Results may differ from the reference program's by a relative error of at most 0.018.
Values may be sent and summed in bfloat16 or wider, within the bound.
No kernel may reach another device: no remote copies, remote signals or barrier semaphores. Data moves between devices by JAX's collectives and lax.ppermute only.
A program may use at most 192 MiB of HBM per device.

```python
import math
from functools import partial
import jax
import jax.numpy as jnp
import numpy as np
from jax import lax

MODEL_WIDTH = 2048
QUERY_HEADS = 32
KEY_VALUE_HEADS = 4
HEAD_SIZE = 128
FF = 768
TOP = 8
BLK = 64
SEQUENCE_COUNT = 1
EXPERTS = 32
SENDERS = 32
SEQUENCE_LENGTH = 1024
TOKEN_TOTAL = 1024
SHARE = 32
CAP = 11
N_CTX = 8


def level_of(key, extent, shards, smallest, high):
    def one(axis_at, shards_of):
        steps = jax.random.uniform(jax.random.fold_in(jax.random.fold_in(key, 6), axis_at), (shards_of,), jnp.float32, smallest / len(shards), high / len(shards))
        return jnp.repeat(jnp.exp(steps), extent[axis_at] // shards_of).reshape((-1,) + (1,) * (len(extent) - axis_at - 1))

    gain = one(*shards[0])
    for cut in shards[1:]:
        gain = gain * one(*cut)
    return gain


def routed_block(key, own, number, rows, number_of, top, most, lean):
    sequence = jax.random.permutation(key, number_of)
    heavy_load, usual = load_shares(number_of, rows * top, most, lean, True), load_shares(number_of, rows * top, most, lean, False)
    places = jnp.arange(number_of)

    def named(tallies, rotation):
        used = int((tallies > 0).sum())
        fixed = max(1, used // 4)
        shifted = fixed + (places - fixed + rotation * (used - fixed)) % max(1, number_of - fixed)
        return jnp.zeros((number_of,), jnp.int32).at[sequence[jnp.where(places < fixed, places, shifted)]].set(jnp.asarray(tallies, jnp.int32))

    tallies = jnp.where(number % 4 == 0, named(heavy_load, number // 4), named(usual, number - number // 4 - 1))
    mixed = jax.random.permutation(jax.random.fold_in(own, 3), number_of)
    giver, taker = mixed[0:number_of // 2 * 2:2], mixed[1:number_of // 2 * 2:2]
    slack = jnp.minimum(tallies[giver] - 1, most - tallies[taker]) // 2
    slack = jnp.where((giver == sequence[0]) | (taker == sequence[0]) | (tallies[taker] == 0), 0, jnp.maximum(slack, 0))
    shifted = jax.random.randint(jax.random.fold_in(own, 4), (number_of // 2,), 0, 1 << 20) % (slack + 1)
    tallies = tallies.at[giver].add(-shifted).at[taker].add(shifted)
    members = jnp.searchsorted(jnp.cumsum(tallies), jnp.arange(rows * top), side="right").astype(jnp.int32)
    table = members.reshape(top, rows).T
    table = table[jax.random.permutation(jax.random.fold_in(own, 1), rows)]
    rotation = jax.random.randint(jax.random.fold_in(own, 2), (rows, 1), 0, top)
    return jnp.take_along_axis(table, (jnp.arange(top)[None, :] + rotation) % top, axis=1)


def load_shares(number_of, total, reach, slope, full):
    portions = [(1 << 20) // math.isqrt(grade ** slope) + 1 for grade in range(1, number_of + 1)]
    largest = reach if full else min(reach, max(-(-total // number_of), total * portions[0] // sum(portions)))
    least = 1 if total - largest >= number_of - 1 else 0
    given, surplus = [largest] + [least] * (number_of - 1), total - largest - least * (number_of - 1)
    while surplus > 0:
        free = [i for i in range(1, number_of) if given[i] < largest] or [i for i in range(1, number_of) if given[i] < reach]
        mass, remaining = sum([portions[i] for i in free]), surplus
        for i in free:
            extra = min(reach - given[i], max(1, remaining * portions[i] // mass), surplus)
            given[i] = given[i] + extra
            surplus = surplus - extra
    return np.array(given)


def centred(stream_key, extent, spread, bound, shards=(), held_as=jnp.bfloat16):
    factor_of = level_of(stream_key, extent, shards, -0.22, 0.18) if shards else 1.0
    values = jax.random.normal(stream_key, extent, jnp.float32) * spread * factor_of
    return jnp.minimum(jnp.maximum(values, -bound), bound).astype(held_as)


def setup_inputs(seed: int = 0) -> dict:
    key_list = jax.random.split(jax.random.key(seed), 15)
    tokens = centred(key_list[0], (SEQUENCE_COUNT, SEQUENCE_LENGTH, MODEL_WIDTH), 1.0, 6.0, ((1, 8),))
    cotangent = centred(key_list[1], (SEQUENCE_COUNT, SEQUENCE_LENGTH, MODEL_WIDTH), 1.0, 6.0, ((1, 8),))
    routes_keys = jax.random.split(jax.random.fold_in(key_list[2], 1), TOKEN_TOTAL // SHARE)
    routes_turns = jax.random.permutation(jax.random.fold_in(key_list[2], 3), TOKEN_TOTAL // SHARE)
    routes = jax.vmap(lambda own, number: routed_block(jax.random.fold_in(key_list[2], 2), own, number, SHARE, EXPERTS, TOP, CAP, 2))(routes_keys, routes_turns).reshape((TOKEN_TOTAL, TOP))
    attn_gain = jnp.clip(1.0 + 0.1 * jax.random.normal(key_list[3], (MODEL_WIDTH,), jnp.float32), 0.5, 1.5)
    query_gain = jnp.clip(1.0 + 0.15 * jax.random.normal(key_list[4], (HEAD_SIZE,), jnp.float32), 0.25, 1.75)
    key_gain = jnp.clip(1.0 + 0.15 * jax.random.normal(key_list[5], (HEAD_SIZE,), jnp.float32), 0.25, 1.75)
    w_query = centred(key_list[6], (MODEL_WIDTH, QUERY_HEADS * HEAD_SIZE), MODEL_WIDTH ** -0.5, 0.125, ((1, 4),))
    key_weight = centred(key_list[7], (MODEL_WIDTH, KEY_VALUE_HEADS * HEAD_SIZE), MODEL_WIDTH ** -0.5, 0.125, ((1, 4),))
    value_weight = centred(key_list[8], (MODEL_WIDTH, KEY_VALUE_HEADS * HEAD_SIZE), MODEL_WIDTH ** -0.5, 0.125, ((1, 4),))
    w_output = centred(key_list[9], (QUERY_HEADS * HEAD_SIZE, MODEL_WIDTH), (QUERY_HEADS * HEAD_SIZE // 128) ** -0.5, 1.0, ((0, 4),))
    moe_gain = jnp.clip(1.0 + 0.1 * jax.random.normal(key_list[10], (MODEL_WIDTH,), jnp.float32), 0.5, 1.5)
    w_router = centred(key_list[11], (MODEL_WIDTH, EXPERTS), (4 * MODEL_WIDTH) ** -0.5, 0.0625)
    w_gate_up = centred(key_list[12], (EXPERTS, MODEL_WIDTH, 2 * FF), MODEL_WIDTH ** -0.5, 0.125, ((0, 32),))
    w_down = centred(key_list[13], (EXPERTS, FF, MODEL_WIDTH), (FF // 16) ** -0.5, 0.875, ((0, 32),))
    return dict(tokens=tokens, cotangent=cotangent, routes=routes, attn_gain=attn_gain, query_gain=query_gain, key_gain=key_gain, w_query=w_query, key_weight=key_weight, value_weight=value_weight, w_output=w_output, moe_gain=moe_gain, w_router=w_router, w_gate_up=w_gate_up, w_down=w_down)


epsilon = 1e-06
rope_base = 1000000.0
highest_precision = lax.Precision.HIGHEST

@jax.custom_vjp
def lower_precision(v):
    return lax.optimization_barrier(v.astype(jnp.bfloat16)).astype(jnp.float32)

@jax.custom_vjp
def lower_backward(v):
    return v

def low_keep(v):
    return (lower_precision(v), None)

def low_pass(kept, grad):
    return (grad,)

def back_keep(v):
    return (v, None)

def back_low(kept, grad):
    return (lower_precision(grad),)
lower_precision.defvjp(low_keep, low_pass)
lower_backward.defvjp(back_keep, back_low)

def rms_scale(value_matrix):
    return lax.rsqrt(lax.optimization_barrier(jnp.mean(value_matrix * value_matrix, axis=-1, keepdims=True)) + epsilon)

def mirrored(device, offset, groups, block_len):
    which_block = jnp.where(offset < block_len, device, 2 * groups - 1 - device)
    return which_block * block_len + offset % block_len

def rope_tables(positions, head_dim):
    halfway = head_dim // 2
    frequency = rope_base ** (-2.0 * jnp.arange(halfway, dtype=jnp.float32) / head_dim)
    angles = positions.astype(jnp.float32)[:, None] * frequency[None, :]
    return (jnp.cos(angles), jnp.sin(angles))

def rotate(value_matrix, cosine_table, sine_table):
    halfway = value_matrix.shape[-1] // 2
    leading = value_matrix[..., :halfway]
    trailing = value_matrix[..., halfway:]
    cosine = cosine_table[:, None, :]
    sine_part = sine_table[:, None, :]
    return jnp.concatenate([leading * cosine - trailing * sine_part, trailing * cosine + leading * sine_part], axis=-1)

def to_devices(array):
    trailing = array.shape[2]
    return array.reshape(SEQUENCE_COUNT, N_CTX, 2 * BLK, trailing).transpose(1, 0, 2, 3).reshape(TOKEN_TOTAL, trailing)

def from_devices(array):
    trailing = array.shape[1]
    return array.reshape(N_CTX, SEQUENCE_COUNT, 2 * BLK, trailing).transpose(1, 0, 2, 3).reshape(SEQUENCE_COUNT, SEQUENCE_LENGTH, trailing)

def each_sequence(array):
    heads = array.shape[1]
    return array.reshape(N_CTX, SEQUENCE_COUNT, 2 * BLK, heads, HEAD_SIZE).transpose(1, 3, 0, 2, 4).reshape(SEQUENCE_COUNT, heads, SEQUENCE_LENGTH, HEAD_SIZE)

def attend_one(query_block, key_block, value_block, positions):
    scores = lower_backward(jnp.einsum('gqd,kd->gqk', query_block, key_block, precision=highest_precision) * HEAD_SIZE ** (-0.5))
    allowed = positions[None, :] <= positions[:, None]
    scores = jnp.where(allowed[None], scores, -1e+30)
    probs = lower_precision(jax.nn.softmax(scores, axis=-1))
    return jnp.einsum('gqk,kd->gqd', probs, value_block, precision=highest_precision)

def layer(routes, tokens, attn_gain, query_gain, key_gain, w_query, key_weight, value_weight, w_output, moe_gain, w_router, w_gate_up, w_down):
    rows_all = to_devices(tokens)
    first_normed = lower_precision(rows_all * rms_scale(rows_all) * attn_gain)
    raw_query = lower_backward(jnp.dot(first_normed, w_query, precision=highest_precision)).reshape(TOKEN_TOTAL, QUERY_HEADS, HEAD_SIZE)
    unnormed_key = lower_backward(jnp.dot(first_normed, key_weight, precision=highest_precision)).reshape(TOKEN_TOTAL, KEY_VALUE_HEADS, HEAD_SIZE)
    value_matrix = lower_backward(lower_precision(jnp.dot(first_normed, value_weight, precision=highest_precision))).reshape(TOKEN_TOTAL, KEY_VALUE_HEADS, HEAD_SIZE)
    places = jnp.arange(SEQUENCE_LENGTH, dtype=jnp.int32)
    seq_positions = mirrored(places // (2 * BLK), places % (2 * BLK), N_CTX, BLK)
    token_positions = jnp.tile(seq_positions.reshape(N_CTX, 1, 2 * BLK), (1, SEQUENCE_COUNT, 1)).reshape(TOKEN_TOTAL)
    cosine_table, sine_table = rope_tables(token_positions, HEAD_SIZE)
    query_matrix = lower_backward(lower_precision(rotate(raw_query * rms_scale(raw_query) * query_gain, cosine_table, sine_table)))
    key_matrix = lower_backward(lower_precision(rotate(unnormed_key * rms_scale(unnormed_key) * key_gain, cosine_table, sine_table)))
    query_sequence = each_sequence(query_matrix).reshape(SEQUENCE_COUNT * KEY_VALUE_HEADS, QUERY_HEADS // KEY_VALUE_HEADS, SEQUENCE_LENGTH, HEAD_SIZE)
    key_sequence = each_sequence(key_matrix).reshape(SEQUENCE_COUNT * KEY_VALUE_HEADS, SEQUENCE_LENGTH, HEAD_SIZE)
    value_sequence = each_sequence(value_matrix).reshape(SEQUENCE_COUNT * KEY_VALUE_HEADS, SEQUENCE_LENGTH, HEAD_SIZE)

    def attend_item(item):
        return attend_one(item[0], item[1], item[2], seq_positions)
    attended = lax.map(jax.checkpoint(attend_item), (query_sequence, key_sequence, value_sequence))
    attended = attended.reshape(SEQUENCE_COUNT, QUERY_HEADS, N_CTX, 2 * BLK, HEAD_SIZE).transpose(2, 0, 3, 1, 4).reshape(TOKEN_TOTAL, QUERY_HEADS * HEAD_SIZE)
    attn_rows = lower_backward(lower_precision(attended))
    middle = rows_all + lower_backward(jnp.dot(attn_rows, w_output, precision=highest_precision))
    normed_two = lower_precision(middle * rms_scale(middle) * moe_gain)
    logits = jnp.dot(normed_two, w_router, precision=highest_precision)
    expert_ids = jnp.arange(EXPERTS, dtype=jnp.int32)
    chosen_int = (routes[:, :, None] == expert_ids[None, None, :]).astype(jnp.int32)
    picked = lax.optimization_barrier(jnp.sum(chosen_int.astype(logits.dtype) * logits[:, None, :], axis=-1))
    route_weights = jax.nn.softmax(picked, axis=-1)
    flat = chosen_int.reshape(SENDERS, SHARE * TOP, EXPERTS)
    before = jnp.cumsum(flat, axis=1) - flat
    slot_index = lax.optimization_barrier(jnp.sum(before * flat, axis=-1)).astype(jnp.int32)
    targets = (routes.reshape(SENDERS, SHARE * TOP) * CAP + slot_index).astype(jnp.int32)
    normed_blocks = normed_two.reshape(SENDERS, SHARE, MODEL_WIDTH)

    def place(block_rows, block_targets):
        empty = jnp.zeros((EXPERTS * CAP, MODEL_WIDTH), block_rows.dtype)
        return empty.at[block_targets].add(jnp.repeat(block_rows, TOP, axis=0))
    sent = jax.vmap(place)(normed_blocks, targets)
    arrived = lower_backward(sent.reshape(SENDERS, EXPERTS, CAP, MODEL_WIDTH).transpose(1, 0, 2, 3).reshape(EXPERTS, SENDERS * CAP, MODEL_WIDTH))

    def expert_apply(item):
        rows_in, gate_up_weight, down_weight = item
        gate_up = lower_backward(jnp.dot(rows_in, gate_up_weight, precision=highest_precision))
        hidden = lower_precision(jax.nn.silu(gate_up[:, :FF]) * gate_up[:, FF:])
        return lower_backward(lower_precision(jnp.dot(hidden, down_weight, precision=highest_precision)))
    outputs = lax.map(jax.checkpoint(expert_apply), (arrived, w_gate_up, w_down))
    returned = outputs.reshape(EXPERTS, SENDERS, CAP, MODEL_WIDTH).transpose(1, 0, 2, 3).reshape(SENDERS, EXPERTS * CAP, MODEL_WIDTH)

    def take_rows(block_rows, block_targets):
        return block_rows[block_targets]
    picked_rows = jax.vmap(take_rows)(returned, targets).reshape(TOKEN_TOTAL, TOP, MODEL_WIDTH)
    moe_rows = lax.optimization_barrier(jnp.sum(route_weights[:, :, None] * picked_rows, axis=1))
    return from_devices(middle + moe_rows)

def reference(tokens, cotangent, routes, attn_gain, query_gain, key_gain, w_query, key_weight, value_weight, w_output, moe_gain, w_router, w_gate_up, w_down):
    params = (tokens, attn_gain, query_gain, key_gain, w_query, key_weight, value_weight, w_output, moe_gain, w_router, w_gate_up, w_down)
    floats = tuple((item.astype(jnp.float32) for item in params))
    output, pullback = jax.vjp(partial(layer, routes), *floats)
    grads = pullback(cotangent.astype(jnp.float32))
    return (output.astype(jnp.bfloat16), grads[0].astype(jnp.bfloat16), grads[1], grads[2], grads[3], grads[4], grads[5], grads[6], grads[7], grads[8], grads[9], grads[10], grads[11])
```

```python
import functools

import jax
import jax.numpy as jnp
from jax import lax
from jax.experimental import pallas as pl
from jax.experimental.pallas import tpu as pltpu
from jax.sharding import PartitionSpec as P

epsilon = 1e-06
rope_base = 1000000.0
low = jnp.bfloat16
full = jnp.float32
vmem_bytes = 60 * 1024 * 1024

in_vmem = pl.BlockSpec(memory_space=pltpu.VMEM)
in_smem = pl.BlockSpec(memory_space=pltpu.SMEM)
in_any = pl.BlockSpec(memory_space=pl.ANY)


def dot(a, b, a_dim=1, b_dim=0):
    return lax.dot_general(a, b, (((a_dim,), (b_dim,)), ((), ())), preferred_element_type=full)


def swap(array, axis, mask):
    count = lax.axis_size(axis)
    return lax.ppermute(array, axis, [(i, i ^ mask) for i in range(count)])


def fence(*values):
    return lax.optimization_barrier(values)


def shape_of(shape, dtype):
    return jax.ShapeDtypeStruct(tuple(shape), dtype)


def kernel_call(kernel, outs, ins, args, **more):
    return pl.pallas_call(
        kernel,
        out_shape=outs,
        in_specs=ins,
        compiler_params=pltpu.CompilerParams(vmem_limit_bytes=vmem_bytes),
        **more,
    )(*args)


def rms_scale(value_matrix):
    return lax.rsqrt(jnp.mean(value_matrix * value_matrix, axis=-1, keepdims=True) + epsilon)


def norm_back(grad_out, value_matrix, inverse, gain_vec):
    scaled = grad_out * gain_vec
    inner_mean = jnp.mean(scaled * value_matrix, axis=-1, keepdims=True)
    return inverse * (scaled - value_matrix * inverse * inverse * inner_mean)


def mirrored(device, offset, groups, block_len):
    which_block = jnp.where(offset < block_len, device, 2 * groups - 1 - device)
    return which_block * block_len + offset % block_len


def rotate(value_matrix, cosine, sine):
    return value_matrix * cosine + pltpu.roll(value_matrix, value_matrix.shape[-1] // 2, 1) * sine


def front_kernel(
    index_ref, x_ref, gain_ref, kw_ref, vw_ref, kgain_ref, cos_ref, sin_ref,
    rows_ref, normed_ref, inv_ref, raw_ref, kv_ref,
):
    blocks, share, _ = x_ref.shape
    for i in range(blocks):
        x_low = x_ref[index_ref[0] ^ i]
        rows_ref[i] = x_low
        x = x_low.astype(full)
        inverse = rms_scale(x)
        inv_ref[i * share : (i + 1) * share] = inverse
        normed_ref[i * share : (i + 1) * share] = (x * inverse * gain_ref[...]).astype(low)
    normed = normed_ref[...]
    raw = dot(normed, kw_ref[...])
    raw_ref[...] = raw
    head_dim = raw.shape[1]
    turned = rotate(raw * rms_scale(raw) * kgain_ref[...], cos_ref[...], sin_ref[...])
    kv_ref[:, :head_dim] = turned.astype(low)
    kv_ref[:, head_dim:] = dot(normed, vw_ref[...]).astype(low)


def query_kernel(normed_ref, w_ref, gain_ref, cos_ref, sin_ref, raw_ref, q_ref):
    rows, head_dim = cos_ref.shape
    raw = dot(normed_ref[...], w_ref[...])
    raw_ref[...] = raw
    for h in range(raw.shape[1] // head_dim):
        one = raw[:, h * head_dim : (h + 1) * head_dim]
        turned = rotate(one * rms_scale(one) * gain_ref[...], cos_ref[...], sin_ref[...])
        q_ref[h * rows : (h + 1) * rows] = turned.astype(low)


def message_kernel(index_ref, g_ref, *refs):
    blocks, share, width = g_ref.shape
    mask_refs, out_refs = refs[:blocks], refs[blocks:]
    each = blocks // len(out_refs)
    for i in range(blocks):
        out_ref = out_refs[i // each]
        rows = slice(i % each * share, (i % each + 1) * share)
        out_ref[rows, :width] = g_ref[index_ref[0] ^ i]
        out_ref[rows, width:] = mask_refs[i][...]


def attend_kernel(scale, pieces, qpos_ref, kpos_ref, q_ref, w_ref, *refs):
    kv_refs = refs[:pieces]
    rows_ref, probs_ref, keys_ref, values_ref, own_ref, *rest_refs, attn, weight, sem = refs[pieces:]
    step = pl.program_id(0)
    tokens, head_dim = kv_refs[0].shape[0], kv_refs[0].shape[1] // 2
    copy = pltpu.make_async_copy(w_ref, weight, sem)

    @pl.when(step == 0)
    def _():
        copy.start()
        for i, ref in enumerate(kv_refs):
            keys_ref[i * tokens : (i + 1) * tokens] = ref[:, :head_dim]
            values_ref[i * tokens : (i + 1) * tokens] = ref[:, head_dim:]

    scores = dot(q_ref[...], keys_ref[...], 1, 1) * scale
    scores = jnp.where(kpos_ref[...] <= qpos_ref[...], scores, -1e30)
    weights = jnp.exp(scores - jnp.max(scores, axis=-1, keepdims=True))
    probs = (weights / jnp.sum(weights, axis=-1, keepdims=True)).astype(low)
    probs_ref[...] = probs
    out = dot(probs, values_ref[...]).astype(low)
    heads = out.shape[0] // tokens
    attn[step] = jnp.concatenate([out[h * tokens : (h + 1) * tokens] for h in range(heads)], axis=1)

    @pl.when(step == pl.num_programs(0) - 1)
    def _():
        copy.wait()
        for i in range(attn.shape[0]):
            rows_ref[:, i * heads * head_dim : (i + 1) * heads * head_dim] = attn[i]
        total = dot(rows_ref[...], weight[...])
        share = own_ref.shape[0]
        own_ref[...] = total[:share]
        for i, ref in enumerate(rest_refs):
            ref[...] = total[(i + 1) * share : (i + 2) * share].astype(low)


def expert_kernel(
    tiles, expert_ref, row_near, row_far, grad_near, grad_far, router_ref, gu_any, down_any,
    near_ref, far_ref, moe_near_ref, moe_far_ref, x_ref, hidden_ref, dgu_ref, deo_ref,
    x_tile, g_tile, gu, down, sems,
):
    step = pl.program_id(0)
    width = x_tile.shape[1]
    ffw = down.shape[0]
    experts = router_ref.shape[1]
    copy_gu = pltpu.make_async_copy(gu_any.at[0], gu, sems.at[0])
    copy_down = pltpu.make_async_copy(down_any.at[0], down, sems.at[1])

    @pl.when(step == 0)
    def _():
        copy_gu.start()
        copy_down.start()

    @pl.when(step < tiles // 2)
    def _():
        x_tile[...] = row_near[...]
        g_tile[...] = grad_near[...]

    @pl.when(step >= tiles // 2)
    def _():
        x_tile[...] = row_far[...]
        g_tile[...] = grad_far[...]

    x = x_tile[...]
    x_ref[...] = x
    g = g_tile[:, :width].astype(full)
    chosen = g_tile[:, width:][:, :experts].astype(full) > 0.5
    logits = jnp.where(chosen, dot(x, router_ref[...]), -1e30)
    shifted = jnp.exp(logits - jnp.max(logits, axis=-1, keepdims=True))
    shifted = jnp.where(chosen, shifted, 0.0)
    mine = lax.broadcasted_iota(jnp.int32, shifted.shape, 1) == expert_ref[0]
    own = jnp.sum(jnp.where(mine, shifted, 0.0), axis=-1, keepdims=True) / jnp.sum(
        shifted, axis=-1, keepdims=True
    )
    deo = (g * own).astype(low)
    deo_ref[...] = deo

    @pl.when(step == 0)
    def _():
        copy_gu.wait()

    gate_up = dot(x, gu[...])

    @pl.when(step == 0)
    def _():
        copy_down.wait()

    gate, up = gate_up[:, :ffw], gate_up[:, ffw:]
    dhid = dot(deo, down[...], 1, 1)
    sig = jax.nn.sigmoid(gate)
    silu = gate * sig
    hidden = (silu * up).astype(low)
    hidden_ref[...] = hidden
    dgate = (dhid * up * (sig + silu * (1.0 - sig))).astype(low)
    dup = (dhid * silu).astype(low)
    dgu_ref[:, :ffw] = dgate
    dgu_ref[:, ffw:] = dup
    out = dot(hidden, down[...]).astype(low).astype(full)
    dlw = jnp.sum(out * g, axis=-1, keepdims=True)
    moe = (out * own).astype(low)
    back = (dot(dgate, gu[:, :ffw], 1, 1) + dot(dup, gu[:, ffw:], 1, 1)).astype(low)
    high = dlw.astype(low)
    rest = (dlw - high.astype(full)).astype(low).astype(full)
    cols = near_ref.shape[1] - width
    lane = lax.broadcasted_iota(jnp.int32, (x.shape[0], cols), 1)
    extra = jnp.where(lane == expert_ref[0], high.astype(full), 0.0)
    extra = jnp.where(lane == experts + expert_ref[0], rest, extra).astype(low)

    def store(row_ref, moe_ref):
        row_ref[:, :width] = back
        row_ref[:, width:] = extra
        moe_ref[...] = moe

    @pl.when(step < tiles // 2)
    def _():
        store(near_ref, moe_near_ref)

    @pl.when(step >= tiles // 2)
    def _():
        store(far_ref, moe_far_ref)


def run_expert(part, part_count, rows, grads, w_router, w_gate_up, w_down, expert, into, cols):
    half_rows, width = rows[0].shape
    tile = min(256, half_rows)
    near = half_rows // tile
    tiles = 2 * near
    ffw = w_down.shape[1]
    extra = grads[0].shape[1]
    everything = 2 * half_rows * part_count
    offset = part * tiles
    outs = [
        shape_of((half_rows, cols), low),
        shape_of((half_rows, cols), low),
        shape_of((half_rows, width), low),
        shape_of((half_rows, width), low),
        shape_of((everything, width), low),
        shape_of((everything, ffw), low),
        shape_of((everything, 2 * ffw), low),
        shape_of((everything, width), low),
    ]
    near_map = lambda i: (jnp.minimum(i, near - 1), 0)
    far_map = lambda i: (jnp.maximum(i - near, 0), 0)
    all_map = lambda i: (i + offset, 0)
    out_specs = [
        pl.BlockSpec((tile, cols), near_map),
        pl.BlockSpec((tile, cols), far_map),
        pl.BlockSpec((tile, width), near_map),
        pl.BlockSpec((tile, width), far_map),
        pl.BlockSpec((tile, width), all_map),
        pl.BlockSpec((tile, ffw), all_map),
        pl.BlockSpec((tile, 2 * ffw), all_map),
        pl.BlockSpec((tile, width), all_map),
    ]
    ins = [
        in_smem,
        pl.BlockSpec((tile, width), near_map),
        pl.BlockSpec((tile, width), far_map),
        pl.BlockSpec((tile, extra), near_map),
        pl.BlockSpec((tile, extra), far_map),
        pl.BlockSpec(w_router.shape, lambda i: (0, 0)),
        in_any,
        in_any,
    ]
    args = [expert.reshape(1), *rows, *grads, w_router, w_gate_up, w_down]
    lead = len(args)
    aliases = {}
    if into is not None:
        for i, array in enumerate(into):
            aliases[len(args)] = 4 + i
            ins.append(in_any)
            args.append(array)

    def body(*refs):
        expert_kernel(tiles, *refs[:lead], *refs[len(args) :])

    return kernel_call(
        body,
        outs,
        ins,
        args,
        grid=(tiles,),
        out_specs=out_specs,
        scratch_shapes=[
            pltpu.VMEM((tile, width), low),
            pltpu.VMEM((tile, extra), low),
            pltpu.VMEM(w_gate_up.shape[1:], low),
            pltpu.VMEM(w_down.shape[1:], low),
            pltpu.SemaphoreType.DMA((2,)),
        ],
        input_output_aliases=aliases,
    )


def attend_back_kernel(scale, pieces, w_ref, probs_ref, keys_ref, values_ref, q_ref, raw_ref,
                       gain_ref, cos_ref, sin_ref, *refs):
    da_refs = refs[:pieces]
    kv_near_ref, kv_far_ref, dq_ref, part_ref, da_ref, logits_ref, acc = refs[pieces:]
    step = pl.program_id(0)
    tokens, head_dim = cos_ref.shape
    share = da_refs[0].shape[0]
    width = da_ref.shape[1]

    @pl.when(step == 0)
    def _():
        for i, ref in enumerate(da_refs):
            da_ref[i * share : (i + 1) * share] = ref[:, :width]
            logits_ref[i * share : (i + 1) * share] = ref[:, width:]
        acc[...] = jnp.zeros_like(acc)
        part_ref[...] = jnp.zeros_like(part_ref)

    dattn = dot(da_ref[...], w_ref[...], 1, 1).astype(low)
    heads = dattn.shape[1] // head_dim
    out_grad = jnp.concatenate(
        [dattn[:, h * head_dim : (h + 1) * head_dim] for h in range(heads)], axis=0
    )
    probs_low = probs_ref[...]
    probs = probs_low.astype(full)
    prob_grad = dot(out_grad, values_ref[...], 1, 1)
    inner = jnp.sum(probs * prob_grad, axis=-1, keepdims=True)
    score_grad = (probs * (prob_grad - inner)).astype(low)
    query_grad = (dot(score_grad, keys_ref[...]) * scale).astype(low).astype(full)
    acc[:, :head_dim] += dot(score_grad, q_ref[...], 0, 0)
    acc[:, head_dim:] += dot(probs_low, out_grad, 0, 0)
    gain = gain_ref[...]
    part = part_ref[...]
    for h in range(heads):
        cols = slice(h * head_dim, (h + 1) * head_dim)
        turned = rotate(query_grad[h * tokens : (h + 1) * tokens], cos_ref[...], -sin_ref[...])
        raw = raw_ref[:, cols]
        inverse = rms_scale(raw)
        part = part + jnp.sum(turned * raw * inverse, axis=0, keepdims=True)
        dq_ref[:, cols] = norm_back(turned, raw, inverse, gain).astype(low)
    part_ref[...] = part

    @pl.when(step == pl.num_programs(0) - 1)
    def _():
        near = kv_near_ref.shape[0]
        for ref, at in ((kv_near_ref, 0), (kv_far_ref, near)):
            ref[:, :head_dim] = (acc[at : at + near, :head_dim] * scale).astype(low)
            ref[:, head_dim:] = acc[at : at + near, head_dim:].astype(low)


def tail_kernel(pieces, dn_ref, dq_ref, raw_ref, kgain_ref, cos_ref, sin_ref, kw_ref, vw_ref, x_ref,
                inv_ref, *refs):
    kv_refs = refs[:pieces]
    own_ref, *rest_refs, proj_ref, kpart_ref, apart_ref = refs[pieces:]
    total = kv_refs[0][...].astype(full)
    for ref in kv_refs[1:]:
        total = total + ref[...].astype(full)
    head_dim = raw_ref.shape[1]
    query_cols = dq_ref.shape[1]
    turned = rotate(total[:, :head_dim].astype(low).astype(full), cos_ref[...], -sin_ref[...])
    dv = total[:, head_dim:].astype(low)
    raw = raw_ref[...]
    inverse = rms_scale(raw)
    kpart_ref[...] = jnp.sum(turned * raw * inverse, axis=0, keepdims=True)
    dk = norm_back(turned, raw, inverse, kgain_ref[...]).astype(low)
    proj_ref[:, :query_cols] = dq_ref[...]
    proj_ref[:, query_cols : query_cols + head_dim] = dk
    proj_ref[:, query_cols + head_dim :] = dv
    grad = dn_ref[...] + dot(dk, kw_ref[...], 1, 1) + dot(dv, vw_ref[...], 1, 1)
    blocks, share, _ = x_ref.shape
    part = jnp.zeros_like(apart_ref)
    for i in range(blocks):
        one = grad[i * share : (i + 1) * share]
        x = x_ref[i].astype(full)
        part = part + jnp.sum(one * x * inv_ref[i * share : (i + 1) * share], axis=0, keepdims=True)
        if i == 0:
            own_ref[...] = one
        else:
            rest_refs[i - 1][...] = one.astype(low)
    apart_ref[...] = part


def transposed_kernel(out_ref, a_ref, b_ref):
    out_ref[...] = dot(a_ref[...], b_ref[...], 0, 0)


def projection_kernel(pieces, *refs):
    a_refs, b_refs = refs[:pieces], refs[pieces : 2 * pieces]
    query_ref, key_ref, value_ref, a, b = refs[2 * pieces :]
    at = 0
    for a_one, b_one in zip(a_refs, b_refs):
        rows = a_one.shape[0]
        a[at : at + rows] = a_one[...]
        b[at : at + rows] = b_one[...]
        at += rows
    total = dot(a[...], b[...], 0, 0)
    cols, more = query_ref.shape[1], key_ref.shape[1]
    query_ref[...] = total[:, :cols]
    key_ref[...] = total[:, cols : cols + more]
    value_ref[...] = total[:, cols + more :]


def router_kernel(index_ref, blocks, rows_ref, grad_ref, out_ref):
    part_count, groups, inner, share, _ = rows_ref.shape

    def add(i, _):
        mask = i ^ index_ref[0]
        at = (mask & 1) * (groups // 2) + (mask >> 1)
        rows = []
        grads = []
        for w in range(part_count * inner):
            other = w ^ index_ref[1]
            rows.append(rows_ref[other // inner, at, other % inner])
            grads.append(grad_ref[at, other])
        out_ref[...] += dot(jnp.concatenate(grads, 0), jnp.concatenate(rows, 0), 0, 0)
        return 0

    out_ref[...] = jnp.zeros_like(out_ref)
    lax.fori_loop(0, blocks, add, 0)


def place_kernel(index_ref, *refs):
    out_ref = refs[-1]
    for i, ref in enumerate(refs[:-1]):
        out_ref[index_ref[0] ^ i] = ref[...]


def place_rows(index, pieces):
    share, width = pieces[0].shape
    return kernel_call(
        place_kernel,
        shape_of((len(pieces), share, width), pieces[0].dtype),
        [in_smem] + [in_vmem] * len(pieces),
        [index.reshape(1), *pieces],
    )


def gather_wt(array):
    return [array] + [swap(array, "wt", m) for m in range(1, lax.axis_size("wt"))]


def near_ctx(array):
    return [array] + [swap(array, "ctx", 2 * k) for k in range(1, lax.axis_size("ctx") // 2)]


def far_ctx(arrays):
    return [swap(one, "ctx", 1) for one in arrays]


def split_low(array):
    high = array.astype(low)
    return high, (array - high.astype(full)).astype(low)


def on_device(
    tokens,
    cotangent,
    routes,
    attn_gain,
    query_gain,
    key_gain,
    w_query,
    key_weight,
    value_weight,
    w_output,
    moe_gain,
    w_router,
    w_gate_up,
    w_down,
):
    _, pair_len, width = tokens.shape
    head_dim = query_gain.shape[0]
    query_cols = w_query.shape[1]
    heads = query_cols // head_dim
    share, top_count = routes.shape
    experts = w_router.shape[1]
    ctx_count = lax.axis_size("ctx")
    wt_count = lax.axis_size("wt")
    half = ctx_count // 2
    ctx_index = lax.axis_index("ctx")
    wt_index = lax.axis_index("wt")
    my_expert = ctx_index * wt_count + wt_index
    scale = head_dim ** (-0.5)
    head_step = 2
    parts = 2
    inner = wt_count // parts
    mask_cols = -(-experts // 128) * 128
    extra_cols = -(-2 * experts // 128) * 128
    index = wt_index.reshape(1)

    place = jnp.arange(pair_len, dtype=jnp.int32)
    offsets = ((place // share) ^ wt_index) * share + place % share
    near_masks = 2 * jnp.arange(half, dtype=jnp.int32)
    masks = jnp.concatenate([near_masks, near_masks + 1])
    own_positions = mirrored(ctx_index, offsets, ctx_count, pair_len // 2)
    key_positions = mirrored(
        (ctx_index ^ masks)[:, None], offsets[None, :], ctx_count, pair_len // 2
    ).reshape(1, -1)
    row_positions = jnp.tile(own_positions, head_step).reshape(-1, 1)
    frequency = rope_base ** (-2.0 * jnp.arange(head_dim // 2, dtype=full) / head_dim)
    angles = own_positions.astype(full)[:, None] * frequency[None, :]
    cosine, sine = jnp.cos(angles), jnp.sin(angles)
    cosine = jnp.concatenate([cosine, cosine], axis=1)
    sine = jnp.concatenate([-sine, sine], axis=1)

    expert_ids = jnp.arange(mask_cols, dtype=jnp.int32)
    own_mask = jnp.any(routes[:, :, None] == expert_ids, axis=1).astype(low)
    token_rows, normed_one, inverse_one, raw_key, kv_own = kernel_call(
        front_kernel,
        [
            shape_of((wt_count, share, width), low),
            shape_of((pair_len, width), low),
            shape_of((pair_len, 1), full),
            shape_of((pair_len, head_dim), full),
            shape_of((pair_len, 2 * head_dim), low),
        ],
        [in_smem] + [in_vmem] * 7,
        [
            index,
            tokens.reshape(wt_count, share, width),
            attn_gain.reshape(1, -1),
            key_weight,
            value_weight,
            key_gain.reshape(1, -1),
            cosine,
            sine,
        ],
    )

    kv_own, own_mask, normed_one = fence(kv_own, own_mask, normed_one)
    kv_near = near_ctx(kv_own)
    mask_rows = gather_wt(own_mask)
    raw_query, queries = kernel_call(
        query_kernel,
        [shape_of((pair_len, query_cols), full), shape_of((heads * pair_len, head_dim), low)],
        [
            pl.BlockSpec((pair_len, width), lambda i: (0, 0)),
            pl.BlockSpec((width, head_step * head_dim), lambda i: (0, i)),
            pl.BlockSpec((1, head_dim), lambda i: (0, 0)),
            pl.BlockSpec((pair_len, head_dim), lambda i: (0, 0)),
            pl.BlockSpec((pair_len, head_dim), lambda i: (0, 0)),
        ],
        [normed_one, w_query, query_gain.reshape(1, -1), cosine, sine],
        grid=(heads // head_step,),
        out_specs=[
            pl.BlockSpec((pair_len, head_step * head_dim), lambda i: (0, i)),
            pl.BlockSpec((head_step * pair_len, head_dim), lambda i: (i, 0)),
        ],
    )

    kv_near, mask_rows, queries = fence(kv_near, mask_rows, queries)
    kv_pieces = kv_near + far_ctx(kv_near)
    grad_own = kernel_call(
        message_kernel,
        [shape_of((inner * share, width + mask_cols), low)] * parts,
        [in_smem] + [in_vmem] * (1 + wt_count),
        [index, cotangent.reshape(wt_count, share, width), *mask_rows],
    )

    kv_pieces, grad_own, queries = fence(kv_pieces, grad_own, queries)
    grad_near = near_ctx(grad_own[0])
    total_keys = ctx_count * pair_len
    attn_rows, probs, keys, values, branch_own, *branch_rest = kernel_call(
        functools.partial(attend_kernel, scale, ctx_count),
        [
            shape_of((pair_len, query_cols), low),
            shape_of((heads * pair_len, total_keys), low),
            shape_of((total_keys, head_dim), low),
            shape_of((total_keys, head_dim), low),
            shape_of((share, width), full),
        ]
        + [shape_of((share, width), low)] * (wt_count - 1),
        [
            pl.BlockSpec((head_step * pair_len, 1), lambda i: (0, 0)),
            pl.BlockSpec((1, total_keys), lambda i: (0, 0)),
            pl.BlockSpec((head_step * pair_len, head_dim), lambda i: (i, 0)),
            in_any,
        ]
        + [pl.BlockSpec((pair_len, 2 * head_dim), lambda i: (0, 0))] * ctx_count,
        [row_positions, key_positions, queries, w_output, *kv_pieces],
        grid=(heads // head_step,),
        out_specs=[
            pl.BlockSpec((pair_len, query_cols), lambda i: (0, 0)),
            pl.BlockSpec((head_step * pair_len, total_keys), lambda i: (i, 0)),
            pl.BlockSpec((total_keys, head_dim), lambda i: (0, 0)),
            pl.BlockSpec((total_keys, head_dim), lambda i: (0, 0)),
        ]
        + [pl.BlockSpec((share, width), lambda i: (0, 0))] * wt_count,
        scratch_shapes=[
            pltpu.VMEM((heads // head_step, pair_len, head_step * head_dim), low),
            pltpu.VMEM(w_output.shape, low),
            pltpu.SemaphoreType.DMA,
        ],
    )
    branch_rest, branch_own, attn_rows = fence(branch_rest, branch_own, attn_rows)
    received = [swap(branch_rest[m - 1], "wt", m) for m in range(1, wt_count)]
    grad_near, received, branch_own = fence(grad_near, received, branch_own)
    branch = branch_own
    for one in received:
        branch = branch + one.astype(full)
    residual_rows = token_rows[0].astype(full)
    mid_rows = residual_rows + branch
    inverse_two = rms_scale(mid_rows)
    normed_two = (mid_rows * inverse_two * moe_gain).astype(low)

    def joined(pieces):
        return jnp.concatenate(pieces, axis=0) if len(pieces) > 1 else pieces[0]

    normed_two, mid_rows = fence(normed_two, mid_rows)
    first = joined([normed_two] + [swap(normed_two, "wt", m) for m in range(1, inner)])
    grads_first = joined(grad_near)
    grads_first = [grads_first, swap(grads_first, "ctx", 1)]
    first, grads_first, normed_two = fence(first, grads_first, normed_two)
    near_first = near_ctx(first)
    others = [swap(normed_two, "wt", m) for m in range(inner, wt_count)]
    near_first, others = fence(near_first, others)
    rows_first = joined(near_first)
    rows_first = [rows_first, swap(rows_first, "ctx", 1)]
    second = joined(others)
    rows_first, second, grads_first, grad_second = fence(rows_first, second, grads_first, grad_own[1])
    near_second = near_ctx(second)
    grad_near = near_ctx(grad_second)
    results = run_expert(
        0, parts, rows_first, grads_first, w_router, w_gate_up, w_down, my_expert, None,
        width + extra_cols,
    )
    results, near_second, grad_near = fence(results, near_second, grad_near)
    rows_second, grads_second = joined(near_second), joined(grad_near)
    rows_second = [rows_second, swap(rows_second, "ctx", 1)]
    grads_second = [grads_second, swap(grads_second, "ctx", 1)]

    def split_parts(near, far_sent):
        cols = near.shape[1]
        total = (near + far_sent).reshape(half, inner * share, cols)
        return [total[k] for k in range(half)]

    def plane_sum(blocks, received):
        total = blocks[0].astype(full)
        for one in received:
            total = total + one.astype(full)
        return total

    def plane_swap(blocks):
        return [swap(blocks[k], "ctx", 2 * k) for k in range(1, half)]

    def wt_parts(sums):
        return [one[w * share : (w + 1) * share] for one in sums for w in range(inner)]

    back_blocks = [split_parts(results[0], swap(results[1], "ctx", 1))]
    moe_blocks = [split_parts(results[2], swap(results[3], "ctx", 1))]
    rows_second, grads_second, back_blocks, moe_blocks, into = fence(
        rows_second, grads_second, back_blocks, moe_blocks, results[4:]
    )
    back_received = [plane_swap(back_blocks[0])]
    moe_received = [plane_swap(moe_blocks[0])]
    results = run_expert(
        1, parts, rows_second, grads_second, w_router, w_gate_up, w_down, my_expert, into,
        width + extra_cols,
    )

    results, back_received, moe_received = fence(results, back_received, moe_received)
    back_blocks.append(split_parts(results[0], swap(results[1], "ctx", 1)))
    back_blocks, moe_far, results = fence(back_blocks, results[3], results)
    rows_all, hidden, gate_up_grad, expert_grad = results[4:]
    back_received.append(plane_swap(back_blocks[1]))
    moe_far = swap(moe_far, "ctx", 1)
    w_gate_up_grad = dot(rows_all, gate_up_grad, 0, 0)
    w_down_grad = dot(hidden, expert_grad, 0, 0)
    back_received, moe_far, w_gate_up_grad, w_down_grad, attn_rows = fence(
        back_received, moe_far, w_gate_up_grad, w_down_grad, attn_rows
    )
    sums = wt_parts([plane_sum(b, r) for b, r in zip(back_blocks, back_received)])
    sums_low = [one.astype(low) for one in sums[1:]]
    moe_blocks.append(split_parts(results[2], moe_far))
    sums_low, moe_blocks = fence(sums_low, moe_blocks)
    received = [swap(one, "wt", m + 1) for m, one in enumerate(sums_low)]
    received, moe_blocks = fence(received, moe_blocks)
    summed = plane_sum(sums, received)
    rows_sum = summed[:, :width]
    weight_grads = (
        summed[:, width : width + experts] + summed[:, width + experts : width + 2 * experts]
    )
    chosen = own_mask[:, :experts] > 0.5
    logits = jnp.where(chosen, jnp.dot(normed_two, w_router, preferred_element_type=full), -1e30)
    shifted = jnp.where(chosen, jnp.exp(logits - jnp.max(logits, axis=-1, keepdims=True)), 0.0)
    own_routes = shifted / jnp.sum(shifted, axis=-1, keepdims=True)
    logits_grad = own_routes * (
        weight_grads - jnp.sum(own_routes * weight_grads, axis=-1, keepdims=True)
    )
    logits_cols = jnp.concatenate(split_low(logits_grad), axis=1)
    router_term = dot(logits_cols, jnp.concatenate([w_router, w_router], axis=1), 1, 1)
    normed_two_grad = rows_sum + router_term
    moe_gain_part = jnp.sum(normed_two_grad * mid_rows * inverse_two, axis=0)
    grad_rows = lax.dynamic_slice_in_dim(cotangent[0], wt_index * share, share, 0).astype(full)
    mid_grad = grad_rows + norm_back(normed_two_grad, mid_rows, inverse_two, moe_gain)
    logits_cols = jnp.pad(logits_cols, ((0, 0), (0, extra_cols - 2 * experts)))
    mid_message = jnp.concatenate([mid_grad.astype(low), logits_cols], axis=1)

    mid_message, moe_blocks = fence(mid_message, moe_blocks)
    mid_pieces = gather_wt(mid_message)
    moe_received.append(plane_swap(moe_blocks[1]))
    mid_pieces, moe_received, attn_rows = fence(mid_pieces, moe_received, attn_rows)

    moe_sums = wt_parts([plane_sum(b, r) for b, r in zip(moe_blocks, moe_received)])
    moe_low = [one.astype(low) for one in moe_sums[1:]]
    moe_low, mid_pieces, attn_rows = fence(moe_low, mid_pieces, attn_rows)
    attn_near = near_ctx(attn_rows)
    moe_received = [swap(one, "wt", m + 1) for m, one in enumerate(moe_low)]
    kv_part_near, kv_part_far, query_grad, query_gain_part, branch_grad, logits_near = kernel_call(
        functools.partial(attend_back_kernel, scale, wt_count),
        [
            shape_of((total_keys // 2, 2 * head_dim), low),
            shape_of((total_keys // 2, 2 * head_dim), low),
            shape_of((pair_len, query_cols), low),
            shape_of((1, head_dim), full),
            shape_of((pair_len, width), low),
            shape_of((pair_len, extra_cols), low),
        ],
        [
            pl.BlockSpec((head_step * head_dim, width), lambda i: (i, 0)),
            pl.BlockSpec((head_step * pair_len, total_keys), lambda i: (i, 0)),
            pl.BlockSpec((total_keys, head_dim), lambda i: (0, 0)),
            pl.BlockSpec((total_keys, head_dim), lambda i: (0, 0)),
            pl.BlockSpec((head_step * pair_len, head_dim), lambda i: (i, 0)),
            pl.BlockSpec((pair_len, head_step * head_dim), lambda i: (0, i)),
            pl.BlockSpec((1, head_dim), lambda i: (0, 0)),
            pl.BlockSpec((pair_len, head_dim), lambda i: (0, 0)),
            pl.BlockSpec((pair_len, head_dim), lambda i: (0, 0)),
        ]
        + [pl.BlockSpec((share, width + extra_cols), lambda i: (0, 0))] * wt_count,
        [
            w_output, probs, keys, values, queries, raw_query, query_gain.reshape(1, -1),
            cosine, sine, *mid_pieces,
        ],
        grid=(heads // head_step,),
        out_specs=[
            pl.BlockSpec((total_keys // 2, 2 * head_dim), lambda i: (0, 0)),
            pl.BlockSpec((total_keys // 2, 2 * head_dim), lambda i: (0, 0)),
            pl.BlockSpec((pair_len, head_step * head_dim), lambda i: (0, i)),
            pl.BlockSpec((1, head_dim), lambda i: (0, 0)),
            pl.BlockSpec((pair_len, width), lambda i: (0, 0)),
            pl.BlockSpec((pair_len, extra_cols), lambda i: (0, 0)),
        ],
        scratch_shapes=[pltpu.VMEM((total_keys, 2 * head_dim), full)],
    )

    kv_part_near, kv_part_far, query_grad, branch_grad, logits_near, moe_received, attn_near = fence(
        kv_part_near, kv_part_far, query_grad, branch_grad, logits_near, moe_received, attn_near
    )
    kv_near = (kv_part_near + swap(kv_part_far, "ctx", 1)).reshape(half, pair_len, 2 * head_dim)
    kv_near = [kv_near[k] for k in range(half)]
    out_rows = (mid_rows + plane_sum(moe_sums, moe_received)).astype(low)
    block_cols = width // ctx_count

    def pair_slice(array, k):
        start = ((ctx_index ^ (2 * k)) >> 1) * (2 * block_cols)
        return lax.dynamic_slice_in_dim(array, start, 2 * block_cols, 1)

    slices = [
        jnp.concatenate([pair_slice(normed_one, k), pair_slice(branch_grad, k), logits_near], axis=1)
        for k in range(half)
    ]
    kv_near, query_grad, out_rows, slices, attn_near = fence(
        kv_near, query_grad, out_rows, slices, attn_near
    )
    kv_received = plane_swap(kv_near)
    slices_near = [slices[0]] + plane_swap(slices)
    out_pieces = gather_wt(out_rows)
    attn_all = attn_near + far_ctx(attn_near)
    query_term = dot(query_grad, w_query, 1, 1)
    kv_received, slices_near, out_pieces, attn_all, query_term = fence(
        kv_received, slices_near, out_pieces, attn_all, query_term
    )
    one_own, *one_rest, projection_own, key_gain_part, attn_gain_part = kernel_call(
        functools.partial(tail_kernel, half),
        [shape_of((share, width), full)]
        + [shape_of((share, width), low)] * (wt_count - 1)
        + [
            shape_of((pair_len, query_cols + 2 * head_dim), low),
            shape_of((1, head_dim), full),
            shape_of((1, width), full),
        ],
        [in_vmem] * (10 + half),
        [
            query_term, query_grad, raw_key, key_gain.reshape(1, -1), cosine, sine, key_weight,
            value_weight, token_rows, inverse_one, kv_near[0], *kv_received,
        ],
    )
    gains = jnp.concatenate(
        [attn_gain_part[0], moe_gain_part, query_gain_part[0], key_gain_part[0]]
    ).reshape(-1, 128)

    one_own, one_rest, projection_own, gains, slices_near = fence(
        one_own, one_rest, projection_own, gains, slices_near
    )
    received = [swap(one, "wt", m + 1) for m, one in enumerate(one_rest)]
    projection_near = near_ctx(projection_own)
    block_out = place_rows(index, out_pieces)
    odd = (ctx_index & 1) == 1

    def halves(one, start):
        first = one[:, start : start + block_cols]
        second = one[:, start + block_cols : start + 2 * block_cols]
        return jnp.where(odd, second, first), jnp.where(odd, first, second)

    keep_normed, keep_mid, give, logits_all = [], [], [], []
    for one in slices_near:
        keep, other = halves(one, 0)
        keep_normed.append(keep)
        keep, another = halves(one, 2 * block_cols)
        keep_mid.append(keep)
        logits_all.append(one[:, 4 * block_cols :])
        give.append(jnp.concatenate([other, another, logits_all[-1]], axis=1))
    for one in far_ctx(give):
        keep_normed.append(one[:, :block_cols])
        keep_mid.append(one[:, block_cols : 2 * block_cols])
        logits_all.append(one[:, 2 * block_cols :])
    gains = gains + swap(gains, "ctx", 1)
    received, projection_near, gains, keep_normed, keep_mid, logits_all, block_out = fence(
        received, projection_near, gains, keep_normed, keep_mid, logits_all, block_out
    )
    normed_rows = plane_sum([one_own], received)
    input_rows = mid_grad + norm_back(normed_rows, residual_rows, inverse_one[:share], attn_gain)
    input_rows = input_rows.astype(low)

    input_rows, projection_near, gains = fence(input_rows, projection_near, gains)
    input_pieces = gather_wt(input_rows)
    projection_all = projection_near + far_ctx(projection_near)
    mask = 2
    while mask < ctx_count:
        gains = gains + swap(gains, "ctx", mask)
        mask *= 2
    mask = 1
    while mask < wt_count:
        gains = gains + swap(gains, "wt", mask)
        mask *= 2
    gains = gains.reshape(-1)
    w_output_grad = dot(jnp.concatenate(attn_all, 0), jnp.concatenate(keep_mid, 0), 0, 0)

    def router_body(index_ref, rows_ref, grad_ref, out_ref):
        router_kernel(index_ref, ctx_count, rows_ref, grad_ref, out_ref)

    router_block = kernel_call(
        router_body,
        shape_of((extra_cols, width), full),
        [in_smem, in_vmem, in_vmem],
        [
            jnp.stack([ctx_index, wt_index]),
            rows_all.reshape(parts, ctx_count, inner, share, width),
            jnp.stack(logits_all).reshape(ctx_count, wt_count, share, extra_cols),
        ],
    )
    w_router_grad = (router_block[:experts] + router_block[experts : 2 * experts]).T
    w_query_grad, w_key_grad, w_value_grad = kernel_call(
        functools.partial(projection_kernel, ctx_count),
        [
            shape_of((block_cols, query_cols), full),
            shape_of((block_cols, head_dim), full),
            shape_of((block_cols, head_dim), full),
        ],
        [in_vmem] * (2 * ctx_count),
        [*keep_normed, *projection_all],
        scratch_shapes=[
            pltpu.VMEM((total_keys, block_cols), low),
            pltpu.VMEM((total_keys, query_cols + 2 * head_dim), low),
        ],
    )
    tokens_grad = place_rows(index, input_pieces)

    return (
        block_out.reshape(1, pair_len, width),
        tokens_grad.reshape(1, pair_len, width),
        gains[:width],
        gains[2 * width : 2 * width + head_dim],
        gains[2 * width + head_dim :],
        w_query_grad,
        w_key_grad,
        w_value_grad,
        w_output_grad,
        gains[width : 2 * width],
        w_router_grad,
        w_gate_up_grad[None],
        w_down_grad[None],
    )


def solution(mesh):
    in_specs = (
        P(None, "ctx", None),
        P(None, "ctx", None),
        P(("ctx", "wt"), None),
        P(),
        P(),
        P(),
        P(None, "wt"),
        P(None, "wt"),
        P(None, "wt"),
        P("wt", None),
        P(),
        P(),
        P(("ctx", "wt"), None, None),
        P(("ctx", "wt"), None, None),
    )
    out_specs = (
        P(None, "ctx", None),
        P(None, "ctx", None),
        P(),
        P(),
        P(),
        P("ctx", "wt"),
        P("ctx", "wt"),
        P("ctx", "wt"),
        P("wt", "ctx"),
        P(),
        P(),
        P(("ctx", "wt"), None, None),
        P(("ctx", "wt"), None, None),
    )
    return jax.shard_map(
        on_device, mesh=mesh, in_specs=in_specs, out_specs=out_specs, check_vma=False
    )
```

```python
import functools

import jax
import jax.numpy as jnp
from jax import lax
from jax.experimental import pallas as pl
from jax.experimental.pallas import tpu as pltpu
from jax.sharding import PartitionSpec as P

epsilon = 1e-06
rope_base = 1000000.0
low = jnp.bfloat16
full = jnp.float32
vmem_bytes = 60 * 1024 * 1024

in_vmem = pl.BlockSpec(memory_space=pltpu.VMEM)
in_smem = pl.BlockSpec(memory_space=pltpu.SMEM)
in_any = pl.BlockSpec(memory_space=pl.ANY)


def dot(a, b, a_dim=1, b_dim=0):
    return lax.dot_general(a, b, (((a_dim,), (b_dim,)), ((), ())), preferred_element_type=full)


def swap(array, axis, mask):
    count = lax.axis_size(axis)
    return lax.ppermute(array, axis, [(i, i ^ mask) for i in range(count)])


def fence(*values):
    return lax.optimization_barrier(values)


def shape_of(shape, dtype):
    return jax.ShapeDtypeStruct(tuple(shape), dtype)


def kernel_call(kernel, outs, ins, args, **more):
    return pl.pallas_call(
        kernel,
        out_shape=outs,
        in_specs=ins,
        compiler_params=pltpu.CompilerParams(vmem_limit_bytes=vmem_bytes),
        **more,
    )(*args)


def rms_scale(value_matrix):
    return lax.rsqrt(jnp.mean(value_matrix * value_matrix, axis=-1, keepdims=True) + epsilon)


def norm_back(grad_out, value_matrix, inverse, gain_vec):
    scaled = grad_out * gain_vec
    inner_mean = jnp.mean(scaled * value_matrix, axis=-1, keepdims=True)
    return inverse * (scaled - value_matrix * inverse * inverse * inner_mean)


def mirrored(device, offset, groups, block_len):
    which_block = jnp.where(offset < block_len, device, 2 * groups - 1 - device)
    return which_block * block_len + offset % block_len


def rotate(value_matrix, cosine, sine):
    return value_matrix * cosine + pltpu.roll(value_matrix, value_matrix.shape[-1] // 2, 1) * sine


def front_kernel(
    index_ref, x_ref, gain_ref, kw_ref, vw_ref, kgain_ref, cos_ref, sin_ref,
    rows_ref, normed_ref, inv_ref, raw_ref, kv_ref,
):
    blocks, share, _ = x_ref.shape
    for i in range(blocks):
        x_low = x_ref[index_ref[0] ^ i]
        rows_ref[i] = x_low
        x = x_low.astype(full)
        inverse = rms_scale(x)
        inv_ref[i * share : (i + 1) * share] = inverse
        normed_ref[i * share : (i + 1) * share] = (x * inverse * gain_ref[...]).astype(low)
    normed = normed_ref[...]
    raw = dot(normed, kw_ref[...])
    raw_ref[...] = raw
    head_dim = raw.shape[1]
    turned = rotate(raw * rms_scale(raw) * kgain_ref[...], cos_ref[...], sin_ref[...])
    kv_ref[:, :head_dim] = turned.astype(low)
    kv_ref[:, head_dim:] = dot(normed, vw_ref[...]).astype(low)


def query_kernel(normed_ref, w_ref, gain_ref, cos_ref, sin_ref, raw_ref, q_ref):
    rows, head_dim = cos_ref.shape
    raw = dot(normed_ref[...], w_ref[...])
    raw_ref[...] = raw
    for h in range(raw.shape[1] // head_dim):
        one = raw[:, h * head_dim : (h + 1) * head_dim]
        turned = rotate(one * rms_scale(one) * gain_ref[...], cos_ref[...], sin_ref[...])
        q_ref[h * rows : (h + 1) * rows] = turned.astype(low)


def attend_kernel(scale, pieces, qpos_ref, kpos_ref, q_ref, w_ref, *refs):
    kv_refs = refs[:pieces]
    rows_ref, probs_ref, keys_ref, values_ref, own_ref, *rest_refs, attn, weight, sem = refs[pieces:]
    step = pl.program_id(0)
    tokens, head_dim = rows_ref.shape[0], kv_refs[0].shape[1] // 2
    copy = pltpu.make_async_copy(w_ref, weight, sem)

    @pl.when(step == 0)
    def _():
        copy.start()
        at = 0
        for ref in kv_refs:
            keys_ref[at : at + ref.shape[0]] = ref[:, :head_dim]
            values_ref[at : at + ref.shape[0]] = ref[:, head_dim:]
            at += ref.shape[0]

    scores = dot(q_ref[...], keys_ref[...], 1, 1) * scale
    scores = jnp.where(kpos_ref[...] <= qpos_ref[...], scores, -1e30)
    weights = jnp.exp(scores - jnp.max(scores, axis=-1, keepdims=True))
    probs = (weights / jnp.sum(weights, axis=-1, keepdims=True)).astype(low)
    probs_ref[...] = probs
    out = dot(probs, values_ref[...]).astype(low)
    heads = out.shape[0] // tokens
    attn[step] = jnp.concatenate([out[h * tokens : (h + 1) * tokens] for h in range(heads)], axis=1)

    @pl.when(step == pl.num_programs(0) - 1)
    def _():
        copy.wait()
        for i in range(attn.shape[0]):
            rows_ref[:, i * heads * head_dim : (i + 1) * heads * head_dim] = attn[i]
        total = dot(rows_ref[...], weight[...])
        share = own_ref.shape[0]
        own_ref[...] = total[:share]
        for i, ref in enumerate(rest_refs):
            ref[...] = total[(i + 1) * share : (i + 2) * share].astype(low)


def mid_kernel(x_ref, gain_ref, mask_ref, own_ref, *refs):
    received, (mid_ref, inv_ref, message_ref) = refs[:-3], refs[-3:]
    mid = own_ref[...]
    for one in received:
        mid = mid + one[...].astype(full)
    mid = x_ref[0].astype(full) + mid
    inverse = rms_scale(mid)
    mid_ref[...] = mid
    inv_ref[...] = inverse
    width = mid.shape[1]
    message_ref[:, :width] = (mid * inverse * gain_ref[...]).astype(low)
    message_ref[:, width:] = mask_ref[...]


def expert_kernel(
    tiles, first, inner, by_wt, merged, index_ref, row_near, row_far, grad_near, grad_far, router_ref,
    gu_any, down_any, *refs
):
    if merged:
        near_ref, far_ref, *refs = refs
        moe_near_ref, moe_far_ref = near_ref, far_ref
    else:
        near_ref, far_ref, moe_near_ref, moe_far_ref, *refs = refs
    x_ref, hidden_ref, dgu_ref, deo_ref, x_tile, g_tile, gu, down, sems = refs
    step = pl.program_id(0)
    width = g_tile.shape[1]
    ffw = down.shape[0]
    experts = router_ref.shape[0]
    expert = index_ref[0]
    chips, _, share, _ = grad_near.shape
    copy_gu = pltpu.make_async_copy(gu_any.at[0], gu, sems.at[0])
    copy_down = pltpu.make_async_copy(down_any.at[0], down, sems.at[1])

    @pl.when(step == 0)
    def _():
        copy_gu.start()
        copy_down.start()

    def load(row_ref, grad_ref):
        if not by_wt:
            x_tile[...] = row_ref[...]
        for c in range(chips):
            for w in range(inner):
                to = slice((c * inner + w) * share, (c * inner + w + 1) * share)
                if by_wt:
                    x_tile[to] = row_ref[w, c * share : (c + 1) * share]
                g_tile[to] = grad_ref[c, index_ref[1] ^ (first + w)]

    @pl.when(step < tiles // 2)
    def _():
        load(row_near, grad_near)

    @pl.when(step >= tiles // 2)
    def _():
        load(row_far, grad_far)

    x = x_tile[:, :width]
    x_ref[...] = x
    g = g_tile[...].astype(full)
    chosen = x_tile[:, width:][:, :experts].astype(full) > 0.5
    logits = jnp.where(chosen, dot(x, router_ref[...], 1, 1), -1e30)
    shifted = jnp.exp(logits - jnp.max(logits, axis=-1, keepdims=True))
    shifted = jnp.where(chosen, shifted, 0.0)
    mine = lax.broadcasted_iota(jnp.int32, shifted.shape, 1) == expert
    own = jnp.sum(jnp.where(mine, shifted, 0.0), axis=-1, keepdims=True) / jnp.sum(
        shifted, axis=-1, keepdims=True
    )
    deo = (g * own).astype(low)
    deo_ref[...] = deo

    @pl.when(step == 0)
    def _():
        copy_gu.wait()

    gate_up = dot(x, gu[...])

    @pl.when(step == 0)
    def _():
        copy_down.wait()

    gate, up = gate_up[:, :ffw], gate_up[:, ffw:]
    dhid = dot(deo, down[...], 1, 1)
    sig = jax.nn.sigmoid(gate)
    silu = gate * sig
    hidden = (silu * up).astype(low)
    hidden_ref[...] = hidden
    dgate = (dhid * up * (sig + silu * (1.0 - sig))).astype(low)
    dup = (dhid * silu).astype(low)
    dgu_ref[:, :ffw] = dgate
    dgu_ref[:, ffw:] = dup
    out = dot(hidden, down[...]).astype(low).astype(full)
    dlw = jnp.sum(out * g, axis=-1, keepdims=True)
    moe = (out * own).astype(low)
    back = (dot(dgate, gu[:, :ffw], 1, 1) + dot(dup, gu[:, ffw:], 1, 1)).astype(low)
    high = dlw.astype(low)
    rest = (dlw - high.astype(full)).astype(low).astype(full)
    cols = near_ref.shape[1] - (2 if merged else 1) * width
    lane = lax.broadcasted_iota(jnp.int32, (x.shape[0], cols), 1)
    extra = jnp.where(lane == expert, high.astype(full), 0.0)
    extra = jnp.where(lane == experts + expert, rest, extra).astype(low)

    def store(row_ref, moe_ref):
        row_ref[:, :width] = back
        row_ref[:, width : width + cols] = extra
        moe_ref[:, moe_ref.shape[1] - width :] = moe

    @pl.when(step < tiles // 2)
    def _():
        store(near_ref, moe_near_ref)

    @pl.when(step >= tiles // 2)
    def _():
        store(far_ref, moe_far_ref)


def run_expert(part, part_count, inner, by_wt, merged, rows, grads, router, w_gate_up, w_down, index, into, cols):
    chips, wt_count, share, width = grads[0].shape
    half_rows = chips * inner * share
    tile = min(256, half_rows)
    near = half_rows // tile
    tiles = 2 * near
    each = chips // near
    ffw = w_down.shape[1]
    wide = rows[0].shape[-1]
    everything = 2 * half_rows * part_count
    offset = part * tiles
    near_map = lambda i: (jnp.minimum(i, near - 1), 0)
    far_map = lambda i: (jnp.maximum(i - near, 0), 0)
    all_map = lambda i: (i + offset, 0)
    widths = [cols + width] if merged else [cols, width]
    outs, out_specs = [], []
    for one in widths:
        outs += [shape_of((half_rows, one), low)] * 2
        out_specs += [pl.BlockSpec((tile, one), near_map), pl.BlockSpec((tile, one), far_map)]
    lead_outs = len(outs)
    for one in (width, ffw, 2 * ffw, width):
        outs.append(shape_of((everything, one), low))
        out_specs.append(pl.BlockSpec((tile, one), all_map))
    ins = [in_smem]
    for where in (near_map, far_map):
        if by_wt:
            ins.append(pl.BlockSpec((inner, each * share, wide), lambda i, where=where: (0, where(i)[0], 0)))
        else:
            ins.append(pl.BlockSpec((tile, wide), where))
    for where in (near_map, far_map):
        ins.append(pl.BlockSpec((each, wt_count, share, width), lambda i, where=where: (where(i)[0], 0, 0, 0)))
    ins += [pl.BlockSpec(router.shape, lambda i: (0, 0)), in_any, in_any]
    args = [index, *rows, *grads, router, w_gate_up, w_down]
    lead = len(args)
    aliases = {}
    if into is not None:
        for i, array in enumerate(into):
            aliases[len(args)] = lead_outs + i
            ins.append(in_any)
            args.append(array)

    def body(*refs):
        expert_kernel(tiles, part * inner, inner, by_wt, merged, *refs[:lead], *refs[len(args) :])

    results = kernel_call(
        body,
        outs,
        ins,
        args,
        grid=(tiles,),
        out_specs=out_specs,
        scratch_shapes=[
            pltpu.VMEM((tile, wide), low),
            pltpu.VMEM((tile, width), low),
            pltpu.VMEM(w_gate_up.shape[1:], low),
            pltpu.VMEM(w_down.shape[1:], low),
            pltpu.SemaphoreType.DMA((2,)),
        ],
        input_output_aliases=aliases,
    )
    return results[:lead_outs], results[lead_outs:]


def cut_kernel(pieces, index_ref, rows_ref, from_ref, *out_refs):
    whole = rows_ref.shape[1]
    cols = out_refs[0].shape[1] - whole
    for k in range(pieces):
        out_refs[k][:, :whole] = rows_ref[...]
        start = pl.multiple_of((index_ref[0] ^ k) * cols, 128)
        out_refs[k][:, whole:] = from_ref[:, pl.ds(start, cols)]


def deal_kernel(pieces, whole, index_ref, *refs):
    in_refs, (own_ref, keep_ref, give_ref) = refs[:pieces], refs[pieces:]
    rows = in_refs[0].shape[0]
    cols = (in_refs[0].shape[1] - whole) // 2
    for i, ref in enumerate(in_refs):
        at = slice(i * rows, (i + 1) * rows)
        own_ref[at] = ref[:, :whole]
        give_ref[at, :whole] = ref[:, :whole]
        keep = pl.multiple_of(whole + index_ref[0] * cols, 128)
        give = pl.multiple_of(whole + (1 - index_ref[0]) * cols, 128)
        keep_ref[at] = ref[:, pl.ds(keep, cols)]
        give_ref[at, whole:] = ref[:, pl.ds(give, cols)]


def deal(core, pieces, whole):
    rows, wide = pieces[0].shape
    cols = (wide - whole) // 2
    total = rows * len(pieces)
    return kernel_call(
        functools.partial(deal_kernel, len(pieces), whole),
        [shape_of((total, whole), low), shape_of((total, cols), low), shape_of((total, whole + cols), low)],
        [in_smem] + [in_vmem] * len(pieces),
        [core, *pieces],
    )


def attend_back_kernel(scale, pieces, index_ref, w_ref, probs_ref, keys_ref, values_ref, q_ref, raw_ref,
                       gain_ref, cos_ref, sin_ref, *refs):
    da_refs = refs[:pieces]
    kv_near_ref, kv_far_ref, dq_ref, part_ref, *message_refs, da_ref, acc = refs[pieces:]
    step = pl.program_id(0)
    tokens, head_dim = cos_ref.shape
    share = da_refs[0].shape[0]
    width = da_ref.shape[1]
    logit_cols = da_refs[0].shape[1] - width

    @pl.when(step == 0)
    def _():
        for i, ref in enumerate(da_refs):
            da_ref[i * share : (i + 1) * share] = ref[:, :width]
            for k, one in enumerate(message_refs):
                one[i * share : (i + 1) * share, :logit_cols] = ref[:, width:]
        for k, one in enumerate(message_refs):
            cols = one.shape[1] - logit_cols
            start = pl.multiple_of((index_ref[0] ^ k) * cols, 128)
            one[:, logit_cols:] = da_ref[:, pl.ds(start, cols)]
        acc[...] = jnp.zeros_like(acc)
        part_ref[...] = jnp.zeros_like(part_ref)

    dattn = dot(da_ref[...], w_ref[...], 1, 1).astype(low)
    heads = dattn.shape[1] // head_dim
    out_grad = jnp.concatenate(
        [dattn[:, h * head_dim : (h + 1) * head_dim] for h in range(heads)], axis=0
    )
    probs_low = probs_ref[...]
    probs = probs_low.astype(full)
    prob_grad = dot(out_grad, values_ref[...], 1, 1)
    inner = jnp.sum(probs * prob_grad, axis=-1, keepdims=True)
    score_grad = (probs * (prob_grad - inner)).astype(low)
    query_grad = (dot(score_grad, keys_ref[...]) * scale).astype(low).astype(full)
    acc[:, :head_dim] += dot(score_grad, q_ref[...], 0, 0)
    acc[:, head_dim:] += dot(probs_low, out_grad, 0, 0)
    gain = gain_ref[...]
    part = part_ref[...]
    for h in range(heads):
        cols = slice(h * head_dim, (h + 1) * head_dim)
        turned = rotate(query_grad[h * tokens : (h + 1) * tokens], cos_ref[...], -sin_ref[...])
        raw = raw_ref[:, cols]
        inverse = rms_scale(raw)
        part = part + jnp.sum(turned * raw * inverse, axis=0, keepdims=True)
        dq_ref[:, cols] = norm_back(turned, raw, inverse, gain).astype(low)
    part_ref[...] = part

    @pl.when(step == pl.num_programs(0) - 1)
    def _():
        near = kv_near_ref.shape[0]
        for ref, at in ((kv_near_ref, 0), (kv_far_ref, near)):
            ref[:, :head_dim] = (acc[at : at + near, :head_dim] * scale).astype(low)
            ref[:, head_dim:] = acc[at : at + near, head_dim:].astype(low)


def tail_kernel(pieces, dn_ref, dq_ref, raw_ref, kgain_ref, cos_ref, sin_ref, kw_ref, vw_ref, x_ref,
                inv_ref, *refs):
    kv_refs = refs[:pieces]
    own_ref, *rest_refs, proj_ref, kpart_ref, apart_ref = refs[pieces:]
    total = kv_refs[0][...].astype(full)
    for ref in kv_refs[1:]:
        total = total + ref[...].astype(full)
    head_dim = raw_ref.shape[1]
    query_cols = dq_ref.shape[1]
    turned = rotate(total[:, :head_dim].astype(low).astype(full), cos_ref[...], -sin_ref[...])
    dv = total[:, head_dim:].astype(low)
    raw = raw_ref[...]
    inverse = rms_scale(raw)
    kpart_ref[...] = jnp.sum(turned * raw * inverse, axis=0, keepdims=True)
    dk = norm_back(turned, raw, inverse, kgain_ref[...]).astype(low)
    proj_ref[:, :query_cols] = dq_ref[...]
    proj_ref[:, query_cols : query_cols + head_dim] = dk
    proj_ref[:, query_cols + head_dim :] = dv
    grad = dn_ref[...] + dot(dk, kw_ref[...], 1, 1) + dot(dv, vw_ref[...], 1, 1)
    blocks, share, _ = x_ref.shape
    part = jnp.zeros_like(apart_ref)
    for i in range(blocks):
        one = grad[i * share : (i + 1) * share]
        x = x_ref[i].astype(full)
        part = part + jnp.sum(one * x * inv_ref[i * share : (i + 1) * share], axis=0, keepdims=True)
        if i == 0:
            own_ref[...] = one
        else:
            rest_refs[i - 1][...] = one.astype(low)
    apart_ref[...] = part


def output_kernel(a_near, a_far, b_near, b_far, out_ref):
    rows, cols = out_ref.shape
    far = b_far.shape[1] - cols
    out_ref[...] = dot(a_near[...], b_near[...], 0, 0) + dot(a_far[:, :rows], b_far[:, far:], 0, 0)


def projection_kernel(a_near, a_far, b_near, b_far, query_ref, key_ref, value_ref):
    far = a_far.shape[1] - a_near.shape[1]
    total = dot(a_near[...], b_near[...], 0, 0) + dot(a_far[:, far:], b_far[...], 0, 0)
    cols, more = query_ref.shape[1], key_ref.shape[1]
    query_ref[...] = total[:, :cols]
    key_ref[...] = total[:, cols : cols + more]
    value_ref[...] = total[:, cols + more :]


def router_kernel(index_ref, rows_any, near_ref, far_ref, out_ref, rows, grads, sems):
    part_count, groups, inner, share, _ = rows_any.shape
    copies = []
    for p in range(part_count):
        for c in range(groups):
            half = groups // 2
            mask = 2 * (c % half) + c // half
            for w in range(inner):
                to = (index_ref[0] ^ mask) * (part_count * inner) + (index_ref[1] ^ (p * inner + w))
                copy = pltpu.make_async_copy(rows_any.at[p, c, w], rows.at[to], sems.at[len(copies)])
                copy.start()
                copies.append(copy)
                grad_ref = near_ref if c < half else far_ref
                at = ((c % half) * (part_count * inner) + p * inner + w) * share
                grads[to] = grad_ref[at : at + share, : grads.shape[2]]
    for copy in copies:
        copy.wait()
    count = rows.shape[0] * share
    total = dot(grads[...].reshape(count, grads.shape[2]), rows[...].reshape(count, rows.shape[2]), 0, 0)
    experts = out_ref.shape[0]
    out_ref[...] = total[:experts] + total[experts : 2 * experts]


def place_kernel(index_ref, *refs):
    out_ref = refs[-1]
    for i, ref in enumerate(refs[:-1]):
        out_ref[index_ref[0] ^ i] = ref[...]


def place_rows(index, pieces):
    share, width = pieces[0].shape
    return kernel_call(
        place_kernel,
        shape_of((len(pieces), share, width), pieces[0].dtype),
        [in_smem] + [in_vmem] * len(pieces),
        [index.reshape(1), *pieces],
    )


def gather_wt(array):
    return [array] + [swap(array, "wt", m) for m in range(1, lax.axis_size("wt"))]


def near_ctx(array):
    return [array] + [swap(array, "ctx", 2 * k) for k in range(1, lax.axis_size("ctx") // 2)]


def far_ctx(arrays):
    return [swap(one, "ctx", 1) for one in arrays]


def split_low(array):
    high = array.astype(low)
    return high, (array - high.astype(full)).astype(low)


def on_device(
    tokens,
    cotangent,
    routes,
    attn_gain,
    query_gain,
    key_gain,
    w_query,
    key_weight,
    value_weight,
    w_output,
    moe_gain,
    w_router,
    w_gate_up,
    w_down,
):
    _, pair_len, width = tokens.shape
    head_dim = query_gain.shape[0]
    query_cols = w_query.shape[1]
    heads = query_cols // head_dim
    share, top_count = routes.shape
    experts = w_router.shape[1]
    ctx_count = lax.axis_size("ctx")
    wt_count = lax.axis_size("wt")
    half = ctx_count // 2
    ctx_index = lax.axis_index("ctx")
    wt_index = lax.axis_index("wt")
    my_expert = ctx_index * wt_count + wt_index
    scale = head_dim ** (-0.5)
    head_step = 2
    parts = 2
    inner = wt_count // parts
    mask_cols = -(-experts // 128) * 128
    extra_cols = -(-2 * experts // 128) * 128
    index = wt_index.reshape(1)
    chip = (ctx_index >> 1).reshape(1)
    core = (ctx_index & 1).reshape(1)
    router = w_router.T

    def joined(pieces):
        return jnp.concatenate(pieces, axis=0) if len(pieces) > 1 else pieces[0]

    def both(pieces):
        near = joined(pieces)
        return [near, swap(near, "ctx", 1)]


    place = jnp.arange(pair_len, dtype=jnp.int32)
    offsets = ((place // share) ^ wt_index) * share + place % share
    near_masks = 2 * jnp.arange(half, dtype=jnp.int32)
    masks = jnp.concatenate([near_masks, near_masks + 1])
    own_positions = mirrored(ctx_index, offsets, ctx_count, pair_len // 2)
    key_positions = mirrored(
        (ctx_index ^ masks)[:, None], offsets[None, :], ctx_count, pair_len // 2
    ).reshape(1, -1)
    row_positions = jnp.tile(own_positions, head_step).reshape(-1, 1)
    frequency = rope_base ** (-2.0 * jnp.arange(head_dim // 2, dtype=full) / head_dim)
    angles = own_positions.astype(full)[:, None] * frequency[None, :]
    cosine, sine = jnp.cos(angles), jnp.sin(angles)
    cosine = jnp.concatenate([cosine, cosine], axis=1)
    sine = jnp.concatenate([-sine, sine], axis=1)

    expert_ids = jnp.arange(mask_cols, dtype=jnp.int32)
    own_mask = jnp.any(routes[:, :, None] == expert_ids, axis=1).astype(low)
    token_rows, normed_one, inverse_one, raw_key, kv_own = kernel_call(
        front_kernel,
        [
            shape_of((wt_count, share, width), low),
            shape_of((pair_len, width), low),
            shape_of((pair_len, 1), full),
            shape_of((pair_len, head_dim), full),
            shape_of((pair_len, 2 * head_dim), low),
        ],
        [in_smem] + [in_vmem] * 7,
        [
            index,
            tokens.reshape(wt_count, share, width),
            attn_gain.reshape(1, -1),
            key_weight,
            value_weight,
            key_gain.reshape(1, -1),
            cosine,
            sine,
        ],
    )

    kv_own, own_mask, normed_one = fence(kv_own, own_mask, normed_one)
    kv_near = near_ctx(kv_own)
    raw_query, queries = kernel_call(
        query_kernel,
        [shape_of((pair_len, query_cols), full), shape_of((heads * pair_len, head_dim), low)],
        [
            pl.BlockSpec((pair_len, width), lambda i: (0, 0)),
            pl.BlockSpec((width, head_step * head_dim), lambda i: (0, i)),
            pl.BlockSpec((1, head_dim), lambda i: (0, 0)),
            pl.BlockSpec((pair_len, head_dim), lambda i: (0, 0)),
            pl.BlockSpec((pair_len, head_dim), lambda i: (0, 0)),
        ],
        [normed_one, w_query, query_gain.reshape(1, -1), cosine, sine],
        grid=(heads // head_step,),
        out_specs=[
            pl.BlockSpec((pair_len, head_step * head_dim), lambda i: (0, i)),
            pl.BlockSpec((head_step * pair_len, head_dim), lambda i: (i, 0)),
        ],
    )

    kv_near, queries, grad_own = fence(kv_near, queries, cotangent[0])
    grad_near = near_ctx(grad_own)
    kv_pieces = both(kv_near)

    kv_pieces, queries = fence(kv_pieces, queries)
    total_keys = ctx_count * pair_len
    attn_rows, probs, keys, values, branch_own, *branch_rest = kernel_call(
        functools.partial(attend_kernel, scale, 2),
        [
            shape_of((pair_len, query_cols), low),
            shape_of((heads * pair_len, total_keys), low),
            shape_of((total_keys, head_dim), low),
            shape_of((total_keys, head_dim), low),
            shape_of((share, width), full),
        ]
        + [shape_of((share, width), low)] * (wt_count - 1),
        [
            pl.BlockSpec((head_step * pair_len, 1), lambda i: (0, 0)),
            pl.BlockSpec((1, total_keys), lambda i: (0, 0)),
            pl.BlockSpec((head_step * pair_len, head_dim), lambda i: (i, 0)),
            in_any,
        ]
        + [pl.BlockSpec((half * pair_len, 2 * head_dim), lambda i: (0, 0))] * 2,
        [row_positions, key_positions, queries, w_output, *kv_pieces],
        grid=(heads // head_step,),
        out_specs=[
            pl.BlockSpec((pair_len, query_cols), lambda i: (0, 0)),
            pl.BlockSpec((head_step * pair_len, total_keys), lambda i: (i, 0)),
            pl.BlockSpec((total_keys, head_dim), lambda i: (0, 0)),
            pl.BlockSpec((total_keys, head_dim), lambda i: (0, 0)),
        ]
        + [pl.BlockSpec((share, width), lambda i: (0, 0))] * wt_count,
        scratch_shapes=[
            pltpu.VMEM((heads // head_step, pair_len, head_step * head_dim), low),
            pltpu.VMEM(w_output.shape, low),
            pltpu.SemaphoreType.DMA,
        ],
    )
    branch_rest, branch_own, attn_rows = fence(branch_rest, branch_own, attn_rows)
    received = [swap(branch_rest[m - 1], "wt", m) for m in range(1, wt_count)]
    mid_rows, inverse_two, message = kernel_call(
        mid_kernel,
        [
            shape_of((share, width), full),
            shape_of((share, 1), full),
            shape_of((share, width + mask_cols), low),
        ],
        [in_vmem] * (3 + wt_count),
        [token_rows, moe_gain.reshape(1, -1), own_mask, branch_own, *received],
    )
    residual_rows = token_rows[0].astype(full)

    message, mid_rows = fence(message, mid_rows)
    first = [message] + [swap(message, "wt", m) for m in range(1, inner)]
    first_near = [near_ctx(first[0])]
    first, grad_near, again = fence(first, grad_near, message)
    first_near += [near_ctx(one) for one in first[1:]]
    grads = [one.reshape(half, wt_count, share, width) for one in both(grad_near)]
    others = [swap(again, "wt", m) for m in range(inner, wt_count)]
    first_near, others, grads = fence(first_near, others, grads)
    rows_first = both([one for pieces in first_near for one in pieces])
    second = joined(others)
    rows_first, second = fence(rows_first, second)
    near_second = near_ctx(second)
    rows_first = [one.reshape(inner, half * share, width + mask_cols) for one in rows_first]
    places = jnp.stack([my_expert, wt_index])
    sums_cols = width + extra_cols
    results, into = run_expert(
        0, parts, inner, True, True, rows_first, grads, router, w_gate_up, w_down, places, None, sums_cols,
    )
    results, into, near_second = fence(results, into, near_second)
    rows_second = both(near_second)

    def split_parts(near, far_sent):
        cols = near.shape[1]
        total = (near + far_sent).reshape(half, inner * share, cols)
        return [total[k] for k in range(half)]

    def plane_sum(blocks, received):
        total = blocks[0].astype(full)
        for one in received:
            total = total + one.astype(full)
        return total

    def plane_swap(blocks):
        return [swap(blocks[k], "ctx", 2 * k) for k in range(1, half)]

    def wt_parts(sums):
        return [one[w * share : (w + 1) * share] for one in sums for w in range(inner)]

    back_blocks = [split_parts(results[0], swap(results[1], "ctx", 1))]
    rows_second, back_blocks, into = fence(rows_second, back_blocks, into)
    back_received = [plane_swap(back_blocks[0])]
    results, into = run_expert(
        1, parts, inner, False, False, rows_second, grads, router, w_gate_up, w_down, places, into, sums_cols,
    )

    results, into, back_received = fence(results, into, back_received)
    back_blocks.append(split_parts(results[0], swap(results[1], "ctx", 1)))
    back_blocks, moe_far, into = fence(back_blocks, results[3], into)
    rows_all, hidden, gate_up_grad, expert_grad = into
    back_received.append(plane_swap(back_blocks[1]))
    moe_far = swap(moe_far, "ctx", 1)
    w_gate_up_grad = dot(rows_all, gate_up_grad, 0, 0)
    w_down_grad = dot(hidden, expert_grad, 0, 0)
    back_received, moe_far, w_gate_up_grad, w_down_grad, attn_rows = fence(
        back_received, moe_far, w_gate_up_grad, w_down_grad, attn_rows
    )
    moe_blocks = [[one[:, sums_cols:] for one in back_blocks[0]], split_parts(results[2], moe_far)]
    moe_received = [[one[:, sums_cols:] for one in back_received[0]]]
    back_blocks[0] = [one[:, :sums_cols] for one in back_blocks[0]]
    back_received[0] = [one[:, :sums_cols] for one in back_received[0]]
    sums = wt_parts([plane_sum(b, r) for b, r in zip(back_blocks, back_received)])
    sums_low = [one.astype(low) for one in sums[1:]]
    sums_low, attn_rows, moe_blocks = fence(sums_low, attn_rows, moe_blocks)
    received = [swap(one, "wt", m + 1) for m, one in enumerate(sums_low)]
    block_cols = width // ctx_count
    attn_messages = kernel_call(
        functools.partial(cut_kernel, half),
        [shape_of((pair_len, query_cols + 2 * block_cols), low)] * half,
        [in_smem, in_vmem, in_vmem],
        [chip, attn_rows, normed_one],
    )
    attn_near = [attn_messages[0]] + plane_swap(attn_messages)
    received, moe_blocks = fence(received, moe_blocks)
    summed = plane_sum(sums, received)
    rows_sum = summed[:, :width]
    weight_grads = (
        summed[:, width : width + experts] + summed[:, width + experts : width + 2 * experts]
    )
    chosen = own_mask[:, :experts] > 0.5
    logits = jnp.where(chosen, dot(message[:, :width], router, 1, 1), -1e30)
    shifted = jnp.where(chosen, jnp.exp(logits - jnp.max(logits, axis=-1, keepdims=True)), 0.0)
    own_routes = shifted / jnp.sum(shifted, axis=-1, keepdims=True)
    logits_grad = own_routes * (
        weight_grads - jnp.sum(own_routes * weight_grads, axis=-1, keepdims=True)
    )
    logits_cols = jnp.concatenate(split_low(logits_grad), axis=1)
    router_term = dot(logits_cols, jnp.concatenate([router, router], axis=0), 1, 0)
    normed_two_grad = rows_sum + router_term
    moe_gain_part = jnp.sum(normed_two_grad * mid_rows * inverse_two, axis=0)
    grad_rows = lax.dynamic_slice_in_dim(cotangent[0], wt_index * share, share, 0).astype(full)
    mid_grad = grad_rows + norm_back(normed_two_grad, mid_rows, inverse_two, moe_gain)
    logits_cols = jnp.pad(logits_cols, ((0, 0), (0, extra_cols - 2 * experts)))
    mid_message = jnp.concatenate([mid_grad.astype(low), logits_cols], axis=1)

    mid_message, moe_blocks = fence(mid_message, moe_blocks)
    mid_pieces = gather_wt(mid_message)
    moe_received.append(plane_swap(moe_blocks[1]))
    mid_pieces, moe_received, attn_near = fence(mid_pieces, moe_received, attn_near)
    attn_own, normed_keep, attn_give = deal(core, attn_near, query_cols)

    moe_sums = wt_parts([plane_sum(b, r) for b, r in zip(moe_blocks, moe_received)])
    moe_low = [one.astype(low) for one in moe_sums[1:]]
    moe_low, mid_pieces, attn_give = fence(moe_low, mid_pieces, attn_give)
    attn_got = swap(attn_give, "ctx", 1)
    moe_received = [swap(one, "wt", m + 1) for m, one in enumerate(moe_low)]
    kv_part_near, kv_part_far, query_grad, query_gain_part, *logits_messages, _ = kernel_call(
        functools.partial(attend_back_kernel, scale, wt_count),
        [
            shape_of((total_keys // 2, 2 * head_dim), low),
            shape_of((total_keys // 2, 2 * head_dim), low),
            shape_of((pair_len, query_cols), low),
            shape_of((1, head_dim), full),
        ]
        + [shape_of((pair_len, extra_cols + 2 * block_cols), low)] * half
        + [shape_of((pair_len, width), low)],
        [
            in_smem,
            pl.BlockSpec((head_step * head_dim, width), lambda i: (i, 0)),
            pl.BlockSpec((head_step * pair_len, total_keys), lambda i: (i, 0)),
            pl.BlockSpec((total_keys, head_dim), lambda i: (0, 0)),
            pl.BlockSpec((total_keys, head_dim), lambda i: (0, 0)),
            pl.BlockSpec((head_step * pair_len, head_dim), lambda i: (i, 0)),
            pl.BlockSpec((pair_len, head_step * head_dim), lambda i: (0, i)),
            pl.BlockSpec((1, head_dim), lambda i: (0, 0)),
            pl.BlockSpec((pair_len, head_dim), lambda i: (0, 0)),
            pl.BlockSpec((pair_len, head_dim), lambda i: (0, 0)),
        ]
        + [pl.BlockSpec((share, width + extra_cols), lambda i: (0, 0))] * wt_count,
        [
            chip, w_output, probs, keys, values, queries, raw_query, query_gain.reshape(1, -1),
            cosine, sine, *mid_pieces,
        ],
        grid=(heads // head_step,),
        out_specs=[
            pl.BlockSpec((total_keys // 2, 2 * head_dim), lambda i: (0, 0)),
            pl.BlockSpec((total_keys // 2, 2 * head_dim), lambda i: (0, 0)),
            pl.BlockSpec((pair_len, head_step * head_dim), lambda i: (0, i)),
            pl.BlockSpec((1, head_dim), lambda i: (0, 0)),
        ]
        + [pl.BlockSpec((pair_len, extra_cols + 2 * block_cols), lambda i: (0, 0))] * half
        + [pl.BlockSpec((pair_len, width), lambda i: (0, 0))],
        scratch_shapes=[pltpu.VMEM((total_keys, 2 * head_dim), full)],
    )

    kv_part_near, kv_part_far, query_grad, moe_received, attn_got = fence(
        kv_part_near, kv_part_far, query_grad, moe_received, attn_got
    )
    kv_near = (kv_part_near + swap(kv_part_far, "ctx", 1)).reshape(half, pair_len, 2 * head_dim)
    kv_near = [kv_near[k] for k in range(half)]
    out_rows = (mid_rows + plane_sum(moe_sums, moe_received)).astype(low)
    kv_near, query_grad, out_rows = fence(kv_near, query_grad, out_rows)
    kv_received = plane_swap(kv_near)
    out_pieces = gather_wt(out_rows)
    query_term = dot(query_grad, w_query, 1, 1)
    kv_received, query_term = fence(kv_received, query_term)
    one_own, *one_rest, projection_own, key_gain_part, attn_gain_part = kernel_call(
        functools.partial(tail_kernel, half),
        [shape_of((share, width), full)]
        + [shape_of((share, width), low)] * (wt_count - 1)
        + [
            shape_of((pair_len, query_cols + 2 * head_dim), low),
            shape_of((1, head_dim), full),
            shape_of((1, width), full),
        ],
        [in_vmem] * (10 + half),
        [
            query_term, query_grad, raw_key, key_gain.reshape(1, -1), cosine, sine, key_weight,
            value_weight, token_rows, inverse_one, kv_near[0], *kv_received,
        ],
    )
    gains = jnp.concatenate(
        [attn_gain_part[0], moe_gain_part, query_gain_part[0], key_gain_part[0]]
    ).reshape(-1, 128)

    one_own, one_rest, projection_own, gains, logits_messages = fence(
        one_own, one_rest, projection_own, gains, logits_messages
    )
    received = [swap(one, "wt", m + 1) for m, one in enumerate(one_rest)]
    logits_near = [logits_messages[0]] + plane_swap(logits_messages)
    projection_near = near_ctx(projection_own)
    gains = gains + swap(gains, "ctx", 1)
    block_out = place_rows(index, out_pieces)
    received, logits_near, gains, block_out = fence(received, logits_near, gains, block_out)
    normed_rows = plane_sum([one_own], received)
    input_rows = mid_grad + norm_back(normed_rows, residual_rows, inverse_one[:share], attn_gain)
    input_rows = input_rows.astype(low)

    input_rows, logits_near, gains = fence(input_rows, logits_near, gains)
    input_pieces = gather_wt(input_rows)
    steps = []
    mask = 2
    while mask < ctx_count:
        steps.append(("ctx", mask))
        mask *= 2
    mask = 1
    while mask < wt_count:
        steps.append(("wt", mask))
        mask *= 2

    def add_gains(gains, step):
        return gains + swap(gains, *step)

    logits_own, mid_keep, logits_give = deal(core, logits_near, extra_cols)
    logits_give, gains = fence(logits_give, gains)
    logits_got = swap(logits_give, "ctx", 1)
    gains = add_gains(gains, steps[0])
    projection_both = both(projection_near)
    logits_got, gains, projection_both = fence(logits_got, gains, projection_both)
    gains = add_gains(gains, steps[1])
    w_output_grad = kernel_call(
        output_kernel,
        shape_of((query_cols, block_cols), full),
        [in_vmem] * 4,
        [attn_own, attn_got, mid_keep, logits_got],
    )
    gains, w_output_grad = fence(gains, w_output_grad)
    gains = add_gains(gains, steps[2])
    rows_blocks = rows_all.reshape(parts, ctx_count, inner, share, width)
    router_grad = kernel_call(
        router_kernel,
        shape_of((experts, width), full),
        [in_smem, in_any, in_vmem, in_vmem],
        [jnp.stack([ctx_index, wt_index]), rows_blocks, logits_own, logits_got],
        scratch_shapes=[
            pltpu.VMEM((ctx_count * wt_count, share, width), low),
            pltpu.VMEM((ctx_count * wt_count, share, extra_cols), low),
            pltpu.SemaphoreType.DMA((ctx_count * wt_count,)),
        ],
    )
    gains, router_grad = fence(gains, router_grad)
    w_router_grad = router_grad.T
    for step in steps[3:]:
        gains = add_gains(gains, step)
    gains = gains.reshape(-1)
    w_query_grad, w_key_grad, w_value_grad = kernel_call(
        projection_kernel,
        [
            shape_of((block_cols, query_cols), full),
            shape_of((block_cols, head_dim), full),
            shape_of((block_cols, head_dim), full),
        ],
        [in_vmem] * 4,
        [normed_keep, attn_got, *projection_both],
    )
    tokens_grad = place_rows(index, input_pieces)

    return (
        block_out.reshape(1, pair_len, width),
        tokens_grad.reshape(1, pair_len, width),
        gains[:width],
        gains[2 * width : 2 * width + head_dim],
        gains[2 * width + head_dim :],
        w_query_grad,
        w_key_grad,
        w_value_grad,
        w_output_grad,
        gains[width : 2 * width],
        w_router_grad,
        w_gate_up_grad[None],
        w_down_grad[None],
    )


def solution(mesh):
    in_specs = (
        P(None, "ctx", None),
        P(None, "ctx", None),
        P(("ctx", "wt"), None),
        P(),
        P(),
        P(),
        P(None, "wt"),
        P(None, "wt"),
        P(None, "wt"),
        P("wt", None),
        P(),
        P(),
        P(("ctx", "wt"), None, None),
        P(("ctx", "wt"), None, None),
    )
    out_specs = (
        P(None, "ctx", None),
        P(None, "ctx", None),
        P(),
        P(),
        P(),
        P("ctx", "wt"),
        P("ctx", "wt"),
        P("ctx", "wt"),
        P("wt", "ctx"),
        P(),
        P(),
        P(("ctx", "wt"), None, None),
        P(("ctx", "wt"), None, None),
    )
    return jax.shard_map(
        on_device, mesh=mesh, in_specs=in_specs, out_specs=out_specs, check_vma=False
    )
```

```python
import functools

import jax
import jax.numpy as jnp
from jax import lax
from jax.experimental import pallas as pl
from jax.experimental.pallas import tpu as pltpu
from jax.sharding import PartitionSpec as P

epsilon = 1e-06
rope_base = 1000000.0
low = jnp.bfloat16
full = jnp.float32
vmem_bytes = 60 * 1024 * 1024

in_vmem = pl.BlockSpec(memory_space=pltpu.VMEM)
in_smem = pl.BlockSpec(memory_space=pltpu.SMEM)
in_any = pl.BlockSpec(memory_space=pl.ANY)


def dot(a, b, a_dim=1, b_dim=0):
    return lax.dot_general(a, b, (((a_dim,), (b_dim,)), ((), ())), preferred_element_type=full)


def swap(array, axis, mask):
    count = lax.axis_size(axis)
    return lax.ppermute(array, axis, [(i, i ^ mask) for i in range(count)])


def fence(*values):
    return lax.optimization_barrier(values)


def shape_of(shape, dtype):
    return jax.ShapeDtypeStruct(tuple(shape), dtype)


def kernel_call(kernel, outs, ins, args, after=(), through=(), **more):
    single = not isinstance(outs, list)
    outs = [outs] if single else list(outs)
    after, through = jax.tree.leaves(after), jax.tree.leaves(through)
    count, lead = len(args), len(outs)
    every = count + len(after) + len(through)

    def body(*refs):
        kernel(*refs[:count], *refs[every : every + lead], *refs[every + lead + len(through) :])

    aliases = dict(more.pop("input_output_aliases", {}))
    if through:
        aliases.update({count + len(after) + i: lead + i for i in range(len(through))})
        more["out_specs"] = list(more.get("out_specs", [in_vmem] * lead)) + [in_any] * len(through)
    results = pl.pallas_call(
        body,
        out_shape=outs + [shape_of(one.shape, one.dtype) for one in through],
        in_specs=[*ins] + [in_any] * (len(after) + len(through)),
        input_output_aliases=aliases,
        compiler_params=pltpu.CompilerParams(vmem_limit_bytes=vmem_bytes),
        **more,
    )(*args, *after, *through)
    return results[0] if single else results


def rms_scale(value_matrix):
    return lax.rsqrt(jnp.mean(value_matrix * value_matrix, axis=-1, keepdims=True) + epsilon)


def norm_back(grad_out, value_matrix, inverse, gain_vec):
    scaled = grad_out * gain_vec
    inner_mean = jnp.mean(scaled * value_matrix, axis=-1, keepdims=True)
    return inverse * (scaled - value_matrix * inverse * inverse * inner_mean)


def mirrored(device, offset, groups, block_len):
    which_block = jnp.where(offset < block_len, device, 2 * groups - 1 - device)
    return which_block * block_len + offset % block_len


def rotate(value_matrix, cosine, sine):
    return value_matrix * cosine + pltpu.roll(value_matrix, value_matrix.shape[-1] // 2, 1) * sine


def front_kernel(
    index_ref, x_ref, gain_ref, kw_ref, vw_ref, kgain_ref, cos_ref, sin_ref,
    rows_ref, normed_ref, inv_ref, raw_ref, *message_refs
):
    blocks, share, _ = x_ref.shape
    for i in range(blocks):
        x_low = x_ref[index_ref[0] ^ i]
        rows_ref[i] = x_low
        x = x_low.astype(full)
        inverse = rms_scale(x)
        inv_ref[i * share : (i + 1) * share] = inverse
        normed_ref[i * share : (i + 1) * share] = (x * inverse * gain_ref[...]).astype(low)
    normed = normed_ref[...]
    raw = dot(normed, kw_ref[...])
    raw_ref[...] = raw
    head_dim = raw.shape[1]
    turned = rotate(raw * rms_scale(raw) * kgain_ref[...], cos_ref[...], sin_ref[...])
    keys = turned.astype(low)
    values = dot(normed, vw_ref[...]).astype(low)
    for k, ref in enumerate(message_refs):
        ref[:, :head_dim] = keys
        ref[:, head_dim : 2 * head_dim] = values
        cols = ref.shape[1] - 2 * head_dim
        start = pl.multiple_of((index_ref[1] ^ k) * cols, 128)
        ref[:, 2 * head_dim :] = normed_ref[:, pl.ds(start, cols)]


def query_kernel(normed_ref, w_ref, gain_ref, cos_ref, sin_ref, raw_ref, q_ref):
    rows, head_dim = cos_ref.shape
    raw = dot(normed_ref[...], w_ref[...])
    raw_ref[...] = raw
    for h in range(raw.shape[1] // head_dim):
        one = raw[:, h * head_dim : (h + 1) * head_dim]
        turned = rotate(one * rms_scale(one) * gain_ref[...], cos_ref[...], sin_ref[...])
        q_ref[h * rows : (h + 1) * rows] = turned.astype(low)


def attend_kernel(scale, pieces, qpos_ref, kpos_ref, q_ref, w_ref, *refs):
    kv_refs = refs[:pieces]
    rows_ref, probs_ref, keys_ref, values_ref, own_ref, *rest_refs, attn, weight, sem = refs[pieces:]
    step = pl.program_id(0)
    tokens, head_dim = rows_ref.shape[0], kv_refs[0].shape[1] // 2
    copy = pltpu.make_async_copy(w_ref, weight, sem)

    @pl.when(step == 0)
    def _():
        copy.start()
        at = 0
        for ref in kv_refs:
            keys_ref[at : at + ref.shape[0]] = ref[:, :head_dim]
            values_ref[at : at + ref.shape[0]] = ref[:, head_dim : 2 * head_dim]
            at += ref.shape[0]

    scores = dot(q_ref[...], keys_ref[...], 1, 1) * scale
    scores = jnp.where(kpos_ref[...] <= qpos_ref[...], scores, -1e30)
    weights = jnp.exp(scores - jnp.max(scores, axis=-1, keepdims=True))
    probs = (weights / jnp.sum(weights, axis=-1, keepdims=True)).astype(low)
    probs_ref[...] = probs
    out = dot(probs, values_ref[...]).astype(low)
    heads = out.shape[0] // tokens
    attn[step] = jnp.concatenate([out[h * tokens : (h + 1) * tokens] for h in range(heads)], axis=1)

    @pl.when(step == pl.num_programs(0) - 1)
    def _():
        copy.wait()
        for i in range(attn.shape[0]):
            rows_ref[:, i * heads * head_dim : (i + 1) * heads * head_dim] = attn[i]
        total = dot(rows_ref[...], weight[...])
        share = own_ref.shape[0]
        own_ref[...] = total[:share]
        for i, ref in enumerate(rest_refs):
            ref[...] = total[(i + 1) * share : (i + 2) * share].astype(low)


def mid_kernel(x_ref, gain_ref, mask_ref, own_ref, *refs):
    received, (mid_ref, inv_ref, message_ref) = refs[:-3], refs[-3:]
    mid = own_ref[...]
    for one in received:
        mid = mid + one[...].astype(full)
    mid = x_ref[0].astype(full) + mid
    inverse = rms_scale(mid)
    mid_ref[...] = mid
    inv_ref[...] = inverse
    width = mid.shape[1]
    message_ref[:, :width] = (mid * inverse * gain_ref[...]).astype(low)
    message_ref[:, width:] = mask_ref[...]


def expert_kernel(
    tiles, first, inner, merged, index_ref, row_near, row_far, grad_near, grad_far, router_ref,
    gu_any, down_any, *refs
):
    if merged:
        near_ref, far_ref, *refs = refs
        moe_near_ref, moe_far_ref = near_ref, far_ref
    else:
        near_ref, far_ref, moe_near_ref, moe_far_ref, *refs = refs
    x_ref, hidden_ref, dgu_ref, deo_ref, x_tile, g_tile, gu, down, sems = refs
    step = pl.program_id(0)
    width = g_tile.shape[1]
    ffw = down.shape[0]
    experts = router_ref.shape[0]
    expert = index_ref[0]
    chips, _, share, _ = grad_near.shape
    copy_gu = pltpu.make_async_copy(gu_any.at[0], gu, sems.at[0])
    copy_down = pltpu.make_async_copy(down_any.at[0], down, sems.at[1])

    @pl.when(step == 0)
    def _():
        copy_gu.start()
        copy_down.start()

    def load(row_ref, grad_ref):
        x_tile[...] = row_ref[...]
        for c in range(chips):
            for w in range(inner):
                to = slice((c * inner + w) * share, (c * inner + w + 1) * share)
                g_tile[to] = grad_ref[c, index_ref[1] ^ (first + w)][:, : g_tile.shape[1]]

    @pl.when(step < tiles // 2)
    def _():
        load(row_near, grad_near)

    @pl.when(step >= tiles // 2)
    def _():
        load(row_far, grad_far)

    x = x_tile[:, :width]
    x_ref[...] = x
    g = g_tile[...].astype(full)
    chosen = x_tile[:, width:][:, :experts].astype(full) > 0.5
    logits = jnp.where(chosen, dot(x, router_ref[...], 1, 1), -1e30)
    shifted = jnp.exp(logits - jnp.max(logits, axis=-1, keepdims=True))
    shifted = jnp.where(chosen, shifted, 0.0)
    mine = lax.broadcasted_iota(jnp.int32, shifted.shape, 1) == expert
    own = jnp.sum(jnp.where(mine, shifted, 0.0), axis=-1, keepdims=True) / jnp.sum(
        shifted, axis=-1, keepdims=True
    )
    deo = (g * own).astype(low)
    deo_ref[...] = deo

    @pl.when(step == 0)
    def _():
        copy_gu.wait()

    gate_up = dot(x, gu[...])

    @pl.when(step == 0)
    def _():
        copy_down.wait()

    gate, up = gate_up[:, :ffw], gate_up[:, ffw:]
    dhid = dot(deo, down[...], 1, 1)
    sig = jax.nn.sigmoid(gate)
    silu = gate * sig
    hidden = (silu * up).astype(low)
    hidden_ref[...] = hidden
    dgate = (dhid * up * (sig + silu * (1.0 - sig))).astype(low)
    dup = (dhid * silu).astype(low)
    dgu_ref[:, :ffw] = dgate
    dgu_ref[:, ffw:] = dup
    out = dot(hidden, down[...]).astype(low).astype(full)
    dlw = jnp.sum(out * g, axis=-1, keepdims=True)
    moe = (out * own).astype(low)
    back = (dot(dgate, gu[:, :ffw], 1, 1) + dot(dup, gu[:, ffw:], 1, 1)).astype(low)
    high = dlw.astype(low)
    rest = (dlw - high.astype(full)).astype(low).astype(full)
    cols = near_ref.shape[1] - (2 if merged else 1) * width
    lane = lax.broadcasted_iota(jnp.int32, (x.shape[0], cols), 1)
    extra = jnp.where(lane == expert, high.astype(full), 0.0)
    extra = jnp.where(lane == experts + expert, rest, extra).astype(low)

    def store(row_ref, moe_ref):
        row_ref[:, :width] = back
        row_ref[:, width : width + cols] = extra
        moe_ref[:, moe_ref.shape[1] - width :] = moe

    @pl.when(step < tiles // 2)
    def _():
        store(near_ref, moe_near_ref)

    @pl.when(step >= tiles // 2)
    def _():
        store(far_ref, moe_far_ref)


def run_expert(part, part_count, inner, merged, rows, grads, router, w_gate_up, w_down, index, into, cols):
    chips, wt_count, share, width = grads[0].shape
    half_rows = chips * inner * share
    tile = min(256, half_rows)
    near = half_rows // tile
    tiles = 2 * near
    each = chips // near
    ffw = w_down.shape[1]
    wide = rows[0].shape[-1]
    everything = 2 * half_rows * part_count
    offset = part * tiles
    near_map = lambda i: (jnp.minimum(i, near - 1), 0)
    far_map = lambda i: (jnp.maximum(i - near, 0), 0)
    all_map = lambda i: (i + offset, 0)
    widths = [cols + width] if merged else [cols, width]
    outs, out_specs = [], []
    for one in widths:
        outs += [shape_of((half_rows, one), low)] * 2
        out_specs += [pl.BlockSpec((tile, one), near_map), pl.BlockSpec((tile, one), far_map)]
    lead_outs = len(outs)
    for one in (width, ffw, 2 * ffw, width):
        outs.append(shape_of((everything, one), low))
        out_specs.append(pl.BlockSpec((tile, one), all_map))
    ins = [in_smem]
    for where in (near_map, far_map):
        ins.append(pl.BlockSpec((tile, wide), where))
    for where, grad in ((near_map, grads[0]), (far_map, grads[1])):
        ins.append(pl.BlockSpec((each, *grad.shape[1:]), lambda i, where=where: (where(i)[0], 0, 0, 0)))
    ins += [pl.BlockSpec(router.shape, lambda i: (0, 0)), in_any, in_any]
    args = [index, *rows, *grads, router, w_gate_up, w_down]
    lead = len(args)
    aliases = {}
    if into is not None:
        for i, array in enumerate(into):
            aliases[len(args)] = lead_outs + i
            ins.append(in_any)
            args.append(array)

    def body(*refs):
        expert_kernel(tiles, part * inner, inner, merged, *refs[:lead], *refs[len(args) :])

    results = kernel_call(
        body,
        outs,
        ins,
        args,
        grid=(tiles,),
        out_specs=out_specs,
        scratch_shapes=[
            pltpu.VMEM((tile, wide), low),
            pltpu.VMEM((tile, width), low),
            pltpu.VMEM(w_gate_up.shape[1:], low),
            pltpu.VMEM(w_down.shape[1:], low),
            pltpu.SemaphoreType.DMA((2,)),
        ],
        input_output_aliases=aliases,
    )
    return results[:lead_outs], results[lead_outs:]


def pack_kernel(attn_ref, *refs):
    out_ref, share = refs[-1], refs[0].shape[0]
    wide = refs[0].shape[1]
    for i, ref in enumerate(refs[:-1]):
        out_ref[i * share : (i + 1) * share, :wide] = ref[...]
    rows, cols = out_ref.shape[0], attn_ref.shape[1]
    for i in range(attn_ref.shape[0] // rows):
        out_ref[:, wide + i * cols : wide + (i + 1) * cols] = attn_ref[i * rows : (i + 1) * rows]


def unpack_kernel(*refs):
    in_refs, (rows_ref, attn_ref) = refs[:-2], refs[-2:]
    rows, wide, cols = in_refs[0].shape[0], rows_ref.shape[1], attn_ref.shape[1]
    at = 0
    for i, ref in enumerate(in_refs):
        rows_ref[i * rows : (i + 1) * rows] = ref[:, :wide]
        for j in range((ref.shape[1] - wide) // cols):
            attn_ref[at : at + rows] = ref[:, wide + j * cols : wide + (j + 1) * cols]
            at += rows


def last_kernel(index_ref, x_ref, inv_ref, gain_ref, grad_ref, out_rows_ref, proj_ref, gains_ref, own_ref, *refs):
    *received, last_ref, message_ref, parts, stack = refs
    total = own_ref[...]
    share, width = total.shape
    for one in received:
        total = total + one[:, :width].astype(full)
    last_ref[:, :width] = out_rows_ref[...]
    grad = grad_ref[...] + norm_back(total, x_ref[0].astype(full), inv_ref[:share], gain_ref[...])
    last_ref[:, width:] = grad.astype(low)
    parts[index_ref[0]] = gains_ref[...]
    for i, one in enumerate(received):
        for j in range(gains_ref.shape[0] // share):
            cols = slice(width + j * 128, width + (j + 1) * 128)
            parts[index_ref[0] ^ (i + 1), j * share : (j + 1) * share] = one[:, cols].astype(full)
    gains = parts[0]
    for i in range(1, parts.shape[0]):
        gains = gains + parts[i]
    count = 2 * width // 128 + 2 * 1
    stack_split(stack, gains[:count] + gains[count : 2 * count])
    rows = proj_ref.shape[0]
    more = message_ref.shape[0] - rows
    message_ref[:rows] = proj_ref[...]
    message_ref[rows:] = jnp.zeros((more, message_ref.shape[1]), low)
    for j in range(stack.shape[0] // more):
        message_ref[rows:, j * 128 : (j + 1) * 128] = stack[j * more : (j + 1) * more].astype(low)


def join_kernel(*refs):
    out_ref, at = refs[-1], 0
    for ref in refs[:-1]:
        out_ref[at : at + ref.shape[0]] = ref[...]
        at += ref.shape[0]


def join(pieces, after=()):
    rows = sum(one.shape[0] for one in pieces)
    return kernel_call(
        join_kernel,
        shape_of((rows, pieces[0].shape[1]), pieces[0].dtype),
        [in_vmem] * len(pieces),
        list(pieces),
        after,
    )


def cut_kernel(pieces, index_ref, rows_ref, from_ref, *out_refs):
    whole = rows_ref.shape[1]
    cols = out_refs[0].shape[1] - whole
    for k in range(pieces):
        out_refs[k][:, :whole] = rows_ref[...]
        start = pl.multiple_of((index_ref[0] ^ k) * cols, 128)
        out_refs[k][:, whole:] = from_ref[:, pl.ds(start, cols)]


def deal_kernel(pieces, whole, index_ref, *refs):
    in_refs, (own_ref, keep_ref, give_ref) = refs[:pieces], refs[pieces:]
    rows = in_refs[0].shape[0]
    cols = (in_refs[0].shape[1] - whole) // 2
    for i, ref in enumerate(in_refs):
        at = slice(i * rows, (i + 1) * rows)
        own_ref[at] = ref[:, :whole]
        give_ref[at, :whole] = ref[:, :whole]
        keep = pl.multiple_of(whole + index_ref[0] * cols, 128)
        give = pl.multiple_of(whole + (1 - index_ref[0]) * cols, 128)
        keep_ref[at] = ref[:, pl.ds(keep, cols)]
        give_ref[at, whole:] = ref[:, pl.ds(give, cols)]


def deal(core, pieces, whole, **more):
    rows, wide = pieces[0].shape
    cols = (wide - whole) // 2
    total = rows * len(pieces)
    return kernel_call(
        functools.partial(deal_kernel, len(pieces), whole),
        [shape_of((total, whole), low), shape_of((total, cols), low), shape_of((total, whole + cols), low)],
        [in_smem] + [in_vmem] * len(pieces),
        [core, *pieces],
        **more,
    )


def attend_back_kernel(scale, pieces, index_ref, w_ref, probs_ref, keys_ref, values_ref, q_ref, raw_ref,
                       gain_ref, cos_ref, sin_ref, *refs):
    da_refs = refs[:pieces]
    kv_near_ref, kv_far_ref, dq_ref, part_ref, *message_refs, da_ref, acc = refs[pieces:]
    step = pl.program_id(0)
    tokens, head_dim = cos_ref.shape
    share = da_refs[0].shape[0]
    width = da_ref.shape[1]
    logit_cols = da_refs[0].shape[1] - width

    @pl.when(step == 0)
    def _():
        for i, ref in enumerate(da_refs):
            da_ref[i * share : (i + 1) * share] = ref[:, :width]
            for k, one in enumerate(message_refs):
                one[i * share : (i + 1) * share, :logit_cols] = ref[:, width:]
        for k, one in enumerate(message_refs):
            cols = one.shape[1] - logit_cols
            start = pl.multiple_of((index_ref[0] ^ k) * cols, 128)
            one[:, logit_cols:] = da_ref[:, pl.ds(start, cols)]
        acc[...] = jnp.zeros_like(acc)
        part_ref[...] = jnp.zeros_like(part_ref)

    dattn = dot(da_ref[...], w_ref[...], 1, 1).astype(low)
    heads = dattn.shape[1] // head_dim
    out_grad = jnp.concatenate(
        [dattn[:, h * head_dim : (h + 1) * head_dim] for h in range(heads)], axis=0
    )
    probs_low = probs_ref[...]
    probs = probs_low.astype(full)
    prob_grad = dot(out_grad, values_ref[...], 1, 1)
    inner = jnp.sum(probs * prob_grad, axis=-1, keepdims=True)
    score_grad = (probs * (prob_grad - inner)).astype(low)
    query_grad = (dot(score_grad, keys_ref[...]) * scale).astype(low).astype(full)
    acc[:, :head_dim] += dot(score_grad, q_ref[...], 0, 0)
    acc[:, head_dim:] += dot(probs_low, out_grad, 0, 0)
    gain = gain_ref[...]
    part = part_ref[...]
    for h in range(heads):
        cols = slice(h * head_dim, (h + 1) * head_dim)
        turned = rotate(query_grad[h * tokens : (h + 1) * tokens], cos_ref[...], -sin_ref[...])
        raw = raw_ref[:, cols]
        inverse = rms_scale(raw)
        part = part + jnp.sum(turned * raw * inverse, axis=0, keepdims=True)
        dq_ref[:, cols] = norm_back(turned, raw, inverse, gain).astype(low)
    part_ref[...] = part

    @pl.when(step == pl.num_programs(0) - 1)
    def _():
        near = kv_near_ref.shape[0]
        for ref, at in ((kv_near_ref, 0), (kv_far_ref, near)):
            ref[:, :head_dim] = (acc[at : at + near, :head_dim] * scale).astype(low)
            ref[:, head_dim:] = acc[at : at + near, head_dim:].astype(low)


def stack_rows(stack, at, row):
    for k in range(row.shape[1] // 128):
        stack[at + k : at + k + 1] = row[:, k * 128 : (k + 1) * 128]


def stack_split(stack, values):
    count = values.shape[0]
    high = values.astype(low).astype(full)
    stack[...] = jnp.zeros_like(stack)
    stack[:count] = high
    stack[count : 2 * count] = (values - high).astype(low).astype(full)


def tail_kernel(pieces, moe_part_ref, query_part_ref, dn_ref, dq_ref, raw_ref, kgain_ref, cos_ref, sin_ref, kw_ref, vw_ref, x_ref,
                inv_ref, *refs):
    kv_refs = refs[:pieces]
    own_ref, *rest_refs, proj_ref, gains_ref, values = refs[pieces:]
    total = kv_refs[0][...].astype(full)
    for ref in kv_refs[1:]:
        total = total + ref[...].astype(full)
    head_dim = raw_ref.shape[1]
    query_cols = dq_ref.shape[1]
    turned = rotate(total[:, :head_dim].astype(low).astype(full), cos_ref[...], -sin_ref[...])
    dv = total[:, head_dim:].astype(low)
    raw = raw_ref[...]
    inverse = rms_scale(raw)
    key_part = jnp.sum(turned * raw * inverse, axis=0, keepdims=True)
    dk = norm_back(turned, raw, inverse, kgain_ref[...]).astype(low)
    proj_ref[:, :query_cols] = dq_ref[...]
    proj_ref[:, query_cols : query_cols + head_dim] = dk
    proj_ref[:, query_cols + head_dim :] = dv
    grad = dn_ref[...] + dot(dk, kw_ref[...], 1, 1) + dot(dv, vw_ref[...], 1, 1)
    blocks, share, _ = x_ref.shape
    width = grad.shape[1]
    part = jnp.zeros((1, width), full)
    for i in range(blocks):
        one = grad[i * share : (i + 1) * share]
        x = x_ref[i].astype(full)
        part = part + jnp.sum(one * x * inv_ref[i * share : (i + 1) * share], axis=0, keepdims=True)
        if i == 0:
            own_ref[...] = one
        else:
            rest_refs[i - 1][:, :width] = one.astype(low)
    stack_rows(values, 0, part)
    stack_rows(values, width // 128, moe_part_ref[...])
    stack_rows(values, 2 * width // 128, query_part_ref[...])
    stack_rows(values, (2 * width + head_dim) // 128, key_part)
    stack_split(gains_ref, values[...])
    for ref in rest_refs:
        for j in range(gains_ref.shape[0] // share):
            cols = slice(width + j * 128, width + (j + 1) * 128)
            ref[:, cols] = gains_ref[j * share : (j + 1) * share].astype(low)


def output_kernel(a_near, a_far, b_near, b_far, out_ref):
    rows, cols = out_ref.shape
    far = b_far.shape[1] - cols
    out_ref[...] = dot(a_near[...], b_near[...], 0, 0) + dot(a_far[:, :rows], b_far[:, far:], 0, 0)


def projection_kernel(pieces, index_ref, a_near, a_far, b_near, b_far, query_ref, key_ref, value_ref, *refs):
    *gain_refs, b, parts = refs
    far = a_far.shape[1] - a_near.shape[1]
    each = a_near.shape[0] // pieces
    rows = b_near.shape[0] // pieces
    more = rows - each
    for i, b_ref in enumerate((b_near, b_far)):
        for k in range(pieces):
            at = i * pieces + k
            b[at * each : (at + 1) * each] = b_ref[k * rows : k * rows + each]
            for j in range(parts.shape[1] // more):
                cols = slice(j * 128, (j + 1) * 128)
                parts[index_ref[0] ^ (2 * k + i), j * more : (j + 1) * more] = b_ref[
                    k * rows + each : (k + 1) * rows, cols
                ].astype(full)
    gains = parts[0]
    for i in range(1, 2 * pieces):
        gains = gains + parts[i]
    count = sum(ref.shape[0] for ref in gain_refs)
    gains = gains[:count] + gains[count : 2 * count]
    at = 0
    for ref in gain_refs:
        ref[...] = gains[at : at + ref.shape[0]]
        at += ref.shape[0]
    half = pieces * each
    total = dot(a_near[...], b[:half], 0, 0) + dot(a_far[:, far:], b[half:], 0, 0)
    cols, more = query_ref.shape[1], key_ref.shape[1]
    query_ref[...] = total[:, :cols]
    key_ref[...] = total[:, cols : cols + more]
    value_ref[...] = total[:, cols + more :]


def router_kernel(index_ref, rows_any, near_ref, far_ref, out_ref, rows, grads, sems):
    part_count, groups, inner, share, _ = rows_any.shape
    copies = []
    for p in range(part_count):
        for c in range(groups):
            half = groups // 2
            mask = 2 * (c % half) + c // half
            for w in range(inner):
                to = (index_ref[0] ^ mask) * (part_count * inner) + (index_ref[1] ^ (p * inner + w))
                copy = pltpu.make_async_copy(rows_any.at[p, c, w], rows.at[to], sems.at[len(copies)])
                copy.start()
                copies.append(copy)
                grad_ref = near_ref if c < half else far_ref
                at = ((c % half) * (part_count * inner) + p * inner + w) * share
                grads[to] = grad_ref[at : at + share, : grads.shape[2]]
    for copy in copies:
        copy.wait()
    count = rows.shape[0] * share
    total = dot(grads[...].reshape(count, grads.shape[2]), rows[...].reshape(count, rows.shape[2]), 0, 0)
    experts = out_ref.shape[0]
    out_ref[...] = total[:experts] + total[experts : 2 * experts]


def place_kernel(pieces, index_ref, *refs):
    piece_refs, out_refs = refs[:pieces], refs[pieces:]
    width = out_refs[0].shape[2]
    for i, ref in enumerate(piece_refs):
        for j, out_ref in enumerate(out_refs):
            out_ref[index_ref[0] ^ i] = ref[:, j * width : (j + 1) * width]


def place_rows(index, pieces, width, count, **more):
    share = pieces[0].shape[0]
    return kernel_call(
        functools.partial(place_kernel, len(pieces)),
        [shape_of((len(pieces), share, width), pieces[0].dtype)] * count,
        [in_smem] + [in_vmem] * len(pieces),
        [index.reshape(1), *pieces],
        **more,
    )


def gather_wt(array):
    return [array] + [swap(array, "wt", m) for m in range(1, lax.axis_size("wt"))]


def near_ctx(array):
    return [array] + [swap(array, "ctx", 2 * k) for k in range(1, lax.axis_size("ctx") // 2)]


def far_ctx(arrays):
    return [swap(one, "ctx", 1) for one in arrays]


def split_low(array):
    high = array.astype(low)
    return high, (array - high.astype(full)).astype(low)


def on_device(
    tokens,
    cotangent,
    routes,
    attn_gain,
    query_gain,
    key_gain,
    w_query,
    key_weight,
    value_weight,
    w_output,
    moe_gain,
    w_router,
    w_gate_up,
    w_down,
):
    _, pair_len, width = tokens.shape
    head_dim = query_gain.shape[0]
    query_cols = w_query.shape[1]
    heads = query_cols // head_dim
    share, top_count = routes.shape
    experts = w_router.shape[1]
    ctx_count = lax.axis_size("ctx")
    wt_count = lax.axis_size("wt")
    half = ctx_count // 2
    ctx_index = lax.axis_index("ctx")
    wt_index = lax.axis_index("wt")
    my_expert = ctx_index * wt_count + wt_index
    scale = head_dim ** (-0.5)
    head_step = 2
    parts = 2
    inner = wt_count // parts
    mask_cols = -(-experts // 128) * 128
    extra_cols = -(-2 * experts // 128) * 128
    index = wt_index.reshape(1)
    chip = (ctx_index >> 1).reshape(1)
    core = (ctx_index & 1).reshape(1)
    router = w_router.T

    def plane_swap(blocks):
        return [swap(blocks[k], "ctx", 2 * k) for k in range(1, half)]

    def joined(pieces):
        return jnp.concatenate(pieces, axis=0) if len(pieces) > 1 else pieces[0]

    def both(pieces, after=()):
        near = join(pieces, after)
        return [near, swap(near, "ctx", 1)]


    place = jnp.arange(pair_len, dtype=jnp.int32)
    offsets = ((place // share) ^ wt_index) * share + place % share
    near_masks = 2 * jnp.arange(half, dtype=jnp.int32)
    masks = jnp.concatenate([near_masks, near_masks + 1])
    own_positions = mirrored(ctx_index, offsets, ctx_count, pair_len // 2)
    key_positions = mirrored(
        (ctx_index ^ masks)[:, None], offsets[None, :], ctx_count, pair_len // 2
    ).reshape(1, -1)
    row_positions = jnp.tile(own_positions, head_step).reshape(-1, 1)
    frequency = rope_base ** (-2.0 * jnp.arange(head_dim // 2, dtype=full) / head_dim)
    angles = own_positions.astype(full)[:, None] * frequency[None, :]
    cosine, sine = jnp.cos(angles), jnp.sin(angles)
    cosine = jnp.concatenate([cosine, cosine], axis=1)
    sine = jnp.concatenate([-sine, sine], axis=1)

    expert_ids = jnp.arange(mask_cols, dtype=jnp.int32)
    own_mask = jnp.any(routes[:, :, None] == expert_ids, axis=1).astype(low)
    block_cols = width // ctx_count
    token_rows, normed_one, inverse_one, raw_key, *kv_messages = kernel_call(
        front_kernel,
        [
            shape_of((wt_count, share, width), low),
            shape_of((pair_len, width), low),
            shape_of((pair_len, 1), full),
            shape_of((pair_len, head_dim), full),
        ]
        + [shape_of((pair_len, 2 * head_dim + 2 * block_cols), low)] * half,
        [in_smem] + [in_vmem] * 7,
        [
            jnp.stack([wt_index, ctx_index >> 1]),
            tokens.reshape(wt_count, share, width),
            attn_gain.reshape(1, -1),
            key_weight,
            value_weight,
            key_gain.reshape(1, -1),
            cosine,
            sine,
        ],
    )

    kv_near = [kv_messages[0]] + plane_swap(kv_messages)
    raw_query, queries = kernel_call(
        query_kernel,
        [shape_of((pair_len, query_cols), full), shape_of((heads * pair_len, head_dim), low)],
        [
            pl.BlockSpec((pair_len, width), lambda i: (0, 0)),
            pl.BlockSpec((width, head_step * head_dim), lambda i: (0, i)),
            pl.BlockSpec((1, head_dim), lambda i: (0, 0)),
            pl.BlockSpec((pair_len, head_dim), lambda i: (0, 0)),
            pl.BlockSpec((pair_len, head_dim), lambda i: (0, 0)),
        ],
        [normed_one, w_query, query_gain.reshape(1, -1), cosine, sine],
        grid=(heads // head_step,),
        out_specs=[
            pl.BlockSpec((pair_len, head_step * head_dim), lambda i: (0, i)),
            pl.BlockSpec((head_step * pair_len, head_dim), lambda i: (i, 0)),
        ],
    )

    grad_near = near_ctx(cotangent[0])
    kv_here, normed_keep, kv_give = deal(core, kv_near, 2 * head_dim)
    kv_got = swap(kv_give, "ctx", 1)
    kv_pieces = [kv_here, kv_got]

    total_keys = ctx_count * pair_len
    attn_rows, probs, keys, values, branch_own, *branch_rest = kernel_call(
        functools.partial(attend_kernel, scale, 2),
        [
            shape_of((pair_len, query_cols), low),
            shape_of((heads * pair_len, total_keys), low),
            shape_of((total_keys, head_dim), low),
            shape_of((total_keys, head_dim), low),
            shape_of((share, width), full),
        ]
        + [shape_of((share, width), low)] * (wt_count - 1),
        [
            pl.BlockSpec((head_step * pair_len, 1), lambda i: (0, 0)),
            pl.BlockSpec((1, total_keys), lambda i: (0, 0)),
            pl.BlockSpec((head_step * pair_len, head_dim), lambda i: (i, 0)),
            in_any,
        ]
        + [pl.BlockSpec(one.shape, lambda i: (0, 0)) for one in kv_pieces],
        [row_positions, key_positions, queries, w_output, *kv_pieces],
        grid=(heads // head_step,),
        out_specs=[
            pl.BlockSpec((pair_len, query_cols), lambda i: (0, 0)),
            pl.BlockSpec((head_step * pair_len, total_keys), lambda i: (i, 0)),
            pl.BlockSpec((total_keys, head_dim), lambda i: (0, 0)),
            pl.BlockSpec((total_keys, head_dim), lambda i: (0, 0)),
        ]
        + [pl.BlockSpec((share, width), lambda i: (0, 0))] * wt_count,
        scratch_shapes=[
            pltpu.VMEM((heads // head_step, pair_len, head_step * head_dim), low),
            pltpu.VMEM(w_output.shape, low),
            pltpu.SemaphoreType.DMA,
        ],
    )
    branch_rest, branch_own, attn_rows = fence(branch_rest, branch_own, attn_rows)
    received = [swap(branch_rest[m - 1], "wt", m) for m in range(1, wt_count)]
    mid_rows, inverse_two, message = kernel_call(
        mid_kernel,
        [
            shape_of((share, width), full),
            shape_of((share, 1), full),
            shape_of((share, width + mask_cols), low),
        ],
        [in_vmem] * (3 + wt_count),
        [token_rows, moe_gain.reshape(1, -1), own_mask, branch_own, *received],
    )
    residual_rows = token_rows[0].astype(full)

    first = join([message] + [swap(message, "wt", m) for m in range(1, inner)])
    others = [swap(message, "wt", m) for m in range(inner, wt_count)]
    grads = [one.reshape(half, wt_count, share, width) for one in both(grad_near, message)]
    rows_first = both(near_ctx(first), others)
    chunks = pair_len // (inner * share)
    second = kernel_call(
        pack_kernel,
        shape_of((inner * share, width + mask_cols + chunks * query_cols), low),
        [in_vmem] * (1 + inner),
        [attn_rows, *others],
    )
    near_second = near_ctx(second)
    places = jnp.stack([my_expert, wt_index])
    sums_cols = width + extra_cols
    results, into = run_expert(
        0, parts, inner, True, rows_first, grads, router, w_gate_up, w_down, places, None, sums_cols,
    )
    results, into, near_second = fence(results, into, near_second)
    rows_second, attn_near = kernel_call(
        unpack_kernel,
        [shape_of((half * inner * share, width + mask_cols), low), shape_of((half * pair_len, query_cols), low)],
        [in_vmem] * half,
        near_second,
    )
    rows_second = [rows_second, swap(rows_second, "ctx", 1)]
    attn_got = swap(attn_near, "ctx", 1)

    def split_parts(near, far_sent):
        cols = near.shape[1]
        total = (near + far_sent).reshape(half, inner * share, cols)
        return [total[k] for k in range(half)]

    def plane_sum(blocks, received):
        total = blocks[0].astype(full)
        for one in received:
            total = total + one.astype(full)
        return total

    def wt_parts(sums):
        return [one[w * share : (w + 1) * share] for one in sums for w in range(inner)]

    back_blocks = [split_parts(results[0], swap(results[1], "ctx", 1))]
    rows_second, back_blocks, into = fence(rows_second, back_blocks, into)
    back_received = [plane_swap(back_blocks[0])]
    results, into = run_expert(
        1, parts, inner, False, rows_second, grads, router, w_gate_up, w_down, places, into, sums_cols,
    )

    results, into, back_received = fence(results, into, back_received)
    back_blocks.append(split_parts(results[0], swap(results[1], "ctx", 1)))
    back_blocks, moe_far, into = fence(back_blocks, results[3], into)
    rows_all, hidden, gate_up_grad, expert_grad = into
    back_received.append(plane_swap(back_blocks[1]))
    moe_far = swap(moe_far, "ctx", 1)
    w_gate_up_grad = dot(rows_all, gate_up_grad, 0, 0)
    w_down_grad = dot(hidden, expert_grad, 0, 0)
    back_received, moe_far, w_gate_up_grad, w_down_grad, attn_rows = fence(
        back_received, moe_far, w_gate_up_grad, w_down_grad, attn_rows
    )
    moe_blocks = [[one[:, sums_cols:] for one in back_blocks[0]], split_parts(results[2], moe_far)]
    moe_received = [[one[:, sums_cols:] for one in back_received[0]]]
    back_blocks[0] = [one[:, :sums_cols] for one in back_blocks[0]]
    back_received[0] = [one[:, :sums_cols] for one in back_received[0]]
    sums = wt_parts([plane_sum(b, r) for b, r in zip(back_blocks, back_received)])
    sums_low = [one.astype(low) for one in sums[1:]]
    sums_low, attn_rows, moe_blocks = fence(sums_low, attn_rows, moe_blocks)
    received = [swap(one, "wt", m + 1) for m, one in enumerate(sums_low)]
    received, moe_blocks = fence(received, moe_blocks)
    summed = plane_sum(sums, received)
    rows_sum = summed[:, :width]
    weight_grads = (
        summed[:, width : width + experts] + summed[:, width + experts : width + 2 * experts]
    )
    chosen = own_mask[:, :experts] > 0.5
    logits = jnp.where(chosen, dot(message[:, :width], router, 1, 1), -1e30)
    shifted = jnp.where(chosen, jnp.exp(logits - jnp.max(logits, axis=-1, keepdims=True)), 0.0)
    own_routes = shifted / jnp.sum(shifted, axis=-1, keepdims=True)
    logits_grad = own_routes * (
        weight_grads - jnp.sum(own_routes * weight_grads, axis=-1, keepdims=True)
    )
    logits_cols = jnp.concatenate(split_low(logits_grad), axis=1)
    router_term = dot(logits_cols, jnp.concatenate([router, router], axis=0), 1, 0)
    normed_two_grad = rows_sum + router_term
    moe_gain_part = jnp.sum(normed_two_grad * mid_rows * inverse_two, axis=0)
    grad_rows = lax.dynamic_slice_in_dim(cotangent[0], wt_index * share, share, 0).astype(full)
    mid_grad = grad_rows + norm_back(normed_two_grad, mid_rows, inverse_two, moe_gain)
    logits_cols = jnp.pad(logits_cols, ((0, 0), (0, extra_cols - 2 * experts)))
    mid_message = jnp.concatenate([mid_grad.astype(low), logits_cols], axis=1)

    mid_message, moe_blocks = fence(mid_message, moe_blocks)
    mid_pieces = gather_wt(mid_message)
    moe_received.append(plane_swap(moe_blocks[1]))
    mid_pieces, moe_received = fence(mid_pieces, moe_received)

    moe_sums = wt_parts([plane_sum(b, r) for b, r in zip(moe_blocks, moe_received)])
    moe_low = [one.astype(low) for one in moe_sums[1:]]
    moe_low, mid_pieces = fence(moe_low, mid_pieces)
    moe_received = [swap(one, "wt", m + 1) for m, one in enumerate(moe_low)]
    kv_part_near, kv_part_far, query_grad, query_gain_part, *logits_messages, _ = kernel_call(
        functools.partial(attend_back_kernel, scale, wt_count),
        [
            shape_of((total_keys // 2, 2 * head_dim), low),
            shape_of((total_keys // 2, 2 * head_dim), low),
            shape_of((pair_len, query_cols), low),
            shape_of((1, head_dim), full),
        ]
        + [shape_of((pair_len, extra_cols + 2 * block_cols), low)] * half
        + [shape_of((pair_len, width), low)],
        [
            in_smem,
            pl.BlockSpec((head_step * head_dim, width), lambda i: (i, 0)),
            pl.BlockSpec((head_step * pair_len, total_keys), lambda i: (i, 0)),
            pl.BlockSpec((total_keys, head_dim), lambda i: (0, 0)),
            pl.BlockSpec((total_keys, head_dim), lambda i: (0, 0)),
            pl.BlockSpec((head_step * pair_len, head_dim), lambda i: (i, 0)),
            pl.BlockSpec((pair_len, head_step * head_dim), lambda i: (0, i)),
            pl.BlockSpec((1, head_dim), lambda i: (0, 0)),
            pl.BlockSpec((pair_len, head_dim), lambda i: (0, 0)),
            pl.BlockSpec((pair_len, head_dim), lambda i: (0, 0)),
        ]
        + [pl.BlockSpec((share, width + extra_cols), lambda i: (0, 0))] * wt_count,
        [
            chip, w_output, probs, keys, values, queries, raw_query, query_gain.reshape(1, -1),
            cosine, sine, *mid_pieces,
        ],
        grid=(heads // head_step,),
        out_specs=[
            pl.BlockSpec((total_keys // 2, 2 * head_dim), lambda i: (0, 0)),
            pl.BlockSpec((total_keys // 2, 2 * head_dim), lambda i: (0, 0)),
            pl.BlockSpec((pair_len, head_step * head_dim), lambda i: (0, i)),
            pl.BlockSpec((1, head_dim), lambda i: (0, 0)),
        ]
        + [pl.BlockSpec((pair_len, extra_cols + 2 * block_cols), lambda i: (0, 0))] * half
        + [pl.BlockSpec((pair_len, width), lambda i: (0, 0))],
        scratch_shapes=[pltpu.VMEM((total_keys, 2 * head_dim), full)],
    )

    kv_part_near, kv_part_far, query_grad, moe_received, logits_messages = fence(
        kv_part_near, kv_part_far, query_grad, moe_received, logits_messages
    )
    kv_near = (kv_part_near + swap(kv_part_far, "ctx", 1)).reshape(half, pair_len, 2 * head_dim)
    kv_near = [kv_near[k] for k in range(half)]
    out_rows = (mid_rows + plane_sum(moe_sums, moe_received)).astype(low)
    kv_near, query_grad, out_rows = fence(kv_near, query_grad, out_rows)
    kv_received = plane_swap(kv_near)
    query_term = dot(query_grad, w_query, 1, 1)
    kv_received, query_term = fence(kv_received, query_term)
    gain_rows = 2 * width // 128 + 2 * head_dim // 128
    gain_blocks = -(-2 * gain_rows // share)
    one_own, *tail_results = kernel_call(
        functools.partial(tail_kernel, half),
        [shape_of((share, width), full)]
        + [shape_of((share, width + gain_blocks * 128), low)] * (wt_count - 1)
        + [
            shape_of((pair_len, query_cols + 2 * head_dim), low),
            shape_of((gain_blocks * share, 128), full),
        ],
        [in_vmem] * (12 + half),
        [
            moe_gain_part.reshape(1, -1), query_gain_part, query_term, query_grad, raw_key,
            key_gain.reshape(1, -1), cosine, sine, key_weight, value_weight, token_rows, inverse_one,
            kv_near[0], *kv_received,
        ],
        after=attn_got,
        through=logits_messages,
        scratch_shapes=[pltpu.VMEM((gain_rows, 128), full)],
    )
    one_rest, (projection_own, gains) = tail_results[: wt_count - 1], tail_results[wt_count - 1 : wt_count + 1]
    logits_messages = tail_results[wt_count + 1 :]
    received = [swap(one, "wt", m + 1) for m, one in enumerate(one_rest)]
    logits_near = [logits_messages[0]] + plane_swap(logits_messages)
    logits_own, mid_keep, logits_give = deal(core, logits_near, extra_cols)
    logits_got = swap(logits_give, "ctx", 1)
    message_rows = pair_len + 16
    last_rows, projection = kernel_call(
        last_kernel,
        [shape_of((share, 2 * width), low), shape_of((message_rows, query_cols + 2 * head_dim), low)],
        [in_smem] + [in_vmem] * (7 + wt_count),
        [
            index, token_rows, inverse_one, attn_gain.reshape(1, -1), mid_grad, out_rows, projection_own,
            gains, one_own, *received,
        ],
        after=logits_near,
        scratch_shapes=[
            pltpu.VMEM((wt_count, gain_blocks * share, 128), full),
            pltpu.VMEM((-(-2 * gain_rows // 16) * 16, 128), full),
        ],
    )

    last_pieces = gather_wt(last_rows)
    projection_near = near_ctx(projection)
    router_grad = kernel_call(
        router_kernel,
        shape_of((experts, width), full),
        [in_smem, in_any, in_vmem, in_vmem],
        [
            jnp.stack([ctx_index, wt_index]),
            rows_all.reshape(parts, ctx_count, inner, share, width),
            logits_own,
            logits_got,
        ],
        scratch_shapes=[
            pltpu.VMEM((ctx_count * wt_count, share, width), low),
            pltpu.VMEM((ctx_count * wt_count, share, extra_cols), low),
            pltpu.SemaphoreType.DMA((ctx_count * wt_count,)),
        ],
    )
    w_output_grad = kernel_call(
        output_kernel,
        shape_of((query_cols, block_cols), full),
        [in_vmem] * 4,
        [attn_near, attn_got, mid_keep, logits_got],
        after=last_rows,
    )
    w_query_grad, w_key_grad, w_value_grad, *gains = kernel_call(
        functools.partial(projection_kernel, half),
        [
            shape_of((block_cols, query_cols), full),
            shape_of((block_cols, head_dim), full),
            shape_of((block_cols, head_dim), full),
        ]
        + [shape_of((size // 128, 128), full) for size in (width, width, head_dim, head_dim)],
        [in_smem] + [in_vmem] * 4,
        [ctx_index.reshape(1), normed_keep, kv_got, *both(projection_near, [last_pieces[1:], w_output_grad, router_grad])],
        scratch_shapes=[
            pltpu.VMEM((total_keys, query_cols + 2 * head_dim), low),
            pltpu.VMEM((ctx_count, -(-2 * gain_rows // 16) * 16, 128), full),
        ],
    )
    attn_gain_grad, moe_gain_grad, query_gain_grad, key_gain_grad = [one.reshape(-1) for one in gains]
    block_out, tokens_grad = place_rows(
        index, last_pieces, width, 2, after=[router_grad, w_output_grad, w_query_grad]
    )
    w_router_grad = router_grad.T

    return (
        block_out.reshape(1, pair_len, width),
        tokens_grad.reshape(1, pair_len, width),
        attn_gain_grad,
        query_gain_grad,
        key_gain_grad,
        w_query_grad,
        w_key_grad,
        w_value_grad,
        w_output_grad,
        moe_gain_grad,
        w_router_grad,
        w_gate_up_grad[None],
        w_down_grad[None],
    )


def solution(mesh):
    in_specs = (
        P(None, "ctx", None),
        P(None, "ctx", None),
        P(("ctx", "wt"), None),
        P(),
        P(),
        P(),
        P(None, "wt"),
        P(None, "wt"),
        P(None, "wt"),
        P("wt", None),
        P(),
        P(),
        P(("ctx", "wt"), None, None),
        P(("ctx", "wt"), None, None),
    )
    out_specs = (
        P(None, "ctx", None),
        P(None, "ctx", None),
        P(),
        P(),
        P(),
        P("ctx", "wt"),
        P("ctx", "wt"),
        P("ctx", "wt"),
        P("wt", "ctx"),
        P(),
        P(),
        P(("ctx", "wt"), None, None),
        P(("ctx", "wt"), None, None),
    )
    return jax.shard_map(
        on_device, mesh=mesh, in_specs=in_specs, out_specs=out_specs, check_vma=False
    )
```

```python
import functools

import jax
import jax.numpy as jnp
from jax import lax
from jax.experimental import pallas as pl
from jax.experimental.pallas import tpu as pltpu
from jax.sharding import PartitionSpec as P

epsilon = 1e-06
rope_base = 1000000.0
low = jnp.bfloat16
full = jnp.float32
vmem_bytes = 60 * 1024 * 1024

in_vmem = pl.BlockSpec(memory_space=pltpu.VMEM)
in_smem = pl.BlockSpec(memory_space=pltpu.SMEM)
in_any = pl.BlockSpec(memory_space=pl.ANY)


def dot(a, b, a_dim=1, b_dim=0):
    return lax.dot_general(a, b, (((a_dim,), (b_dim,)), ((), ())), preferred_element_type=full)


def swap(array, axis, mask):
    count = lax.axis_size(axis)
    return lax.ppermute(array, axis, [(i, i ^ mask) for i in range(count)])


def fence(*values):
    return lax.optimization_barrier(values)


def shape_of(shape, dtype):
    return jax.ShapeDtypeStruct(tuple(shape), dtype)


def kernel_call(kernel, outs, ins, args, after=(), through=(), **more):
    single = not isinstance(outs, list)
    outs = [outs] if single else list(outs)
    after, through = jax.tree.leaves(after), jax.tree.leaves(through)
    count, lead = len(args), len(outs)
    every = count + len(after) + len(through)

    def body(*refs):
        kernel(*refs[:count], *refs[every : every + lead], *refs[every + lead + len(through) :])

    aliases = dict(more.pop("input_output_aliases", {}))
    if through:
        aliases.update({count + len(after) + i: lead + i for i in range(len(through))})
        more["out_specs"] = list(more.get("out_specs", [in_vmem] * lead)) + [in_any] * len(through)
    results = pl.pallas_call(
        body,
        out_shape=outs + [shape_of(one.shape, one.dtype) for one in through],
        in_specs=[*ins] + [in_any] * (len(after) + len(through)),
        input_output_aliases=aliases,
        compiler_params=pltpu.CompilerParams(vmem_limit_bytes=vmem_bytes),
        **more,
    )(*args, *after, *through)
    return results[0] if single else results


def rms_scale(value_matrix):
    return lax.rsqrt(jnp.mean(value_matrix * value_matrix, axis=-1, keepdims=True) + epsilon)


def norm_back(grad_out, value_matrix, inverse, gain_vec):
    scaled = grad_out * gain_vec
    inner_mean = jnp.mean(scaled * value_matrix, axis=-1, keepdims=True)
    return inverse * (scaled - value_matrix * inverse * inverse * inner_mean)


def mirrored(device, offset, groups, block_len):
    which_block = jnp.where(offset < block_len, device, 2 * groups - 1 - device)
    return which_block * block_len + offset % block_len


def rotate(value_matrix, cosine, sine):
    return value_matrix * cosine + pltpu.roll(value_matrix, value_matrix.shape[-1] // 2, 1) * sine


def front_kernel(
    index_ref, x_ref, gain_ref, kw_ref, vw_ref, kgain_ref, cos_ref, sin_ref,
    rows_ref, normed_ref, inv_ref, raw_ref, *message_refs
):
    blocks, share, _ = x_ref.shape
    for i in range(blocks):
        x_low = x_ref[index_ref[0] ^ i]
        rows_ref[i] = x_low
        x = x_low.astype(full)
        inverse = rms_scale(x)
        inv_ref[i * share : (i + 1) * share] = inverse
        normed_ref[i * share : (i + 1) * share] = (x * inverse * gain_ref[...]).astype(low)
    normed = normed_ref[...]
    raw = dot(normed, kw_ref[...])
    raw_ref[...] = raw
    head_dim = raw.shape[1]
    turned = rotate(raw * rms_scale(raw) * kgain_ref[...], cos_ref[...], sin_ref[...])
    keys = turned.astype(low)
    values = dot(normed, vw_ref[...]).astype(low)
    for k, ref in enumerate(message_refs):
        ref[:, :head_dim] = keys
        ref[:, head_dim : 2 * head_dim] = values
        cols = ref.shape[1] - 2 * head_dim
        start = pl.multiple_of((index_ref[1] ^ k) * cols, 128)
        ref[:, 2 * head_dim :] = normed_ref[:, pl.ds(start, cols)]


def query_kernel(normed_ref, w_ref, gain_ref, cos_ref, sin_ref, raw_ref, q_ref):
    rows, head_dim = cos_ref.shape
    raw = dot(normed_ref[...], w_ref[...])
    raw_ref[...] = raw
    for h in range(raw.shape[1] // head_dim):
        one = raw[:, h * head_dim : (h + 1) * head_dim]
        turned = rotate(one * rms_scale(one) * gain_ref[...], cos_ref[...], sin_ref[...])
        q_ref[h * rows : (h + 1) * rows] = turned.astype(low)


def attend_kernel(scale, pieces, qpos_ref, kpos_ref, q_ref, w_ref, *refs):
    kv_refs = refs[:pieces]
    rows_ref, probs_ref, keys_ref, values_ref, own_ref, *rest_refs, attn, weight, sem = refs[pieces:]
    step = pl.program_id(0)
    tokens, head_dim = rows_ref.shape[0], kv_refs[0].shape[1] // 2
    copy = pltpu.make_async_copy(w_ref, weight, sem)

    @pl.when(step == 0)
    def _():
        copy.start()
        at = 0
        for ref in kv_refs:
            keys_ref[at : at + ref.shape[0]] = ref[:, :head_dim]
            values_ref[at : at + ref.shape[0]] = ref[:, head_dim : 2 * head_dim]
            at += ref.shape[0]

    scores = dot(q_ref[...], keys_ref[...], 1, 1) * scale
    scores = jnp.where(kpos_ref[...] <= qpos_ref[...], scores, -1e30)
    weights = jnp.exp(scores - jnp.max(scores, axis=-1, keepdims=True))
    probs = (weights / jnp.sum(weights, axis=-1, keepdims=True)).astype(low)
    probs_ref[...] = probs
    out = dot(probs, values_ref[...]).astype(low)
    heads = out.shape[0] // tokens
    attn[step] = jnp.concatenate([out[h * tokens : (h + 1) * tokens] for h in range(heads)], axis=1)

    @pl.when(step == pl.num_programs(0) - 1)
    def _():
        copy.wait()
        for i in range(attn.shape[0]):
            rows_ref[:, i * heads * head_dim : (i + 1) * heads * head_dim] = attn[i]
        total = dot(rows_ref[...], weight[...])
        share = own_ref.shape[0]
        own_ref[...] = total[:share]
        for i, ref in enumerate(rest_refs):
            ref[...] = total[(i + 1) * share : (i + 2) * share].astype(low)


def mid_kernel(x_ref, gain_ref, mask_ref, own_ref, *refs):
    received, (mid_ref, inv_ref, message_ref) = refs[:-3], refs[-3:]
    mid = own_ref[...]
    for one in received:
        mid = mid + one[...].astype(full)
    mid = x_ref[0].astype(full) + mid
    inverse = rms_scale(mid)
    mid_ref[...] = mid
    inv_ref[...] = inverse
    width = mid.shape[1]
    message_ref[:, :width] = (mid * inverse * gain_ref[...]).astype(low)
    message_ref[:, width:] = mask_ref[...]


def expert_kernel(
    part, inner, merged, index_ref, row_near, row_far, grad_near, grad_far, router_ref, gu_any, down_any, *refs
):
    if merged:
        near_ref, far_ref, *refs = refs
        moe_near_ref, moe_far_ref = near_ref, far_ref
    else:
        near_ref, far_ref, moe_near_ref, moe_far_ref, *refs = refs
    all_any, x_ref, hidden_ref, dgu_ref, deo_ref, x_tile, g_tile, gu, down, sems = refs
    step = pl.program_id(0)
    rows, width = g_tile.shape
    tile = rows // 2
    slots, ffw = hidden_ref.shape
    experts = router_ref.shape[0]
    expert = index_ref[0]
    share = grad_near.shape[2]
    each = tile // (inner * share)
    half_rows = row_near.shape[0]
    x_in, x_out, g_in = [], [], []
    used = 0
    for i, ref in enumerate((row_near, row_far)):
        here = x_tile.at[pl.ds(i * tile, tile)]
        x_in.append(pltpu.make_async_copy(ref.at[pl.ds(step * tile, tile)], here, sems.at[used]))
        to = (2 * part + i) * half_rows + step * tile
        x_out.append(
            pltpu.make_async_copy(
                x_tile.at[pl.ds(i * tile, tile), pl.ds(0, width)], all_any.at[pl.ds(to, tile)], sems.at[used + 1]
            )
        )
        used += 2
    for i, ref in enumerate((grad_near, grad_far)):
        for c in range(each):
            for w in range(inner):
                at = i * tile + (c * inner + w) * share
                source = ref.at[step * each + c, index_ref[1] ^ (part * inner + w)]
                g_in.append(pltpu.make_async_copy(source, g_tile.at[pl.ds(at, share)], sems.at[used]))
                used += 1
    copy_gu = pltpu.make_async_copy(gu_any.at[0], gu, sems.at[used])
    copy_down = pltpu.make_async_copy(down_any.at[0], down, sems.at[used + 1])
    for one in x_in + g_in:
        one.start()

    @pl.when(step == 0)
    def _():
        copy_gu.start()
        copy_down.start()

    earlier = lax.broadcasted_iota(jnp.int32, (rows, rows), 0) < lax.broadcasted_iota(jnp.int32, (rows, rows), 1)
    for one in x_in:
        one.wait()
    for one in x_out:
        one.start()
    mask = x_tile[:, width:]
    mine = lax.broadcasted_iota(jnp.int32, (8, mask.shape[1]), 1) == expert
    routed = dot(jnp.where(mine, 1.0, 0.0).astype(low), mask, 1, 1)
    place = dot(routed.astype(low), jnp.where(earlier, 1.0, 0.0).astype(low))
    slot = lax.broadcasted_iota(jnp.int32, (slots, rows), 0).astype(full)
    draw = jnp.where(jnp.where(routed[:1] > 0.5, place[:1], -1.0) == slot, 1.0, 0.0).astype(low)
    drawn = dot(draw, x_tile[...]).astype(low)
    x = drawn[:, :width]
    x_ref[...] = x
    chosen = drawn[:, width:][:, :experts].astype(full) > 0.5
    logits = jnp.where(chosen, dot(x, router_ref[...], 1, 1), -1e30)
    shifted = jnp.exp(logits - jnp.max(logits, axis=-1, keepdims=True))
    shifted = jnp.where(chosen, shifted, 0.0)
    own_lane = lax.broadcasted_iota(jnp.int32, shifted.shape, 1) == expert
    total = jnp.sum(shifted, axis=-1, keepdims=True)
    own = jnp.sum(jnp.where(own_lane, shifted, 0.0), axis=-1, keepdims=True) / jnp.where(total > 0.0, total, 1.0)
    for one in g_in:
        one.wait()
    g = dot(draw, g_tile[...])
    deo = (g * own).astype(low)
    deo_ref[...] = deo

    @pl.when(step == 0)
    def _():
        copy_gu.wait()

    gate_up = dot(x, gu[...])

    @pl.when(step == 0)
    def _():
        copy_down.wait()

    gate, up = gate_up[:, :ffw], gate_up[:, ffw:]
    dhid = dot(deo, down[...], 1, 1)
    sig = jax.nn.sigmoid(gate)
    silu = gate * sig
    hidden = (silu * up).astype(low)
    hidden_ref[...] = hidden
    dgate = (dhid * up * (sig + silu * (1.0 - sig))).astype(low)
    dup = (dhid * silu).astype(low)
    dgu_ref[:, :ffw] = dgate
    dgu_ref[:, ffw:] = dup
    out = dot(hidden, down[...]).astype(low).astype(full)
    dlw = jnp.sum(out * g, axis=-1, keepdims=True)
    moe = (out * own).astype(low)
    back = (dot(dgate, gu[:, :ffw], 1, 1) + dot(dup, gu[:, ffw:], 1, 1)).astype(low)
    high = dlw.astype(low)
    rest = (dlw - high.astype(full)).astype(low).astype(full)
    cols = near_ref.shape[1] - (2 if merged else 1) * width
    lane = lax.broadcasted_iota(jnp.int32, (slots, cols), 1)
    extra = jnp.where(lane == expert, high.astype(full), 0.0)
    extra = jnp.where(lane == experts + expert, rest, extra).astype(low)
    for i, (ref, moe_ref) in enumerate(((near_ref, moe_near_ref), (far_ref, moe_far_ref))):
        lay = draw[:, i * tile : (i + 1) * tile]
        ref[:, :width] = dot(lay, back, 0, 0).astype(low)
        ref[:, width : width + cols] = dot(lay, extra, 0, 0).astype(low)
        moe_ref[:, moe_ref.shape[1] - width :] = dot(lay, moe, 0, 0).astype(low)
    for one in x_out:
        one.wait()


def run_expert(part, part_count, inner, merged, rows, grads, router, w_gate_up, w_down, index, into, cols, most):
    chips, wt_count, share, width = grads[0].shape
    half_rows = chips * inner * share
    tile = min(256, half_rows)
    steps = half_rows // tile
    slots = -(-2 * tile // share * most // 16) * 16
    ffw = w_down.shape[1]
    wide = rows[0].shape[-1]
    widths = [cols + width] if merged else [cols, width]
    outs, out_specs = [], []
    for one in widths:
        outs += [shape_of((half_rows, one), low)] * 2
        out_specs += [pl.BlockSpec((tile, one), lambda i: (i, 0))] * 2
    lead_outs = len(outs)
    outs.append(shape_of((2 * half_rows * part_count, width), low))
    out_specs.append(in_any)
    for one in (width, ffw, 2 * ffw, width):
        outs.append(shape_of((part_count * steps * slots, one), low))
        out_specs.append(pl.BlockSpec((slots, one), lambda i: (i + part * steps, 0)))
    ins = [in_smem] + [in_any] * 4 + [pl.BlockSpec(router.shape, lambda i: (0, 0)), in_any, in_any]
    args = [index, *rows, *grads, router, w_gate_up, w_down]
    lead = len(args)
    aliases = {}
    if into is not None:
        for i, array in enumerate(into):
            aliases[len(args)] = lead_outs + i
            ins.append(in_any)
            args.append(array)

    def body(*refs):
        expert_kernel(part, inner, merged, *refs[:lead], *refs[len(args) :])

    results = kernel_call(
        body,
        outs,
        ins,
        args,
        grid=(steps,),
        out_specs=out_specs,
        scratch_shapes=[
            pltpu.VMEM((2 * tile, wide), low),
            pltpu.VMEM((2 * tile, width), low),
            pltpu.VMEM(w_gate_up.shape[1:], low),
            pltpu.VMEM(w_down.shape[1:], low),
            pltpu.SemaphoreType.DMA((6 + 2 * tile // share,)),
        ],
        input_output_aliases=aliases,
    )
    return results[:lead_outs], results[lead_outs:]


def pack_kernel(attn_ref, *refs):
    out_ref, share = refs[-1], refs[0].shape[0]
    wide = refs[0].shape[1]
    for i, ref in enumerate(refs[:-1]):
        out_ref[i * share : (i + 1) * share, :wide] = ref[...]
    rows, cols = out_ref.shape[0], attn_ref.shape[1]
    for i in range(attn_ref.shape[0] // rows):
        out_ref[:, wide + i * cols : wide + (i + 1) * cols] = attn_ref[i * rows : (i + 1) * rows]


def unpack_kernel(*refs):
    in_refs, (rows_ref, attn_ref) = refs[:-2], refs[-2:]
    rows, wide, cols = in_refs[0].shape[0], rows_ref.shape[1], attn_ref.shape[1]
    at = 0
    for i, ref in enumerate(in_refs):
        rows_ref[i * rows : (i + 1) * rows] = ref[:, :wide]
        for j in range((ref.shape[1] - wide) // cols):
            attn_ref[at : at + rows] = ref[:, wide + j * cols : wide + (j + 1) * cols]
            at += rows


def last_kernel(index_ref, x_ref, inv_ref, gain_ref, grad_ref, out_rows_ref, proj_ref, gains_ref, own_ref, *refs):
    *received, last_ref, message_ref, parts, stack = refs
    total = own_ref[...]
    share, width = total.shape
    for one in received:
        total = total + one[:, :width].astype(full)
    last_ref[:, :width] = out_rows_ref[...]
    grad = grad_ref[...] + norm_back(total, x_ref[0].astype(full), inv_ref[:share], gain_ref[...])
    last_ref[:, width:] = grad.astype(low)
    parts[index_ref[0]] = gains_ref[...]
    for i, one in enumerate(received):
        for j in range(gains_ref.shape[0] // share):
            cols = slice(width + j * 128, width + (j + 1) * 128)
            parts[index_ref[0] ^ (i + 1), j * share : (j + 1) * share] = one[:, cols].astype(full)
    gains = parts[0]
    for i in range(1, parts.shape[0]):
        gains = gains + parts[i]
    count = 2 * width // 128 + 2 * 1
    stack_split(stack, gains[:count] + gains[count : 2 * count])
    rows = proj_ref.shape[0]
    more = message_ref.shape[0] - rows
    message_ref[:rows] = proj_ref[...]
    message_ref[rows:] = jnp.zeros((more, message_ref.shape[1]), low)
    for j in range(stack.shape[0] // more):
        message_ref[rows:, j * 128 : (j + 1) * 128] = stack[j * more : (j + 1) * more].astype(low)


def join_kernel(*refs):
    out_ref, at = refs[-1], 0
    for ref in refs[:-1]:
        out_ref[at : at + ref.shape[0]] = ref[...]
        at += ref.shape[0]


def join(pieces, after=()):
    rows = sum(one.shape[0] for one in pieces)
    return kernel_call(
        join_kernel,
        shape_of((rows, pieces[0].shape[1]), pieces[0].dtype),
        [in_vmem] * len(pieces),
        list(pieces),
        after,
    )


def cut_kernel(pieces, index_ref, rows_ref, from_ref, *out_refs):
    whole = rows_ref.shape[1]
    cols = out_refs[0].shape[1] - whole
    for k in range(pieces):
        out_refs[k][:, :whole] = rows_ref[...]
        start = pl.multiple_of((index_ref[0] ^ k) * cols, 128)
        out_refs[k][:, whole:] = from_ref[:, pl.ds(start, cols)]


def deal_kernel(pieces, whole, index_ref, *refs):
    in_refs, (own_ref, keep_ref, give_ref) = refs[:pieces], refs[pieces:]
    rows = in_refs[0].shape[0]
    cols = (in_refs[0].shape[1] - whole) // 2
    for i, ref in enumerate(in_refs):
        at = slice(i * rows, (i + 1) * rows)
        own_ref[at] = ref[:, :whole]
        give_ref[at, :whole] = ref[:, :whole]
        keep = pl.multiple_of(whole + index_ref[0] * cols, 128)
        give = pl.multiple_of(whole + (1 - index_ref[0]) * cols, 128)
        keep_ref[at] = ref[:, pl.ds(keep, cols)]
        give_ref[at, whole:] = ref[:, pl.ds(give, cols)]


def deal(core, pieces, whole, **more):
    rows, wide = pieces[0].shape
    cols = (wide - whole) // 2
    total = rows * len(pieces)
    return kernel_call(
        functools.partial(deal_kernel, len(pieces), whole),
        [shape_of((total, whole), low), shape_of((total, cols), low), shape_of((total, whole + cols), low)],
        [in_smem] + [in_vmem] * len(pieces),
        [core, *pieces],
        **more,
    )


def attend_back_kernel(scale, pieces, index_ref, w_ref, probs_ref, keys_ref, values_ref, q_ref, raw_ref,
                       gain_ref, cos_ref, sin_ref, *refs):
    da_refs = refs[:pieces]
    kv_near_ref, kv_far_ref, dq_ref, part_ref, *message_refs, da_ref, acc = refs[pieces:]
    step = pl.program_id(0)
    tokens, head_dim = cos_ref.shape
    share = da_refs[0].shape[0]
    width = da_ref.shape[1]
    logit_cols = da_refs[0].shape[1] - width

    @pl.when(step == 0)
    def _():
        for i, ref in enumerate(da_refs):
            da_ref[i * share : (i + 1) * share] = ref[:, :width]
            for k, one in enumerate(message_refs):
                one[i * share : (i + 1) * share, :logit_cols] = ref[:, width:]
        for k, one in enumerate(message_refs):
            cols = one.shape[1] - logit_cols
            start = pl.multiple_of((index_ref[0] ^ k) * cols, 128)
            one[:, logit_cols:] = da_ref[:, pl.ds(start, cols)]
        acc[...] = jnp.zeros_like(acc)
        part_ref[...] = jnp.zeros_like(part_ref)

    dattn = dot(da_ref[...], w_ref[...], 1, 1).astype(low)
    heads = dattn.shape[1] // head_dim
    out_grad = jnp.concatenate(
        [dattn[:, h * head_dim : (h + 1) * head_dim] for h in range(heads)], axis=0
    )
    probs_low = probs_ref[...]
    probs = probs_low.astype(full)
    prob_grad = dot(out_grad, values_ref[...], 1, 1)
    inner = jnp.sum(probs * prob_grad, axis=-1, keepdims=True)
    score_grad = (probs * (prob_grad - inner)).astype(low)
    query_grad = (dot(score_grad, keys_ref[...]) * scale).astype(low).astype(full)
    acc[:, :head_dim] += dot(score_grad, q_ref[...], 0, 0)
    acc[:, head_dim:] += dot(probs_low, out_grad, 0, 0)
    gain = gain_ref[...]
    part = part_ref[...]
    for h in range(heads):
        cols = slice(h * head_dim, (h + 1) * head_dim)
        turned = rotate(query_grad[h * tokens : (h + 1) * tokens], cos_ref[...], -sin_ref[...])
        raw = raw_ref[:, cols]
        inverse = rms_scale(raw)
        part = part + jnp.sum(turned * raw * inverse, axis=0, keepdims=True)
        dq_ref[:, cols] = norm_back(turned, raw, inverse, gain).astype(low)
    part_ref[...] = part

    @pl.when(step == pl.num_programs(0) - 1)
    def _():
        near = kv_near_ref.shape[0]
        for ref, at in ((kv_near_ref, 0), (kv_far_ref, near)):
            ref[:, :head_dim] = (acc[at : at + near, :head_dim] * scale).astype(low)
            ref[:, head_dim:] = acc[at : at + near, head_dim:].astype(low)


def stack_rows(stack, at, row):
    for k in range(row.shape[1] // 128):
        stack[at + k : at + k + 1] = row[:, k * 128 : (k + 1) * 128]


def stack_split(stack, values):
    count = values.shape[0]
    high = values.astype(low).astype(full)
    stack[...] = jnp.zeros_like(stack)
    stack[:count] = high
    stack[count : 2 * count] = (values - high).astype(low).astype(full)


def tail_kernel(pieces, moe_part_ref, query_part_ref, dn_ref, dq_ref, raw_ref, kgain_ref, cos_ref, sin_ref, kw_ref, vw_ref, x_ref,
                inv_ref, *refs):
    kv_refs = refs[:pieces]
    own_ref, *rest_refs, proj_ref, gains_ref, values = refs[pieces:]
    total = kv_refs[0][...].astype(full)
    for ref in kv_refs[1:]:
        total = total + ref[...].astype(full)
    head_dim = raw_ref.shape[1]
    query_cols = dq_ref.shape[1]
    turned = rotate(total[:, :head_dim].astype(low).astype(full), cos_ref[...], -sin_ref[...])
    dv = total[:, head_dim:].astype(low)
    raw = raw_ref[...]
    inverse = rms_scale(raw)
    key_part = jnp.sum(turned * raw * inverse, axis=0, keepdims=True)
    dk = norm_back(turned, raw, inverse, kgain_ref[...]).astype(low)
    proj_ref[:, :query_cols] = dq_ref[...]
    proj_ref[:, query_cols : query_cols + head_dim] = dk
    proj_ref[:, query_cols + head_dim :] = dv
    grad = dn_ref[...] + dot(dk, kw_ref[...], 1, 1) + dot(dv, vw_ref[...], 1, 1)
    blocks, share, _ = x_ref.shape
    width = grad.shape[1]
    part = jnp.zeros((1, width), full)
    for i in range(blocks):
        one = grad[i * share : (i + 1) * share]
        x = x_ref[i].astype(full)
        part = part + jnp.sum(one * x * inv_ref[i * share : (i + 1) * share], axis=0, keepdims=True)
        if i == 0:
            own_ref[...] = one
        else:
            rest_refs[i - 1][:, :width] = one.astype(low)
    stack_rows(values, 0, part)
    stack_rows(values, width // 128, moe_part_ref[...])
    stack_rows(values, 2 * width // 128, query_part_ref[...])
    stack_rows(values, (2 * width + head_dim) // 128, key_part)
    stack_split(gains_ref, values[...])
    for ref in rest_refs:
        for j in range(gains_ref.shape[0] // share):
            cols = slice(width + j * 128, width + (j + 1) * 128)
            ref[:, cols] = gains_ref[j * share : (j + 1) * share].astype(low)


def output_kernel(a_near, a_far, b_near, b_far, out_ref):
    rows, cols = out_ref.shape
    far = b_far.shape[1] - cols
    out_ref[...] = dot(a_near[...], b_near[...], 0, 0) + dot(a_far[:, :rows], b_far[:, far:], 0, 0)


def projection_kernel(pieces, index_ref, a_near, a_far, b_near, b_far, query_ref, key_ref, value_ref, *refs):
    *gain_refs, b, parts = refs
    far = a_far.shape[1] - a_near.shape[1]
    each = a_near.shape[0] // pieces
    rows = b_near.shape[0] // pieces
    more = rows - each
    for i, b_ref in enumerate((b_near, b_far)):
        for k in range(pieces):
            at = i * pieces + k
            b[at * each : (at + 1) * each] = b_ref[k * rows : k * rows + each]
            for j in range(parts.shape[1] // more):
                cols = slice(j * 128, (j + 1) * 128)
                parts[index_ref[0] ^ (2 * k + i), j * more : (j + 1) * more] = b_ref[
                    k * rows + each : (k + 1) * rows, cols
                ].astype(full)
    gains = parts[0]
    for i in range(1, 2 * pieces):
        gains = gains + parts[i]
    count = sum(ref.shape[0] for ref in gain_refs)
    gains = gains[:count] + gains[count : 2 * count]
    at = 0
    for ref in gain_refs:
        ref[...] = gains[at : at + ref.shape[0]]
        at += ref.shape[0]
    half = pieces * each
    total = dot(a_near[...], b[:half], 0, 0) + dot(a_far[:, far:], b[half:], 0, 0)
    cols, more = query_ref.shape[1], key_ref.shape[1]
    query_ref[...] = total[:, :cols]
    key_ref[...] = total[:, cols : cols + more]
    value_ref[...] = total[:, cols + more :]


def router_kernel(index_ref, rows_any, near_ref, far_ref, out_ref, rows, grads, sems):
    part_count, groups, inner, share, _ = rows_any.shape
    copies = []
    for p in range(part_count):
        for c in range(groups):
            half = groups // 2
            mask = 2 * (c % half) + c // half
            for w in range(inner):
                to = (index_ref[0] ^ mask) * (part_count * inner) + (index_ref[1] ^ (p * inner + w))
                copy = pltpu.make_async_copy(rows_any.at[p, c, w], rows.at[to], sems.at[len(copies)])
                copy.start()
                copies.append(copy)
                grad_ref = near_ref if c < half else far_ref
                at = ((c % half) * (part_count * inner) + p * inner + w) * share
                grads[to] = grad_ref[at : at + share, : grads.shape[2]]
    for copy in copies:
        copy.wait()
    count = rows.shape[0] * share
    total = dot(grads[...].reshape(count, grads.shape[2]), rows[...].reshape(count, rows.shape[2]), 0, 0)
    experts = out_ref.shape[0]
    out_ref[...] = total[:experts] + total[experts : 2 * experts]


def place_kernel(pieces, index_ref, *refs):
    piece_refs, out_refs = refs[:pieces], refs[pieces:]
    width = out_refs[0].shape[2]
    for i, ref in enumerate(piece_refs):
        for j, out_ref in enumerate(out_refs):
            out_ref[index_ref[0] ^ i] = ref[:, j * width : (j + 1) * width]


def place_rows(index, pieces, width, count, **more):
    share = pieces[0].shape[0]
    return kernel_call(
        functools.partial(place_kernel, len(pieces)),
        [shape_of((len(pieces), share, width), pieces[0].dtype)] * count,
        [in_smem] + [in_vmem] * len(pieces),
        [index.reshape(1), *pieces],
        **more,
    )


def gather_wt(array):
    return [array] + [swap(array, "wt", m) for m in range(1, lax.axis_size("wt"))]


def near_ctx(array):
    return [array] + [swap(array, "ctx", 2 * k) for k in range(1, lax.axis_size("ctx") // 2)]


def far_ctx(arrays):
    return [swap(one, "ctx", 1) for one in arrays]


def split_low(array):
    high = array.astype(low)
    return high, (array - high.astype(full)).astype(low)


def on_device(
    tokens,
    cotangent,
    routes,
    attn_gain,
    query_gain,
    key_gain,
    w_query,
    key_weight,
    value_weight,
    w_output,
    moe_gain,
    w_router,
    w_gate_up,
    w_down,
):
    _, pair_len, width = tokens.shape
    head_dim = query_gain.shape[0]
    query_cols = w_query.shape[1]
    heads = query_cols // head_dim
    share, top_count = routes.shape
    experts = w_router.shape[1]
    ctx_count = lax.axis_size("ctx")
    wt_count = lax.axis_size("wt")
    half = ctx_count // 2
    ctx_index = lax.axis_index("ctx")
    wt_index = lax.axis_index("wt")
    my_expert = ctx_index * wt_count + wt_index
    scale = head_dim ** (-0.5)
    head_step = 2
    parts = 2
    inner = wt_count // parts
    mask_cols = -(-experts // 128) * 128
    extra_cols = -(-2 * experts // 128) * 128
    index = wt_index.reshape(1)
    chip = (ctx_index >> 1).reshape(1)
    core = (ctx_index & 1).reshape(1)
    router = w_router.T

    def plane_swap(blocks):
        return [swap(blocks[k], "ctx", 2 * k) for k in range(1, half)]

    def joined(pieces):
        return jnp.concatenate(pieces, axis=0) if len(pieces) > 1 else pieces[0]

    def both(pieces, after=()):
        near = join(pieces, after)
        return [near, swap(near, "ctx", 1)]


    place = jnp.arange(pair_len, dtype=jnp.int32)
    offsets = ((place // share) ^ wt_index) * share + place % share
    near_masks = 2 * jnp.arange(half, dtype=jnp.int32)
    masks = jnp.concatenate([near_masks, near_masks + 1])
    own_positions = mirrored(ctx_index, offsets, ctx_count, pair_len // 2)
    key_positions = mirrored(
        (ctx_index ^ masks)[:, None], offsets[None, :], ctx_count, pair_len // 2
    ).reshape(1, -1)
    row_positions = jnp.tile(own_positions, head_step).reshape(-1, 1)
    frequency = rope_base ** (-2.0 * jnp.arange(head_dim // 2, dtype=full) / head_dim)
    angles = own_positions.astype(full)[:, None] * frequency[None, :]
    cosine, sine = jnp.cos(angles), jnp.sin(angles)
    cosine = jnp.concatenate([cosine, cosine], axis=1)
    sine = jnp.concatenate([-sine, sine], axis=1)

    expert_ids = jnp.arange(mask_cols, dtype=jnp.int32)
    own_mask = jnp.any(routes[:, :, None] == expert_ids, axis=1).astype(low)
    block_cols = width // ctx_count
    token_rows, normed_one, inverse_one, raw_key, *kv_messages = kernel_call(
        front_kernel,
        [
            shape_of((wt_count, share, width), low),
            shape_of((pair_len, width), low),
            shape_of((pair_len, 1), full),
            shape_of((pair_len, head_dim), full),
        ]
        + [shape_of((pair_len, 2 * head_dim + 2 * block_cols), low)] * half,
        [in_smem] + [in_vmem] * 7,
        [
            jnp.stack([wt_index, ctx_index >> 1]),
            tokens.reshape(wt_count, share, width),
            attn_gain.reshape(1, -1),
            key_weight,
            value_weight,
            key_gain.reshape(1, -1),
            cosine,
            sine,
        ],
    )

    kv_near = [kv_messages[0]] + plane_swap(kv_messages)
    raw_query, queries = kernel_call(
        query_kernel,
        [shape_of((pair_len, query_cols), full), shape_of((heads * pair_len, head_dim), low)],
        [
            pl.BlockSpec((pair_len, width), lambda i: (0, 0)),
            pl.BlockSpec((width, head_step * head_dim), lambda i: (0, i)),
            pl.BlockSpec((1, head_dim), lambda i: (0, 0)),
            pl.BlockSpec((pair_len, head_dim), lambda i: (0, 0)),
            pl.BlockSpec((pair_len, head_dim), lambda i: (0, 0)),
        ],
        [normed_one, w_query, query_gain.reshape(1, -1), cosine, sine],
        grid=(heads // head_step,),
        out_specs=[
            pl.BlockSpec((pair_len, head_step * head_dim), lambda i: (0, i)),
            pl.BlockSpec((head_step * pair_len, head_dim), lambda i: (i, 0)),
        ],
    )

    grad_near = near_ctx(cotangent[0])
    kv_here, normed_keep, kv_give = deal(core, kv_near, 2 * head_dim)
    kv_got = swap(kv_give, "ctx", 1)
    kv_pieces = [kv_here, kv_got]

    total_keys = ctx_count * pair_len
    attn_rows, probs, keys, values, branch_own, *branch_rest = kernel_call(
        functools.partial(attend_kernel, scale, 2),
        [
            shape_of((pair_len, query_cols), low),
            shape_of((heads * pair_len, total_keys), low),
            shape_of((total_keys, head_dim), low),
            shape_of((total_keys, head_dim), low),
            shape_of((share, width), full),
        ]
        + [shape_of((share, width), low)] * (wt_count - 1),
        [
            pl.BlockSpec((head_step * pair_len, 1), lambda i: (0, 0)),
            pl.BlockSpec((1, total_keys), lambda i: (0, 0)),
            pl.BlockSpec((head_step * pair_len, head_dim), lambda i: (i, 0)),
            in_any,
        ]
        + [pl.BlockSpec(one.shape, lambda i: (0, 0)) for one in kv_pieces],
        [row_positions, key_positions, queries, w_output, *kv_pieces],
        grid=(heads // head_step,),
        out_specs=[
            pl.BlockSpec((pair_len, query_cols), lambda i: (0, 0)),
            pl.BlockSpec((head_step * pair_len, total_keys), lambda i: (i, 0)),
            pl.BlockSpec((total_keys, head_dim), lambda i: (0, 0)),
            pl.BlockSpec((total_keys, head_dim), lambda i: (0, 0)),
        ]
        + [pl.BlockSpec((share, width), lambda i: (0, 0))] * wt_count,
        scratch_shapes=[
            pltpu.VMEM((heads // head_step, pair_len, head_step * head_dim), low),
            pltpu.VMEM(w_output.shape, low),
            pltpu.SemaphoreType.DMA,
        ],
    )
    branch_rest, branch_own, attn_rows = fence(branch_rest, branch_own, attn_rows)
    received = [swap(branch_rest[m - 1], "wt", m) for m in range(1, wt_count)]
    mid_rows, inverse_two, message = kernel_call(
        mid_kernel,
        [
            shape_of((share, width), full),
            shape_of((share, 1), full),
            shape_of((share, width + mask_cols), low),
        ],
        [in_vmem] * (3 + wt_count),
        [token_rows, moe_gain.reshape(1, -1), own_mask, branch_own, *received],
    )
    residual_rows = token_rows[0].astype(full)

    first = join([message] + [swap(message, "wt", m) for m in range(1, inner)])
    others = [swap(message, "wt", m) for m in range(inner, wt_count)]
    grads = [one.reshape(half, wt_count, share, width) for one in both(grad_near, message)]
    rows_first = both(near_ctx(first), others)
    chunks = pair_len // (inner * share)
    second = kernel_call(
        pack_kernel,
        shape_of((inner * share, width + mask_cols + chunks * query_cols), low),
        [in_vmem] * (1 + inner),
        [attn_rows, *others],
    )
    near_second = near_ctx(second)
    places = jnp.stack([my_expert, wt_index])
    sums_cols = width + extra_cols
    most = max(2, share * top_count * 5 // (4 * experts) + 1)
    results, into = run_expert(
        0, parts, inner, True, rows_first, grads, router, w_gate_up, w_down, places, None, sums_cols,
        most,
    )
    results, into, near_second = fence(results, into, near_second)
    rows_second, attn_near = kernel_call(
        unpack_kernel,
        [shape_of((half * inner * share, width + mask_cols), low), shape_of((half * pair_len, query_cols), low)],
        [in_vmem] * half,
        near_second,
    )
    rows_second = [rows_second, swap(rows_second, "ctx", 1)]
    attn_got = swap(attn_near, "ctx", 1)

    def split_parts(near, far_sent):
        cols = near.shape[1]
        total = (near + far_sent).reshape(half, inner * share, cols)
        return [total[k] for k in range(half)]

    def plane_sum(blocks, received):
        total = blocks[0].astype(full)
        for one in received:
            total = total + one.astype(full)
        return total

    def wt_parts(sums):
        return [one[w * share : (w + 1) * share] for one in sums for w in range(inner)]

    back_blocks = [split_parts(results[0], swap(results[1], "ctx", 1))]
    rows_second, back_blocks, into = fence(rows_second, back_blocks, into)
    back_received = [plane_swap(back_blocks[0])]
    results, into = run_expert(
        1, parts, inner, False, rows_second, grads, router, w_gate_up, w_down, places, into, sums_cols,
        most,
    )

    results, into, back_received = fence(results, into, back_received)
    back_blocks.append(split_parts(results[0], swap(results[1], "ctx", 1)))
    back_blocks, moe_far, into = fence(back_blocks, results[3], into)
    rows_all, rows_drawn, hidden, gate_up_grad, expert_grad = into
    back_received.append(plane_swap(back_blocks[1]))
    moe_far = swap(moe_far, "ctx", 1)
    w_gate_up_grad = dot(rows_drawn, gate_up_grad, 0, 0)
    w_down_grad = dot(hidden, expert_grad, 0, 0)
    back_received, moe_far, w_gate_up_grad, w_down_grad, attn_rows = fence(
        back_received, moe_far, w_gate_up_grad, w_down_grad, attn_rows
    )
    moe_blocks = [[one[:, sums_cols:] for one in back_blocks[0]], split_parts(results[2], moe_far)]
    moe_received = [[one[:, sums_cols:] for one in back_received[0]]]
    back_blocks[0] = [one[:, :sums_cols] for one in back_blocks[0]]
    back_received[0] = [one[:, :sums_cols] for one in back_received[0]]
    sums = wt_parts([plane_sum(b, r) for b, r in zip(back_blocks, back_received)])
    sums_low = [one.astype(low) for one in sums[1:]]
    sums_low, attn_rows, moe_blocks = fence(sums_low, attn_rows, moe_blocks)
    received = [swap(one, "wt", m + 1) for m, one in enumerate(sums_low)]
    received, moe_blocks = fence(received, moe_blocks)
    summed = plane_sum(sums, received)
    rows_sum = summed[:, :width]
    weight_grads = (
        summed[:, width : width + experts] + summed[:, width + experts : width + 2 * experts]
    )
    chosen = own_mask[:, :experts] > 0.5
    logits = jnp.where(chosen, dot(message[:, :width], router, 1, 1), -1e30)
    shifted = jnp.where(chosen, jnp.exp(logits - jnp.max(logits, axis=-1, keepdims=True)), 0.0)
    own_routes = shifted / jnp.sum(shifted, axis=-1, keepdims=True)
    logits_grad = own_routes * (
        weight_grads - jnp.sum(own_routes * weight_grads, axis=-1, keepdims=True)
    )
    logits_cols = jnp.concatenate(split_low(logits_grad), axis=1)
    router_term = dot(logits_cols, jnp.concatenate([router, router], axis=0), 1, 0)
    normed_two_grad = rows_sum + router_term
    moe_gain_part = jnp.sum(normed_two_grad * mid_rows * inverse_two, axis=0)
    grad_rows = lax.dynamic_slice_in_dim(cotangent[0], wt_index * share, share, 0).astype(full)
    mid_grad = grad_rows + norm_back(normed_two_grad, mid_rows, inverse_two, moe_gain)
    logits_cols = jnp.pad(logits_cols, ((0, 0), (0, extra_cols - 2 * experts)))
    mid_message = jnp.concatenate([mid_grad.astype(low), logits_cols], axis=1)

    mid_message, moe_blocks = fence(mid_message, moe_blocks)
    mid_pieces = gather_wt(mid_message)
    moe_received.append(plane_swap(moe_blocks[1]))
    mid_pieces, moe_received = fence(mid_pieces, moe_received)

    moe_sums = wt_parts([plane_sum(b, r) for b, r in zip(moe_blocks, moe_received)])
    moe_low = [one.astype(low) for one in moe_sums[1:]]
    moe_low, mid_pieces = fence(moe_low, mid_pieces)
    moe_received = [swap(one, "wt", m + 1) for m, one in enumerate(moe_low)]
    kv_part_near, kv_part_far, query_grad, query_gain_part, *logits_messages, _ = kernel_call(
        functools.partial(attend_back_kernel, scale, wt_count),
        [
            shape_of((total_keys // 2, 2 * head_dim), low),
            shape_of((total_keys // 2, 2 * head_dim), low),
            shape_of((pair_len, query_cols), low),
            shape_of((1, head_dim), full),
        ]
        + [shape_of((pair_len, extra_cols + 2 * block_cols), low)] * half
        + [shape_of((pair_len, width), low)],
        [
            in_smem,
            pl.BlockSpec((head_step * head_dim, width), lambda i: (i, 0)),
            pl.BlockSpec((head_step * pair_len, total_keys), lambda i: (i, 0)),
            pl.BlockSpec((total_keys, head_dim), lambda i: (0, 0)),
            pl.BlockSpec((total_keys, head_dim), lambda i: (0, 0)),
            pl.BlockSpec((head_step * pair_len, head_dim), lambda i: (i, 0)),
            pl.BlockSpec((pair_len, head_step * head_dim), lambda i: (0, i)),
            pl.BlockSpec((1, head_dim), lambda i: (0, 0)),
            pl.BlockSpec((pair_len, head_dim), lambda i: (0, 0)),
            pl.BlockSpec((pair_len, head_dim), lambda i: (0, 0)),
        ]
        + [pl.BlockSpec((share, width + extra_cols), lambda i: (0, 0))] * wt_count,
        [
            chip, w_output, probs, keys, values, queries, raw_query, query_gain.reshape(1, -1),
            cosine, sine, *mid_pieces,
        ],
        grid=(heads // head_step,),
        out_specs=[
            pl.BlockSpec((total_keys // 2, 2 * head_dim), lambda i: (0, 0)),
            pl.BlockSpec((total_keys // 2, 2 * head_dim), lambda i: (0, 0)),
            pl.BlockSpec((pair_len, head_step * head_dim), lambda i: (0, i)),
            pl.BlockSpec((1, head_dim), lambda i: (0, 0)),
        ]
        + [pl.BlockSpec((pair_len, extra_cols + 2 * block_cols), lambda i: (0, 0))] * half
        + [pl.BlockSpec((pair_len, width), lambda i: (0, 0))],
        scratch_shapes=[pltpu.VMEM((total_keys, 2 * head_dim), full)],
    )

    kv_part_near, kv_part_far, query_grad, moe_received, logits_messages = fence(
        kv_part_near, kv_part_far, query_grad, moe_received, logits_messages
    )
    kv_near = (kv_part_near + swap(kv_part_far, "ctx", 1)).reshape(half, pair_len, 2 * head_dim)
    kv_near = [kv_near[k] for k in range(half)]
    out_rows = (mid_rows + plane_sum(moe_sums, moe_received)).astype(low)
    kv_near, query_grad, out_rows = fence(kv_near, query_grad, out_rows)
    kv_received = plane_swap(kv_near)
    query_term = dot(query_grad, w_query, 1, 1)
    kv_received, query_term = fence(kv_received, query_term)
    gain_rows = 2 * width // 128 + 2 * head_dim // 128
    gain_blocks = -(-2 * gain_rows // share)
    one_own, *tail_results = kernel_call(
        functools.partial(tail_kernel, half),
        [shape_of((share, width), full)]
        + [shape_of((share, width + gain_blocks * 128), low)] * (wt_count - 1)
        + [
            shape_of((pair_len, query_cols + 2 * head_dim), low),
            shape_of((gain_blocks * share, 128), full),
        ],
        [in_vmem] * (12 + half),
        [
            moe_gain_part.reshape(1, -1), query_gain_part, query_term, query_grad, raw_key,
            key_gain.reshape(1, -1), cosine, sine, key_weight, value_weight, token_rows, inverse_one,
            kv_near[0], *kv_received,
        ],
        after=attn_got,
        through=logits_messages,
        scratch_shapes=[pltpu.VMEM((gain_rows, 128), full)],
    )
    one_rest, (projection_own, gains) = tail_results[: wt_count - 1], tail_results[wt_count - 1 : wt_count + 1]
    logits_messages = tail_results[wt_count + 1 :]
    received = [swap(one, "wt", m + 1) for m, one in enumerate(one_rest)]
    logits_near = [logits_messages[0]] + plane_swap(logits_messages)
    logits_own, mid_keep, logits_give = deal(core, logits_near, extra_cols)
    logits_got = swap(logits_give, "ctx", 1)
    message_rows = pair_len + 16
    last_rows, projection = kernel_call(
        last_kernel,
        [shape_of((share, 2 * width), low), shape_of((message_rows, query_cols + 2 * head_dim), low)],
        [in_smem] + [in_vmem] * (7 + wt_count),
        [
            index, token_rows, inverse_one, attn_gain.reshape(1, -1), mid_grad, out_rows, projection_own,
            gains, one_own, *received,
        ],
        after=logits_near,
        scratch_shapes=[
            pltpu.VMEM((wt_count, gain_blocks * share, 128), full),
            pltpu.VMEM((-(-2 * gain_rows // 16) * 16, 128), full),
        ],
    )

    last_pieces = gather_wt(last_rows)
    projection_near = near_ctx(projection)
    router_grad = kernel_call(
        router_kernel,
        shape_of((experts, width), full),
        [in_smem, in_any, in_vmem, in_vmem],
        [
            jnp.stack([ctx_index, wt_index]),
            rows_all.reshape(parts, ctx_count, inner, share, width),
            logits_own,
            logits_got,
        ],
        scratch_shapes=[
            pltpu.VMEM((ctx_count * wt_count, share, width), low),
            pltpu.VMEM((ctx_count * wt_count, share, extra_cols), low),
            pltpu.SemaphoreType.DMA((ctx_count * wt_count,)),
        ],
    )
    w_output_grad = kernel_call(
        output_kernel,
        shape_of((query_cols, block_cols), full),
        [in_vmem] * 4,
        [attn_near, attn_got, mid_keep, logits_got],
        after=last_rows,
    )
    w_query_grad, w_key_grad, w_value_grad, *gains = kernel_call(
        functools.partial(projection_kernel, half),
        [
            shape_of((block_cols, query_cols), full),
            shape_of((block_cols, head_dim), full),
            shape_of((block_cols, head_dim), full),
        ]
        + [shape_of((size // 128, 128), full) for size in (width, width, head_dim, head_dim)],
        [in_smem] + [in_vmem] * 4,
        [ctx_index.reshape(1), normed_keep, kv_got, *both(projection_near, [last_pieces[1:], w_output_grad, router_grad])],
        scratch_shapes=[
            pltpu.VMEM((total_keys, query_cols + 2 * head_dim), low),
            pltpu.VMEM((ctx_count, -(-2 * gain_rows // 16) * 16, 128), full),
        ],
    )
    attn_gain_grad, moe_gain_grad, query_gain_grad, key_gain_grad = [one.reshape(-1) for one in gains]
    block_out, tokens_grad = place_rows(
        index, last_pieces, width, 2, after=[router_grad, w_output_grad, w_query_grad]
    )
    w_router_grad = router_grad.T

    return (
        block_out.reshape(1, pair_len, width),
        tokens_grad.reshape(1, pair_len, width),
        attn_gain_grad,
        query_gain_grad,
        key_gain_grad,
        w_query_grad,
        w_key_grad,
        w_value_grad,
        w_output_grad,
        moe_gain_grad,
        w_router_grad,
        w_gate_up_grad[None],
        w_down_grad[None],
    )


def solution(mesh):
    in_specs = (
        P(None, "ctx", None),
        P(None, "ctx", None),
        P(("ctx", "wt"), None),
        P(),
        P(),
        P(),
        P(None, "wt"),
        P(None, "wt"),
        P(None, "wt"),
        P("wt", None),
        P(),
        P(),
        P(("ctx", "wt"), None, None),
        P(("ctx", "wt"), None, None),
    )
    out_specs = (
        P(None, "ctx", None),
        P(None, "ctx", None),
        P(),
        P(),
        P(),
        P("ctx", "wt"),
        P("ctx", "wt"),
        P("ctx", "wt"),
        P("wt", "ctx"),
        P(),
        P(),
        P(("ctx", "wt"), None, None),
        P(("ctx", "wt"), None, None),
    )
    return jax.shard_map(
        on_device, mesh=mesh, in_specs=in_specs, out_specs=out_specs, check_vma=False
    )
```

```python
import functools

import jax
import jax.numpy as jnp
from jax import lax
from jax.experimental import pallas as pl
from jax.experimental.pallas import tpu as pltpu
from jax.sharding import PartitionSpec as P

epsilon = 1e-06
rope_base = 1000000.0
low = jnp.bfloat16
full = jnp.float32
vmem_bytes = 60 * 1024 * 1024

in_vmem = pl.BlockSpec(memory_space=pltpu.VMEM)
in_smem = pl.BlockSpec(memory_space=pltpu.SMEM)
in_any = pl.BlockSpec(memory_space=pl.ANY)


def dot(a, b, a_dim=1, b_dim=0):
    return lax.dot_general(a, b, (((a_dim,), (b_dim,)), ((), ())), preferred_element_type=full)


def swap(array, axis, mask):
    count = lax.axis_size(axis)
    return lax.ppermute(array, axis, [(i, i ^ mask) for i in range(count)])


def fence(*values):
    return lax.optimization_barrier(values)


def shape_of(shape, dtype):
    return jax.ShapeDtypeStruct(tuple(shape), dtype)


def kernel_call(kernel, outs, ins, args, after=(), through=(), **more):
    single = not isinstance(outs, list)
    outs = [outs] if single else list(outs)
    after, through = jax.tree.leaves(after), jax.tree.leaves(through)
    count, lead = len(args), len(outs)
    every = count + len(after) + len(through)

    def body(*refs):
        kernel(*refs[:count], *refs[every : every + lead], *refs[every + lead + len(through) :])

    aliases = dict(more.pop("input_output_aliases", {}))
    if through:
        aliases.update({count + len(after) + i: lead + i for i in range(len(through))})
        more["out_specs"] = list(more.get("out_specs", [in_vmem] * lead)) + [in_any] * len(through)
    results = pl.pallas_call(
        body,
        out_shape=outs + [shape_of(one.shape, one.dtype) for one in through],
        in_specs=[*ins] + [in_any] * (len(after) + len(through)),
        input_output_aliases=aliases,
        compiler_params=pltpu.CompilerParams(vmem_limit_bytes=vmem_bytes),
        **more,
    )(*args, *after, *through)
    return results[0] if single else results


def rms_scale(value_matrix):
    return lax.rsqrt(jnp.mean(value_matrix * value_matrix, axis=-1, keepdims=True) + epsilon)


def norm_back(grad_out, value_matrix, inverse, gain_vec):
    scaled = grad_out * gain_vec
    inner_mean = jnp.mean(scaled * value_matrix, axis=-1, keepdims=True)
    return inverse * (scaled - value_matrix * inverse * inverse * inner_mean)


def mirrored(device, offset, groups, block_len):
    which_block = jnp.where(offset < block_len, device, 2 * groups - 1 - device)
    return which_block * block_len + offset % block_len


def rotate(value_matrix, cosine, sine):
    return value_matrix * cosine + pltpu.roll(value_matrix, value_matrix.shape[-1] // 2, 1) * sine


def front_kernel(
    index_ref, x_ref, gain_ref, kw_ref, vw_ref, kgain_ref, cos_ref, sin_ref,
    rows_ref, normed_ref, inv_ref, raw_ref, *message_refs
):
    blocks, share, _ = x_ref.shape
    for i in range(blocks):
        x_low = x_ref[index_ref[0] ^ i]
        rows_ref[i] = x_low
        x = x_low.astype(full)
        inverse = rms_scale(x)
        inv_ref[i * share : (i + 1) * share] = inverse
        normed_ref[i * share : (i + 1) * share] = (x * inverse * gain_ref[...]).astype(low)
    normed = normed_ref[...]
    raw = dot(normed, kw_ref[...])
    raw_ref[...] = raw
    head_dim = raw.shape[1]
    turned = rotate(raw * rms_scale(raw) * kgain_ref[...], cos_ref[...], sin_ref[...])
    keys = turned.astype(low)
    values = dot(normed, vw_ref[...]).astype(low)
    for k, ref in enumerate(message_refs):
        ref[:, :head_dim] = keys
        ref[:, head_dim : 2 * head_dim] = values
        cols = ref.shape[1] - 2 * head_dim
        start = pl.multiple_of((index_ref[1] ^ k) * cols, 128)
        ref[:, 2 * head_dim :] = normed_ref[:, pl.ds(start, cols)]


def query_kernel(normed_ref, w_ref, gain_ref, cos_ref, sin_ref, raw_ref, q_ref):
    rows, head_dim = cos_ref.shape
    raw = dot(normed_ref[...], w_ref[...])
    raw_ref[...] = raw
    for h in range(raw.shape[1] // head_dim):
        one = raw[:, h * head_dim : (h + 1) * head_dim]
        turned = rotate(one * rms_scale(one) * gain_ref[...], cos_ref[...], sin_ref[...])
        q_ref[h * rows : (h + 1) * rows] = turned.astype(low)


def attend_kernel(scale, pieces, qpos_ref, kpos_ref, q_ref, w_ref, *refs):
    kv_refs = refs[:pieces]
    rows_ref, probs_ref, keys_ref, values_ref, own_ref, *rest_refs, attn, weight, sem = refs[pieces:]
    step = pl.program_id(0)
    tokens, head_dim = rows_ref.shape[0], kv_refs[0].shape[1] // 2
    copy = pltpu.make_async_copy(w_ref, weight, sem)

    @pl.when(step == 0)
    def _():
        copy.start()
        at = 0
        for ref in kv_refs:
            keys_ref[at : at + ref.shape[0]] = ref[:, :head_dim]
            values_ref[at : at + ref.shape[0]] = ref[:, head_dim : 2 * head_dim]
            at += ref.shape[0]

    scores = dot(q_ref[...], keys_ref[...], 1, 1) * scale
    scores = jnp.where(kpos_ref[...] <= qpos_ref[...], scores, -1e30)
    weights = jnp.exp(scores - jnp.max(scores, axis=-1, keepdims=True))
    probs = (weights / jnp.sum(weights, axis=-1, keepdims=True)).astype(low)
    probs_ref[...] = probs
    out = dot(probs, values_ref[...]).astype(low)
    heads = out.shape[0] // tokens
    attn[step] = jnp.concatenate([out[h * tokens : (h + 1) * tokens] for h in range(heads)], axis=1)

    @pl.when(step == pl.num_programs(0) - 1)
    def _():
        copy.wait()
        for i in range(attn.shape[0]):
            rows_ref[:, i * heads * head_dim : (i + 1) * heads * head_dim] = attn[i]
        total = dot(rows_ref[...], weight[...])
        share = own_ref.shape[0]
        own_ref[...] = total[:share]
        for i, ref in enumerate(rest_refs):
            ref[...] = total[(i + 1) * share : (i + 2) * share].astype(low)


def mid_kernel(x_ref, gain_ref, mask_ref, own_ref, *refs):
    received, (mid_ref, inv_ref, message_ref) = refs[:-3], refs[-3:]
    mid = own_ref[...]
    for one in received:
        mid = mid + one[...].astype(full)
    mid = x_ref[0].astype(full) + mid
    inverse = rms_scale(mid)
    mid_ref[...] = mid
    inv_ref[...] = inverse
    width = mid.shape[1]
    message_ref[:, :width] = (mid * inverse * gain_ref[...]).astype(low)
    message_ref[:, width:] = mask_ref[...]


def expert_kernel(
    part, inner, index_ref, row_near, row_far, grad_near, grad_far, router_ref, gu_any, down_any, *refs
):
    near_ref, far_ref, moe_near_ref, moe_far_ref, *refs = refs
    all_any, x_ref, hidden_ref, dgu_ref, deo_ref, x_tile, g_tile, gu, down, sems = refs
    step = pl.program_id(0)
    rows, width = g_tile.shape
    tile = rows // 2
    slots, ffw = hidden_ref.shape
    experts = router_ref.shape[0]
    expert = index_ref[0]
    share = grad_near.shape[2]
    each = tile // (inner * share)
    half_rows = row_near.shape[0]
    x_in, x_out, g_in = [], [], []
    used = 0
    for i, ref in enumerate((row_near, row_far)):
        here = x_tile.at[pl.ds(i * tile, tile)]
        x_in.append(pltpu.make_async_copy(ref.at[pl.ds(step * tile, tile)], here, sems.at[used]))
        to = (2 * part + i) * half_rows + step * tile
        x_out.append(
            pltpu.make_async_copy(
                x_tile.at[pl.ds(i * tile, tile), pl.ds(0, width)], all_any.at[pl.ds(to, tile)], sems.at[used + 1]
            )
        )
        used += 2
    for i, ref in enumerate((grad_near, grad_far)):
        for c in range(each):
            for w in range(inner):
                at = i * tile + (c * inner + w) * share
                source = ref.at[step * each + c, index_ref[1] ^ (part * inner + w)]
                g_in.append(pltpu.make_async_copy(source, g_tile.at[pl.ds(at, share)], sems.at[used]))
                used += 1
    copy_gu = pltpu.make_async_copy(gu_any.at[0], gu, sems.at[used])
    copy_down = pltpu.make_async_copy(down_any.at[0], down, sems.at[used + 1])
    for one in x_in + g_in:
        one.start()

    @pl.when(step == 0)
    def _():
        copy_gu.start()
        copy_down.start()

    earlier = lax.broadcasted_iota(jnp.int32, (rows, rows), 0) < lax.broadcasted_iota(jnp.int32, (rows, rows), 1)
    for one in x_in:
        one.wait()
    for one in x_out:
        one.start()
    mask = x_tile[:, width:]
    mine = lax.broadcasted_iota(jnp.int32, (8, mask.shape[1]), 1) == expert
    routed = dot(jnp.where(mine, 1.0, 0.0).astype(low), mask, 1, 1)
    place = dot(routed.astype(low), jnp.where(earlier, 1.0, 0.0).astype(low))
    slot = lax.broadcasted_iota(jnp.int32, (slots, rows), 0).astype(full)
    draw = jnp.where(jnp.where(routed[:1] > 0.5, place[:1], -1.0) == slot, 1.0, 0.0).astype(low)
    drawn = dot(draw, x_tile[...]).astype(low)
    x = drawn[:, :width]
    x_ref[...] = x
    chosen = drawn[:, width:][:, :experts].astype(full) > 0.5
    logits = jnp.where(chosen, dot(x, router_ref[...], 1, 1), -1e30)
    shifted = jnp.exp(logits - jnp.max(logits, axis=-1, keepdims=True))
    shifted = jnp.where(chosen, shifted, 0.0)
    own_lane = lax.broadcasted_iota(jnp.int32, shifted.shape, 1) == expert
    total = jnp.sum(shifted, axis=-1, keepdims=True)
    own = jnp.sum(jnp.where(own_lane, shifted, 0.0), axis=-1, keepdims=True) / jnp.where(total > 0.0, total, 1.0)
    for one in g_in:
        one.wait()
    g = dot(draw, g_tile[...])
    deo = (g * own).astype(low)
    deo_ref[...] = deo

    @pl.when(step == 0)
    def _():
        copy_gu.wait()

    gate_up = dot(x, gu[...])

    @pl.when(step == 0)
    def _():
        copy_down.wait()

    gate, up = gate_up[:, :ffw], gate_up[:, ffw:]
    dhid = dot(deo, down[...], 1, 1)
    sig = jax.nn.sigmoid(gate)
    silu = gate * sig
    hidden = (silu * up).astype(low)
    hidden_ref[...] = hidden
    dgate = (dhid * up * (sig + silu * (1.0 - sig))).astype(low)
    dup = (dhid * silu).astype(low)
    dgu_ref[:, :ffw] = dgate
    dgu_ref[:, ffw:] = dup
    out = dot(hidden, down[...]).astype(low).astype(full)
    dlw = jnp.sum(out * g, axis=-1, keepdims=True)
    moe = (out * own).astype(low)
    back = (dot(dgate, gu[:, :ffw], 1, 1) + dot(dup, gu[:, ffw:], 1, 1)).astype(low)
    high = dlw.astype(low)
    rest = (dlw - high.astype(full)).astype(low).astype(full)
    cols = near_ref.shape[1] - width
    lane = lax.broadcasted_iota(jnp.int32, (slots, cols), 1)
    extra = jnp.where(lane == expert, high.astype(full), 0.0)
    extra = jnp.where(lane == experts + expert, rest, extra).astype(low)
    for i, (ref, moe_ref) in enumerate(((near_ref, moe_near_ref), (far_ref, moe_far_ref))):
        lay = draw[:, i * tile : (i + 1) * tile]
        ref[:, :width] = dot(lay, back, 0, 0).astype(low)
        ref[:, width : width + cols] = dot(lay, extra, 0, 0).astype(low)
        moe_ref[...] = dot(lay, moe, 0, 0).astype(low)
    for one in x_out:
        one.wait()


def run_expert(part, part_count, inner, rows, grads, router, w_gate_up, w_down, index, into, cols, most):
    chips, wt_count, share, width = grads[0].shape
    half_rows = chips * inner * share
    tile = min(256, half_rows)
    steps = half_rows // tile
    slots = -(-2 * tile // share * most // 16) * 16
    ffw = w_down.shape[1]
    wide = rows[0].shape[-1]
    widths = [cols, width]
    outs, out_specs = [], []
    for one in widths:
        outs += [shape_of((half_rows, one), low)] * 2
        out_specs += [pl.BlockSpec((tile, one), lambda i: (i, 0))] * 2
    lead_outs = len(outs)
    outs.append(shape_of((2 * half_rows * part_count, width), low))
    out_specs.append(in_any)
    for one in (width, ffw, 2 * ffw, width):
        outs.append(shape_of((part_count * steps * slots, one), low))
        out_specs.append(pl.BlockSpec((slots, one), lambda i: (i + part * steps, 0)))
    ins = [in_smem] + [in_any] * 4 + [pl.BlockSpec(router.shape, lambda i: (0, 0)), in_any, in_any]
    args = [index, *rows, *grads, router, w_gate_up, w_down]
    lead = len(args)
    aliases = {}
    if into is not None:
        for i, array in enumerate(into):
            aliases[len(args)] = lead_outs + i
            ins.append(in_any)
            args.append(array)

    def body(*refs):
        expert_kernel(part, inner, *refs[:lead], *refs[len(args) :])

    results = kernel_call(
        body,
        outs,
        ins,
        args,
        grid=(steps,),
        out_specs=out_specs,
        scratch_shapes=[
            pltpu.VMEM((2 * tile, wide), low),
            pltpu.VMEM((2 * tile, width), low),
            pltpu.VMEM(w_gate_up.shape[1:], low),
            pltpu.VMEM(w_down.shape[1:], low),
            pltpu.SemaphoreType.DMA((6 + 2 * tile // share,)),
        ],
        input_output_aliases=aliases,
    )
    return results[:lead_outs], results[lead_outs:]


def pack_kernel(attn_ref, *refs):
    out_ref, share = refs[-1], refs[0].shape[0]
    wide = refs[0].shape[1]
    for i, ref in enumerate(refs[:-1]):
        out_ref[i * share : (i + 1) * share, :wide] = ref[...]
    rows, cols = out_ref.shape[0], attn_ref.shape[1]
    for i in range(attn_ref.shape[0] // rows):
        out_ref[:, wide + i * cols : wide + (i + 1) * cols] = attn_ref[i * rows : (i + 1) * rows]


def unpack_kernel(*refs):
    in_refs, (rows_ref, attn_ref) = refs[:-2], refs[-2:]
    rows, wide, cols = in_refs[0].shape[0], rows_ref.shape[1], attn_ref.shape[1]
    at = 0
    for i, ref in enumerate(in_refs):
        rows_ref[i * rows : (i + 1) * rows] = ref[:, :wide]
        for j in range((ref.shape[1] - wide) // cols):
            attn_ref[at : at + rows] = ref[:, wide + j * cols : wide + (j + 1) * cols]
            at += rows


def last_kernel(index_ref, x_ref, inv_ref, gain_ref, grad_ref, proj_ref, gains_ref, own_ref, *refs):
    *received, last_ref, message_ref, parts, stack = refs
    total = own_ref[...]
    share, width = total.shape
    for one in received:
        total = total + one[:, :width].astype(full)
    grad = grad_ref[...] + norm_back(total, x_ref[0].astype(full), inv_ref[:share], gain_ref[...])
    last_ref[...] = grad.astype(low)
    parts[index_ref[0]] = gains_ref[...]
    for i, one in enumerate(received):
        for j in range(gains_ref.shape[0] // share):
            cols = slice(width + j * 128, width + (j + 1) * 128)
            parts[index_ref[0] ^ (i + 1), j * share : (j + 1) * share] = one[:, cols].astype(full)
    gains = parts[0]
    for i in range(1, parts.shape[0]):
        gains = gains + parts[i]
    count = 2 * width // 128 + 2 * 1
    stack_split(stack, gains[:count] + gains[count : 2 * count])
    rows = proj_ref.shape[0]
    more = message_ref.shape[0] - rows
    message_ref[:rows] = proj_ref[...]
    message_ref[rows:] = jnp.zeros((more, message_ref.shape[1]), low)
    for j in range(stack.shape[0] // more):
        message_ref[rows:, j * 128 : (j + 1) * 128] = stack[j * more : (j + 1) * more].astype(low)


def join_kernel(*refs):
    out_ref, at = refs[-1], 0
    for ref in refs[:-1]:
        out_ref[at : at + ref.shape[0]] = ref[...]
        at += ref.shape[0]


def join(pieces, after=()):
    rows = sum(one.shape[0] for one in pieces)
    return kernel_call(
        join_kernel,
        shape_of((rows, pieces[0].shape[1]), pieces[0].dtype),
        [in_vmem] * len(pieces),
        list(pieces),
        after,
    )


def cut_kernel(pieces, index_ref, rows_ref, from_ref, *out_refs):
    whole = rows_ref.shape[1]
    cols = out_refs[0].shape[1] - whole
    for k in range(pieces):
        out_refs[k][:, :whole] = rows_ref[...]
        start = pl.multiple_of((index_ref[0] ^ k) * cols, 128)
        out_refs[k][:, whole:] = from_ref[:, pl.ds(start, cols)]


def deal_kernel(pieces, whole, index_ref, *refs):
    in_refs, (own_ref, keep_ref, give_ref) = refs[:pieces], refs[pieces:]
    rows = in_refs[0].shape[0]
    cols = (in_refs[0].shape[1] - whole) // 2
    for i, ref in enumerate(in_refs):
        at = slice(i * rows, (i + 1) * rows)
        own_ref[at] = ref[:, :whole]
        give_ref[at, :whole] = ref[:, :whole]
        keep = pl.multiple_of(whole + index_ref[0] * cols, 128)
        give = pl.multiple_of(whole + (1 - index_ref[0]) * cols, 128)
        keep_ref[at] = ref[:, pl.ds(keep, cols)]
        give_ref[at, whole:] = ref[:, pl.ds(give, cols)]


def deal(core, pieces, whole, **more):
    rows, wide = pieces[0].shape
    cols = (wide - whole) // 2
    total = rows * len(pieces)
    return kernel_call(
        functools.partial(deal_kernel, len(pieces), whole),
        [shape_of((total, whole), low), shape_of((total, cols), low), shape_of((total, whole + cols), low)],
        [in_smem] + [in_vmem] * len(pieces),
        [core, *pieces],
        **more,
    )


def mid_back_kernel(index_ref, sum_ref, rows_ref, mask_ref, router_ref, mid_ref, inv_ref, gain_ref, g_ref, *refs):
    *received, grad_ref, part_ref, message_ref, cols = refs
    total = sum_ref[...]
    for one in received:
        total = total + one[...].astype(full)
    width = grad_ref.shape[1]
    experts = router_ref.shape[0]
    weight_grads = total[:, width : width + experts] + total[:, width + experts : width + 2 * experts]
    chosen = mask_ref[:, :experts].astype(full) > 0.5
    logits = jnp.where(chosen, dot(rows_ref[:, :width], router_ref[...], 1, 1), -1e30)
    shifted = jnp.where(chosen, jnp.exp(logits - jnp.max(logits, axis=-1, keepdims=True)), 0.0)
    routes = shifted / jnp.sum(shifted, axis=-1, keepdims=True)
    logits_grad = routes * (weight_grads - jnp.sum(routes * weight_grads, axis=-1, keepdims=True))
    high, rest = split_low(logits_grad)
    cols[...] = jnp.zeros_like(cols)
    cols[:, :experts] = high.astype(full)
    cols[:, experts : 2 * experts] = rest.astype(full)
    grad = total[:, :width] + dot(high, router_ref[...]) + dot(rest, router_ref[...])
    mid, inverse = mid_ref[...], inv_ref[...]
    part_ref[...] = jnp.sum(grad * mid * inverse, axis=0, keepdims=True)
    grad = g_ref[index_ref[0]].astype(full) + norm_back(grad, mid, inverse, gain_ref[...])
    grad_ref[...] = grad
    message_ref[:, :width] = grad.astype(low)
    message_ref[:, width:] = cols[...].astype(low)


def attend_back_kernel(scale, pieces, index_ref, w_ref, probs_ref, keys_ref, values_ref, q_ref, raw_ref,
                       gain_ref, cos_ref, sin_ref, *refs):
    da_refs = refs[:pieces]
    kv_near_ref, kv_far_ref, dq_ref, part_ref, *message_refs, da_ref, acc = refs[pieces:]
    step = pl.program_id(0)
    tokens, head_dim = cos_ref.shape
    share = da_refs[0].shape[0]
    width = da_ref.shape[1]
    logit_cols = da_refs[0].shape[1] - width

    @pl.when(step == 0)
    def _():
        for i, ref in enumerate(da_refs):
            da_ref[i * share : (i + 1) * share] = ref[:, :width]
            for k, one in enumerate(message_refs):
                one[i * share : (i + 1) * share, :logit_cols] = ref[:, width:]
        for k, one in enumerate(message_refs):
            cols = one.shape[1] - logit_cols
            start = pl.multiple_of((index_ref[0] ^ k) * cols, 128)
            one[:, logit_cols:] = da_ref[:, pl.ds(start, cols)]
        acc[...] = jnp.zeros_like(acc)
        part_ref[...] = jnp.zeros_like(part_ref)

    dattn = dot(da_ref[...], w_ref[...], 1, 1).astype(low)
    heads = dattn.shape[1] // head_dim
    out_grad = jnp.concatenate(
        [dattn[:, h * head_dim : (h + 1) * head_dim] for h in range(heads)], axis=0
    )
    probs_low = probs_ref[...]
    probs = probs_low.astype(full)
    prob_grad = dot(out_grad, values_ref[...], 1, 1)
    inner = jnp.sum(probs * prob_grad, axis=-1, keepdims=True)
    score_grad = (probs * (prob_grad - inner)).astype(low)
    query_grad = (dot(score_grad, keys_ref[...]) * scale).astype(low).astype(full)
    acc[:, :head_dim] += dot(score_grad, q_ref[...], 0, 0)
    acc[:, head_dim:] += dot(probs_low, out_grad, 0, 0)
    gain = gain_ref[...]
    part = part_ref[...]
    for h in range(heads):
        cols = slice(h * head_dim, (h + 1) * head_dim)
        turned = rotate(query_grad[h * tokens : (h + 1) * tokens], cos_ref[...], -sin_ref[...])
        raw = raw_ref[:, cols]
        inverse = rms_scale(raw)
        part = part + jnp.sum(turned * raw * inverse, axis=0, keepdims=True)
        dq_ref[:, cols] = norm_back(turned, raw, inverse, gain).astype(low)
    part_ref[...] = part

    @pl.when(step == pl.num_programs(0) - 1)
    def _():
        near = kv_near_ref.shape[0]
        for ref, at in ((kv_near_ref, 0), (kv_far_ref, near)):
            ref[:, :head_dim] = (acc[at : at + near, :head_dim] * scale).astype(low)
            ref[:, head_dim:] = acc[at : at + near, head_dim:].astype(low)


def stack_rows(stack, at, row):
    for k in range(row.shape[1] // 128):
        stack[at + k : at + k + 1] = row[:, k * 128 : (k + 1) * 128]


def stack_split(stack, values):
    count = values.shape[0]
    high = values.astype(low).astype(full)
    stack[...] = jnp.zeros_like(stack)
    stack[:count] = high
    stack[count : 2 * count] = (values - high).astype(low).astype(full)


def tail_kernel(pieces, moe_part_ref, query_part_ref, dn_ref, dq_ref, raw_ref, kgain_ref, cos_ref, sin_ref, kw_ref, vw_ref, x_ref,
                inv_ref, *refs):
    kv_refs = refs[:pieces]
    own_ref, *rest_refs, proj_ref, gains_ref, values = refs[pieces:]
    total = kv_refs[0][...].astype(full)
    for ref in kv_refs[1:]:
        total = total + ref[...].astype(full)
    head_dim = raw_ref.shape[1]
    query_cols = dq_ref.shape[1]
    turned = rotate(total[:, :head_dim].astype(low).astype(full), cos_ref[...], -sin_ref[...])
    dv = total[:, head_dim:].astype(low)
    raw = raw_ref[...]
    inverse = rms_scale(raw)
    key_part = jnp.sum(turned * raw * inverse, axis=0, keepdims=True)
    dk = norm_back(turned, raw, inverse, kgain_ref[...]).astype(low)
    proj_ref[:, :query_cols] = dq_ref[...]
    proj_ref[:, query_cols : query_cols + head_dim] = dk
    proj_ref[:, query_cols + head_dim :] = dv
    grad = dn_ref[...] + dot(dk, kw_ref[...], 1, 1) + dot(dv, vw_ref[...], 1, 1)
    blocks, share, _ = x_ref.shape
    width = grad.shape[1]
    part = jnp.zeros((1, width), full)
    for i in range(blocks):
        one = grad[i * share : (i + 1) * share]
        x = x_ref[i].astype(full)
        part = part + jnp.sum(one * x * inv_ref[i * share : (i + 1) * share], axis=0, keepdims=True)
        if i == 0:
            own_ref[...] = one
        else:
            rest_refs[i - 1][:, :width] = one.astype(low)
    stack_rows(values, 0, part)
    stack_rows(values, width // 128, moe_part_ref[...])
    stack_rows(values, 2 * width // 128, query_part_ref[...])
    stack_rows(values, (2 * width + head_dim) // 128, key_part)
    stack_split(gains_ref, values[...])
    for ref in rest_refs:
        for j in range(gains_ref.shape[0] // share):
            cols = slice(width + j * 128, width + (j + 1) * 128)
            ref[:, cols] = gains_ref[j * share : (j + 1) * share].astype(low)


def output_kernel(a_near, a_far, b_near, b_far, out_ref):
    rows, cols = out_ref.shape
    far = b_far.shape[1] - cols
    out_ref[...] = dot(a_near[...], b_near[...], 0, 0) + dot(a_far[:, :rows], b_far[:, far:], 0, 0)


def projection_kernel(pieces, index_ref, a_near, a_far, b_near, b_far, query_ref, key_ref, value_ref, *refs):
    *gain_refs, b, parts = refs
    far = a_far.shape[1] - a_near.shape[1]
    each = a_near.shape[0] // pieces
    rows = b_near.shape[0] // pieces
    more = rows - each
    for i, b_ref in enumerate((b_near, b_far)):
        for k in range(pieces):
            at = i * pieces + k
            b[at * each : (at + 1) * each] = b_ref[k * rows : k * rows + each]
            for j in range(parts.shape[1] // more):
                cols = slice(j * 128, (j + 1) * 128)
                parts[index_ref[0] ^ (2 * k + i), j * more : (j + 1) * more] = b_ref[
                    k * rows + each : (k + 1) * rows, cols
                ].astype(full)
    gains = parts[0]
    for i in range(1, 2 * pieces):
        gains = gains + parts[i]
    count = sum(ref.shape[0] for ref in gain_refs)
    gains = gains[:count] + gains[count : 2 * count]
    at = 0
    for ref in gain_refs:
        ref[...] = gains[at : at + ref.shape[0]]
        at += ref.shape[0]
    half = pieces * each
    total = dot(a_near[...], b[:half], 0, 0) + dot(a_far[:, far:], b[half:], 0, 0)
    cols, more = query_ref.shape[1], key_ref.shape[1]
    query_ref[...] = total[:, :cols]
    key_ref[...] = total[:, cols : cols + more]
    value_ref[...] = total[:, cols + more :]


def router_kernel(index_ref, rows_any, near_ref, far_ref, out_ref, rows, grads, sems):
    part_count, groups, inner, share, _ = rows_any.shape
    copies = []
    for p in range(part_count):
        for c in range(groups):
            half = groups // 2
            mask = 2 * (c % half) + c // half
            for w in range(inner):
                to = (index_ref[0] ^ mask) * (part_count * inner) + (index_ref[1] ^ (p * inner + w))
                copy = pltpu.make_async_copy(rows_any.at[p, c, w], rows.at[to], sems.at[len(copies)])
                copy.start()
                copies.append(copy)
                grad_ref = near_ref if c < half else far_ref
                at = ((c % half) * (part_count * inner) + p * inner + w) * share
                grads[to] = grad_ref[at : at + share, : grads.shape[2]]
    for copy in copies:
        copy.wait()
    count = rows.shape[0] * share
    total = dot(grads[...].reshape(count, grads.shape[2]), rows[...].reshape(count, rows.shape[2]), 0, 0)
    experts = out_ref.shape[0]
    out_ref[...] = total[:experts] + total[experts : 2 * experts]


def place_kernel(pieces, index_ref, *refs):
    piece_refs, out_refs = refs[:pieces], refs[pieces:]
    width = out_refs[0].shape[2]
    for i, ref in enumerate(piece_refs):
        for j, out_ref in enumerate(out_refs):
            out_ref[index_ref[0] ^ i] = ref[:, j * width : (j + 1) * width]


def place_rows(index, pieces, width, count, **more):
    share = pieces[0].shape[0]
    return kernel_call(
        functools.partial(place_kernel, len(pieces)),
        [shape_of((len(pieces), share, width), pieces[0].dtype)] * count,
        [in_smem] + [in_vmem] * len(pieces),
        [index.reshape(1), *pieces],
        **more,
    )


def gather_wt(array):
    return [array] + [swap(array, "wt", m) for m in range(1, lax.axis_size("wt"))]


def near_ctx(array):
    return [array] + [swap(array, "ctx", 2 * k) for k in range(1, lax.axis_size("ctx") // 2)]


def far_ctx(arrays):
    return [swap(one, "ctx", 1) for one in arrays]


def split_low(array):
    high = array.astype(low)
    return high, (array - high.astype(full)).astype(low)


def on_device(
    tokens,
    cotangent,
    routes,
    attn_gain,
    query_gain,
    key_gain,
    w_query,
    key_weight,
    value_weight,
    w_output,
    moe_gain,
    w_router,
    w_gate_up,
    w_down,
):
    _, pair_len, width = tokens.shape
    head_dim = query_gain.shape[0]
    query_cols = w_query.shape[1]
    heads = query_cols // head_dim
    share, top_count = routes.shape
    experts = w_router.shape[1]
    ctx_count = lax.axis_size("ctx")
    wt_count = lax.axis_size("wt")
    half = ctx_count // 2
    ctx_index = lax.axis_index("ctx")
    wt_index = lax.axis_index("wt")
    my_expert = ctx_index * wt_count + wt_index
    scale = head_dim ** (-0.5)
    head_step = 2
    parts = 2
    inner = wt_count // parts
    mask_cols = -(-experts // 128) * 128
    extra_cols = -(-2 * experts // 128) * 128
    index = wt_index.reshape(1)
    chip = (ctx_index >> 1).reshape(1)
    core = (ctx_index & 1).reshape(1)
    router = w_router.T

    def plane_swap(blocks):
        return [swap(blocks[k], "ctx", 2 * k) for k in range(1, half)]

    def joined(pieces):
        return jnp.concatenate(pieces, axis=0) if len(pieces) > 1 else pieces[0]

    def both(pieces, after=()):
        near = join(pieces, after)
        return [near, swap(near, "ctx", 1)]


    place = jnp.arange(pair_len, dtype=jnp.int32)
    offsets = ((place // share) ^ wt_index) * share + place % share
    near_masks = 2 * jnp.arange(half, dtype=jnp.int32)
    masks = jnp.concatenate([near_masks, near_masks + 1])
    own_positions = mirrored(ctx_index, offsets, ctx_count, pair_len // 2)
    key_positions = mirrored(
        (ctx_index ^ masks)[:, None], offsets[None, :], ctx_count, pair_len // 2
    ).reshape(1, -1)
    row_positions = jnp.tile(own_positions, head_step).reshape(-1, 1)
    frequency = rope_base ** (-2.0 * jnp.arange(head_dim // 2, dtype=full) / head_dim)
    angles = own_positions.astype(full)[:, None] * frequency[None, :]
    cosine, sine = jnp.cos(angles), jnp.sin(angles)
    cosine = jnp.concatenate([cosine, cosine], axis=1)
    sine = jnp.concatenate([-sine, sine], axis=1)

    expert_ids = jnp.arange(mask_cols, dtype=jnp.int32)
    own_mask = jnp.any(routes[:, :, None] == expert_ids, axis=1).astype(low)
    block_cols = width // ctx_count
    token_rows, normed_one, inverse_one, raw_key, *kv_messages = kernel_call(
        front_kernel,
        [
            shape_of((wt_count, share, width), low),
            shape_of((pair_len, width), low),
            shape_of((pair_len, 1), full),
            shape_of((pair_len, head_dim), full),
        ]
        + [shape_of((pair_len, 2 * head_dim + 2 * block_cols), low)] * half,
        [in_smem] + [in_vmem] * 7,
        [
            jnp.stack([wt_index, ctx_index >> 1]),
            tokens.reshape(wt_count, share, width),
            attn_gain.reshape(1, -1),
            key_weight,
            value_weight,
            key_gain.reshape(1, -1),
            cosine,
            sine,
        ],
    )

    kv_near = [kv_messages[0]] + plane_swap(kv_messages)
    raw_query, queries = kernel_call(
        query_kernel,
        [shape_of((pair_len, query_cols), full), shape_of((heads * pair_len, head_dim), low)],
        [
            pl.BlockSpec((pair_len, width), lambda i: (0, 0)),
            pl.BlockSpec((width, head_step * head_dim), lambda i: (0, i)),
            pl.BlockSpec((1, head_dim), lambda i: (0, 0)),
            pl.BlockSpec((pair_len, head_dim), lambda i: (0, 0)),
            pl.BlockSpec((pair_len, head_dim), lambda i: (0, 0)),
        ],
        [normed_one, w_query, query_gain.reshape(1, -1), cosine, sine],
        grid=(heads // head_step,),
        out_specs=[
            pl.BlockSpec((pair_len, head_step * head_dim), lambda i: (0, i)),
            pl.BlockSpec((head_step * pair_len, head_dim), lambda i: (i, 0)),
        ],
    )

    grad_near = near_ctx(cotangent[0])
    kv_here, normed_keep, kv_give = deal(core, kv_near, 2 * head_dim)
    kv_got = swap(kv_give, "ctx", 1)
    kv_pieces = [kv_here, kv_got]

    total_keys = ctx_count * pair_len
    attn_rows, probs, keys, values, branch_own, *branch_rest = kernel_call(
        functools.partial(attend_kernel, scale, 2),
        [
            shape_of((pair_len, query_cols), low),
            shape_of((heads * pair_len, total_keys), low),
            shape_of((total_keys, head_dim), low),
            shape_of((total_keys, head_dim), low),
            shape_of((share, width), full),
        ]
        + [shape_of((share, width), low)] * (wt_count - 1),
        [
            pl.BlockSpec((head_step * pair_len, 1), lambda i: (0, 0)),
            pl.BlockSpec((1, total_keys), lambda i: (0, 0)),
            pl.BlockSpec((head_step * pair_len, head_dim), lambda i: (i, 0)),
            in_any,
        ]
        + [pl.BlockSpec(one.shape, lambda i: (0, 0)) for one in kv_pieces],
        [row_positions, key_positions, queries, w_output, *kv_pieces],
        grid=(heads // head_step,),
        out_specs=[
            pl.BlockSpec((pair_len, query_cols), lambda i: (0, 0)),
            pl.BlockSpec((head_step * pair_len, total_keys), lambda i: (i, 0)),
            pl.BlockSpec((total_keys, head_dim), lambda i: (0, 0)),
            pl.BlockSpec((total_keys, head_dim), lambda i: (0, 0)),
        ]
        + [pl.BlockSpec((share, width), lambda i: (0, 0))] * wt_count,
        scratch_shapes=[
            pltpu.VMEM((heads // head_step, pair_len, head_step * head_dim), low),
            pltpu.VMEM(w_output.shape, low),
            pltpu.SemaphoreType.DMA,
        ],
    )
    branch_rest, branch_own, attn_rows = fence(branch_rest, branch_own, attn_rows)
    received = [swap(branch_rest[m - 1], "wt", m) for m in range(1, wt_count)]
    mid_rows, inverse_two, message = kernel_call(
        mid_kernel,
        [
            shape_of((share, width), full),
            shape_of((share, 1), full),
            shape_of((share, width + mask_cols), low),
        ],
        [in_vmem] * (3 + wt_count),
        [token_rows, moe_gain.reshape(1, -1), own_mask, branch_own, *received],
    )
    residual_rows = token_rows[0].astype(full)

    first = join([message] + [swap(message, "wt", m) for m in range(1, inner)])
    others = [swap(message, "wt", m) for m in range(inner, wt_count)]
    grads = [one.reshape(half, wt_count, share, width) for one in both(grad_near, message)]
    chunks = pair_len // (inner * share)
    second = kernel_call(
        pack_kernel,
        shape_of((inner * share, width + mask_cols + chunks * query_cols), low),
        [in_vmem] * (1 + inner),
        [attn_rows, *others],
    )
    rows_first = both(near_ctx(first), second)
    near_second = near_ctx(second)
    places = jnp.stack([my_expert, wt_index])
    sums_cols = width + extra_cols
    most = max(2, share * top_count * 5 // (4 * experts) + 1)
    results, into = run_expert(
        0, parts, inner, rows_first, grads, router, w_gate_up, w_down, places, None, sums_cols,
        most,
    )
    results, into, near_second = fence(results, into, near_second)
    rows_second, attn_near = kernel_call(
        unpack_kernel,
        [shape_of((half * inner * share, width + mask_cols), low), shape_of((half * pair_len, query_cols), low)],
        [in_vmem] * half,
        near_second,
    )
    rows_second = [rows_second, swap(rows_second, "ctx", 1)]
    attn_got = swap(attn_near, "ctx", 1)

    def split_parts(near, far_sent):
        cols = near.shape[1]
        total = (near + far_sent).reshape(half, inner * share, cols)
        return [total[k] for k in range(half)]

    def plane_sum(blocks, received):
        total = blocks[0].astype(full)
        for one in received:
            total = total + one.astype(full)
        return total

    def wt_parts(sums):
        return [one[w * share : (w + 1) * share] for one in sums for w in range(inner)]

    back_blocks = [split_parts(results[0], swap(results[1], "ctx", 1))]
    moe_blocks = [split_parts(results[2], swap(results[3], "ctx", 1))]
    rows_second, back_blocks, into = fence(rows_second, back_blocks, into)
    back_received = [plane_swap(back_blocks[0])]
    results, into = run_expert(
        1, parts, inner, rows_second, grads, router, w_gate_up, w_down, places, into, sums_cols,
        most,
    )

    results, into, back_received = fence(results, into, back_received)
    back_blocks.append(split_parts(results[0], swap(results[1], "ctx", 1)))
    back_blocks, moe_far, into = fence(back_blocks, results[3], into)
    rows_all, rows_drawn, hidden, gate_up_grad, expert_grad = into
    back_received.append(plane_swap(back_blocks[1]))
    moe_far = swap(moe_far, "ctx", 1)
    w_gate_up_grad = dot(rows_drawn, gate_up_grad, 0, 0)
    w_down_grad = dot(hidden, expert_grad, 0, 0)
    back_received, moe_far, w_gate_up_grad, w_down_grad, attn_rows = fence(
        back_received, moe_far, w_gate_up_grad, w_down_grad, attn_rows
    )
    moe_blocks.append(split_parts(results[2], moe_far))
    moe_received = [plane_swap(moe_blocks[0])]
    sums = wt_parts([plane_sum(b, r) for b, r in zip(back_blocks, back_received)])
    sums_low = [one.astype(low) for one in sums[1:]]
    received = [swap(one, "wt", m + 1) for m, one in enumerate(sums_low)]
    mid_grad, moe_gain_part, mid_message = kernel_call(
        mid_back_kernel,
        [
            shape_of((share, width), full),
            shape_of((1, width), full),
            shape_of((share, width + extra_cols), low),
        ],
        [in_smem] + [in_vmem] * (7 + wt_count),
        [
            index, sums[0], message, own_mask, router, mid_rows, inverse_two, moe_gain.reshape(1, -1),
            cotangent.reshape(wt_count, share, width), *received,
        ],
        after=moe_received,
        scratch_shapes=[pltpu.VMEM((share, extra_cols), full)],
    )

    mid_pieces = gather_wt(mid_message)
    moe_received.append(plane_swap(moe_blocks[1]))
    mid_pieces, moe_received = fence(mid_pieces, moe_received)

    moe_sums = wt_parts([plane_sum(b, r) for b, r in zip(moe_blocks, moe_received)])
    moe_low = [one.astype(low) for one in moe_sums[1:]]
    moe_low, mid_pieces = fence(moe_low, mid_pieces)
    moe_received = [swap(one, "wt", m + 1) for m, one in enumerate(moe_low)]
    kv_part_near, kv_part_far, query_grad, query_gain_part, *logits_messages, _ = kernel_call(
        functools.partial(attend_back_kernel, scale, wt_count),
        [
            shape_of((total_keys // 2, 2 * head_dim), low),
            shape_of((total_keys // 2, 2 * head_dim), low),
            shape_of((pair_len, query_cols), low),
            shape_of((1, head_dim), full),
        ]
        + [shape_of((pair_len, extra_cols + 2 * block_cols), low)] * half
        + [shape_of((pair_len, width), low)],
        [
            in_smem,
            pl.BlockSpec((head_step * head_dim, width), lambda i: (i, 0)),
            pl.BlockSpec((head_step * pair_len, total_keys), lambda i: (i, 0)),
            pl.BlockSpec((total_keys, head_dim), lambda i: (0, 0)),
            pl.BlockSpec((total_keys, head_dim), lambda i: (0, 0)),
            pl.BlockSpec((head_step * pair_len, head_dim), lambda i: (i, 0)),
            pl.BlockSpec((pair_len, head_step * head_dim), lambda i: (0, i)),
            pl.BlockSpec((1, head_dim), lambda i: (0, 0)),
            pl.BlockSpec((pair_len, head_dim), lambda i: (0, 0)),
            pl.BlockSpec((pair_len, head_dim), lambda i: (0, 0)),
        ]
        + [pl.BlockSpec((share, width + extra_cols), lambda i: (0, 0))] * wt_count,
        [
            chip, w_output, probs, keys, values, queries, raw_query, query_gain.reshape(1, -1),
            cosine, sine, *mid_pieces,
        ],
        grid=(heads // head_step,),
        out_specs=[
            pl.BlockSpec((total_keys // 2, 2 * head_dim), lambda i: (0, 0)),
            pl.BlockSpec((total_keys // 2, 2 * head_dim), lambda i: (0, 0)),
            pl.BlockSpec((pair_len, head_step * head_dim), lambda i: (0, i)),
            pl.BlockSpec((1, head_dim), lambda i: (0, 0)),
        ]
        + [pl.BlockSpec((pair_len, extra_cols + 2 * block_cols), lambda i: (0, 0))] * half
        + [pl.BlockSpec((pair_len, width), lambda i: (0, 0))],
        scratch_shapes=[pltpu.VMEM((total_keys, 2 * head_dim), full)],
    )

    kv_part_near, kv_part_far, query_grad, moe_received, logits_messages = fence(
        kv_part_near, kv_part_far, query_grad, moe_received, logits_messages
    )
    kv_near = (kv_part_near + swap(kv_part_far, "ctx", 1)).reshape(half, pair_len, 2 * head_dim)
    kv_near = [kv_near[k] for k in range(half)]
    out_rows = (mid_rows + plane_sum(moe_sums, moe_received)).astype(low)
    kv_near, query_grad, out_rows = fence(kv_near, query_grad, out_rows)
    kv_received = plane_swap(kv_near)
    out_pieces = gather_wt(out_rows)
    query_term = dot(query_grad, w_query, 1, 1)
    kv_received, query_term = fence(kv_received, query_term)
    gain_rows = 2 * width // 128 + 2 * head_dim // 128
    gain_blocks = -(-2 * gain_rows // share)
    one_own, *tail_results = kernel_call(
        functools.partial(tail_kernel, half),
        [shape_of((share, width), full)]
        + [shape_of((share, width + gain_blocks * 128), low)] * (wt_count - 1)
        + [
            shape_of((pair_len, query_cols + 2 * head_dim), low),
            shape_of((gain_blocks * share, 128), full),
        ],
        [in_vmem] * (12 + half),
        [
            moe_gain_part.reshape(1, -1), query_gain_part, query_term, query_grad, raw_key,
            key_gain.reshape(1, -1), cosine, sine, key_weight, value_weight, token_rows, inverse_one,
            kv_near[0], *kv_received,
        ],
        after=[attn_got, out_pieces],
        through=logits_messages,
        scratch_shapes=[pltpu.VMEM((gain_rows, 128), full)],
    )
    one_rest, (projection_own, gains) = tail_results[: wt_count - 1], tail_results[wt_count - 1 : wt_count + 1]
    logits_messages = tail_results[wt_count + 1 :]
    received = [swap(one, "wt", m + 1) for m, one in enumerate(one_rest)]
    logits_near = [logits_messages[0]] + plane_swap(logits_messages)
    logits_own, mid_keep, logits_give = deal(core, logits_near, extra_cols)
    logits_got = swap(logits_give, "ctx", 1)
    message_rows = pair_len + 16
    last_rows, projection = kernel_call(
        last_kernel,
        [shape_of((share, width), low), shape_of((message_rows, query_cols + 2 * head_dim), low)],
        [in_smem] + [in_vmem] * (6 + wt_count),
        [
            index, token_rows, inverse_one, attn_gain.reshape(1, -1), mid_grad, projection_own,
            gains, one_own, *received,
        ],
        after=logits_near,
        scratch_shapes=[
            pltpu.VMEM((wt_count, gain_blocks * share, 128), full),
            pltpu.VMEM((-(-2 * gain_rows // 16) * 16, 128), full),
        ],
    )

    last_pieces = gather_wt(last_rows)
    projection_near = near_ctx(projection)
    router_grad = kernel_call(
        router_kernel,
        shape_of((experts, width), full),
        [in_smem, in_any, in_vmem, in_vmem],
        [
            jnp.stack([ctx_index, wt_index]),
            rows_all.reshape(parts, ctx_count, inner, share, width),
            logits_own,
            logits_got,
        ],
        scratch_shapes=[
            pltpu.VMEM((ctx_count * wt_count, share, width), low),
            pltpu.VMEM((ctx_count * wt_count, share, extra_cols), low),
            pltpu.SemaphoreType.DMA((ctx_count * wt_count,)),
        ],
    )
    w_output_grad = kernel_call(
        output_kernel,
        shape_of((query_cols, block_cols), full),
        [in_vmem] * 4,
        [attn_near, attn_got, mid_keep, logits_got],
    )
    w_query_grad, w_key_grad, w_value_grad, *gains = kernel_call(
        functools.partial(projection_kernel, half),
        [
            shape_of((block_cols, query_cols), full),
            shape_of((block_cols, head_dim), full),
            shape_of((block_cols, head_dim), full),
        ]
        + [shape_of((size // 128, 128), full) for size in (width, width, head_dim, head_dim)],
        [in_smem] + [in_vmem] * 4,
        [ctx_index.reshape(1), normed_keep, kv_got, *both(projection_near, [last_pieces[1:], w_output_grad, router_grad])],
        scratch_shapes=[
            pltpu.VMEM((total_keys, query_cols + 2 * head_dim), low),
            pltpu.VMEM((ctx_count, -(-2 * gain_rows // 16) * 16, 128), full),
        ],
    )
    attn_gain_grad, moe_gain_grad, query_gain_grad, key_gain_grad = [one.reshape(-1) for one in gains]
    (block_out,) = place_rows(index, out_pieces, width, 1)
    (tokens_grad,) = place_rows(
        index, last_pieces, width, 1, after=[router_grad, w_output_grad, w_query_grad]
    )
    w_router_grad = router_grad.T

    return (
        block_out.reshape(1, pair_len, width),
        tokens_grad.reshape(1, pair_len, width),
        attn_gain_grad,
        query_gain_grad,
        key_gain_grad,
        w_query_grad,
        w_key_grad,
        w_value_grad,
        w_output_grad,
        moe_gain_grad,
        w_router_grad,
        w_gate_up_grad[None],
        w_down_grad[None],
    )


def solution(mesh):
    in_specs = (
        P(None, "ctx", None),
        P(None, "ctx", None),
        P(("ctx", "wt"), None),
        P(),
        P(),
        P(),
        P(None, "wt"),
        P(None, "wt"),
        P(None, "wt"),
        P("wt", None),
        P(),
        P(),
        P(("ctx", "wt"), None, None),
        P(("ctx", "wt"), None, None),
    )
    out_specs = (
        P(None, "ctx", None),
        P(None, "ctx", None),
        P(),
        P(),
        P(),
        P("ctx", "wt"),
        P("ctx", "wt"),
        P("ctx", "wt"),
        P("wt", "ctx"),
        P(),
        P(),
        P(("ctx", "wt"), None, None),
        P(("ctx", "wt"), None, None),
    )
    return jax.shard_map(
        on_device, mesh=mesh, in_specs=in_specs, out_specs=out_specs, check_vma=False
    )
```

```python
import functools

import jax
import jax.numpy as jnp
from jax import lax
from jax.experimental import pallas as pl
from jax.experimental.pallas import tpu as pltpu
from jax.sharding import PartitionSpec as P

epsilon = 1e-06
rope_base = 1000000.0
low = jnp.bfloat16
full = jnp.float32
vmem_bytes = 60 * 1024 * 1024

in_vmem = pl.BlockSpec(memory_space=pltpu.VMEM)
in_smem = pl.BlockSpec(memory_space=pltpu.SMEM)
in_any = pl.BlockSpec(memory_space=pl.ANY)


def dot(a, b, a_dim=1, b_dim=0):
    return lax.dot_general(a, b, (((a_dim,), (b_dim,)), ((), ())), preferred_element_type=full)


def swap(array, axis, mask):
    count = lax.axis_size(axis)
    return lax.ppermute(array, axis, [(i, i ^ mask) for i in range(count)])


def fence(*values):
    return lax.optimization_barrier(values)


def shape_of(shape, dtype):
    return jax.ShapeDtypeStruct(tuple(shape), dtype)


def kernel_call(kernel, outs, ins, args, after=(), through=(), **more):
    single = not isinstance(outs, list)
    outs = [outs] if single else list(outs)
    after, through = jax.tree.leaves(after), jax.tree.leaves(through)
    count, lead = len(args), len(outs)
    every = count + len(after) + len(through)

    def body(*refs):
        kernel(*refs[:count], *refs[every : every + lead], *refs[every + lead + len(through) :])

    aliases = dict(more.pop("input_output_aliases", {}))
    if through:
        aliases.update({count + len(after) + i: lead + i for i in range(len(through))})
        more["out_specs"] = list(more.get("out_specs", [in_vmem] * lead)) + [in_any] * len(through)
    results = pl.pallas_call(
        body,
        out_shape=outs + [shape_of(one.shape, one.dtype) for one in through],
        in_specs=[*ins] + [in_any] * (len(after) + len(through)),
        input_output_aliases=aliases,
        compiler_params=pltpu.CompilerParams(vmem_limit_bytes=vmem_bytes),
        **more,
    )(*args, *after, *through)
    return results[0] if single else results


def rms_scale(value_matrix):
    return lax.rsqrt(jnp.mean(value_matrix * value_matrix, axis=-1, keepdims=True) + epsilon)


def norm_back(grad_out, value_matrix, inverse, gain_vec):
    scaled = grad_out * gain_vec
    inner_mean = jnp.mean(scaled * value_matrix, axis=-1, keepdims=True)
    return inverse * (scaled - value_matrix * inverse * inverse * inner_mean)


def mirrored(device, offset, groups, block_len):
    which_block = jnp.where(offset < block_len, device, 2 * groups - 1 - device)
    return which_block * block_len + offset % block_len


def rotate(value_matrix, cosine, sine):
    return value_matrix * cosine + pltpu.roll(value_matrix, value_matrix.shape[-1] // 2, 1) * sine


def front_kernel(
    index_ref, x_ref, gain_ref, kw_ref, vw_ref, kgain_ref, cos_ref, sin_ref,
    rows_ref, normed_ref, inv_ref, raw_ref, *message_refs
):
    blocks, share, _ = x_ref.shape
    for i in range(blocks):
        x_low = x_ref[index_ref[0] ^ i]
        rows_ref[i] = x_low
        x = x_low.astype(full)
        inverse = rms_scale(x)
        inv_ref[i * share : (i + 1) * share] = inverse
        normed_ref[i * share : (i + 1) * share] = (x * inverse * gain_ref[...]).astype(low)
    normed = normed_ref[...]
    raw = dot(normed, kw_ref[...])
    raw_ref[...] = raw
    head_dim = raw.shape[1]
    turned = rotate(raw * rms_scale(raw) * kgain_ref[...], cos_ref[...], sin_ref[...])
    keys = turned.astype(low)
    values = dot(normed, vw_ref[...]).astype(low)
    for k, ref in enumerate(message_refs):
        ref[:, :head_dim] = keys
        ref[:, head_dim : 2 * head_dim] = values
        cols = ref.shape[1] - 2 * head_dim
        start = pl.multiple_of((index_ref[1] ^ k) * cols, 128)
        ref[:, 2 * head_dim :] = normed_ref[:, pl.ds(start, cols)]


def query_kernel(normed_ref, w_ref, gain_ref, cos_ref, sin_ref, raw_ref, q_ref):
    rows, head_dim = cos_ref.shape
    raw = dot(normed_ref[...], w_ref[...])
    raw_ref[...] = raw
    for h in range(raw.shape[1] // head_dim):
        one = raw[:, h * head_dim : (h + 1) * head_dim]
        turned = rotate(one * rms_scale(one) * gain_ref[...], cos_ref[...], sin_ref[...])
        q_ref[h * rows : (h + 1) * rows] = turned.astype(low)


def attend_kernel(scale, pieces, qpos_ref, kpos_ref, q_ref, w_ref, *refs):
    kv_refs = refs[:pieces]
    rows_ref, probs_ref, keys_ref, values_ref, own_ref, *rest_refs, attn, weight, sem = refs[pieces:]
    step = pl.program_id(0)
    tokens, head_dim = rows_ref.shape[0], kv_refs[0].shape[1] // 2
    copy = pltpu.make_async_copy(w_ref, weight, sem)

    @pl.when(step == 0)
    def _():
        copy.start()
        at = 0
        for ref in kv_refs:
            keys_ref[at : at + ref.shape[0]] = ref[:, :head_dim]
            values_ref[at : at + ref.shape[0]] = ref[:, head_dim : 2 * head_dim]
            at += ref.shape[0]

    scores = dot(q_ref[...], keys_ref[...], 1, 1) * scale
    scores = jnp.where(kpos_ref[...] <= qpos_ref[...], scores, -1e30)
    weights = jnp.exp(scores - jnp.max(scores, axis=-1, keepdims=True))
    probs = (weights / jnp.sum(weights, axis=-1, keepdims=True)).astype(low)
    probs_ref[...] = probs
    out = dot(probs, values_ref[...]).astype(low)
    heads = out.shape[0] // tokens
    attn[step] = jnp.concatenate([out[h * tokens : (h + 1) * tokens] for h in range(heads)], axis=1)

    @pl.when(step == pl.num_programs(0) - 1)
    def _():
        copy.wait()
        for i in range(attn.shape[0]):
            rows_ref[:, i * heads * head_dim : (i + 1) * heads * head_dim] = attn[i]
        total = dot(rows_ref[...], weight[...])
        share = own_ref.shape[0]
        own_ref[...] = total[:share]
        for i, ref in enumerate(rest_refs):
            ref[...] = total[(i + 1) * share : (i + 2) * share].astype(low)


def mid_kernel(x_ref, gain_ref, mask_ref, own_ref, *refs):
    received, (mid_ref, inv_ref, message_ref) = refs[:-3], refs[-3:]
    mid = own_ref[...]
    for one in received:
        mid = mid + one[...].astype(full)
    mid = x_ref[0].astype(full) + mid
    inverse = rms_scale(mid)
    mid_ref[...] = mid
    inv_ref[...] = inverse
    width = mid.shape[1]
    message_ref[:, :width] = (mid * inverse * gain_ref[...]).astype(low)
    message_ref[:, width:] = mask_ref[...]


def expert_kernel(
    part, inner, index_ref, row_near, row_far, grad_near, grad_far, router_ref, gu_any, down_any, *refs
):
    near_ref, far_ref, moe_near_ref, moe_far_ref, *refs = refs
    all_any, x_ref, hidden_ref, dgu_ref, deo_ref, x_tile, g_tile, gu, down, sems = refs
    step = pl.program_id(0)
    rows, width = g_tile.shape
    tile = rows // 2
    slots, ffw = hidden_ref.shape
    experts = router_ref.shape[0]
    expert = index_ref[0]
    share = grad_near.shape[2]
    each = tile // (inner * share)
    half_rows = row_near.shape[0]
    x_in, x_out, g_in = [], [], []
    used = 0
    for i, ref in enumerate((row_near, row_far)):
        here = x_tile.at[pl.ds(i * tile, tile)]
        x_in.append(pltpu.make_async_copy(ref.at[pl.ds(step * tile, tile)], here, sems.at[used]))
        to = (2 * part + i) * half_rows + step * tile
        x_out.append(
            pltpu.make_async_copy(
                x_tile.at[pl.ds(i * tile, tile), pl.ds(0, width)], all_any.at[pl.ds(to, tile)], sems.at[used + 1]
            )
        )
        used += 2
    for i, ref in enumerate((grad_near, grad_far)):
        for c in range(each):
            for w in range(inner):
                at = i * tile + (c * inner + w) * share
                source = ref.at[step * each + c, index_ref[1] ^ (part * inner + w)]
                g_in.append(pltpu.make_async_copy(source, g_tile.at[pl.ds(at, share)], sems.at[used]))
                used += 1
    copy_gu = pltpu.make_async_copy(gu_any.at[0], gu, sems.at[used])
    copy_down = pltpu.make_async_copy(down_any.at[0], down, sems.at[used + 1])
    for one in x_in + g_in:
        one.start()

    @pl.when(step == 0)
    def _():
        copy_gu.start()
        copy_down.start()

    earlier = lax.broadcasted_iota(jnp.int32, (rows, rows), 0) < lax.broadcasted_iota(jnp.int32, (rows, rows), 1)
    for one in x_in:
        one.wait()
    for one in x_out:
        one.start()
    mask = x_tile[:, width:]
    mine = lax.broadcasted_iota(jnp.int32, (8, mask.shape[1]), 1) == expert
    routed = dot(jnp.where(mine, 1.0, 0.0).astype(low), mask, 1, 1)
    place = dot(routed.astype(low), jnp.where(earlier, 1.0, 0.0).astype(low))
    slot = lax.broadcasted_iota(jnp.int32, (slots, rows), 0).astype(full)
    draw = jnp.where(jnp.where(routed[:1] > 0.5, place[:1], -1.0) == slot, 1.0, 0.0).astype(low)
    drawn = dot(draw, x_tile[...]).astype(low)
    x = drawn[:, :width]
    x_ref[...] = x
    chosen = drawn[:, width:][:, :experts].astype(full) > 0.5
    logits = jnp.where(chosen, dot(x, router_ref[...], 1, 1), -1e30)
    shifted = jnp.exp(logits - jnp.max(logits, axis=-1, keepdims=True))
    shifted = jnp.where(chosen, shifted, 0.0)
    own_lane = lax.broadcasted_iota(jnp.int32, shifted.shape, 1) == expert
    total = jnp.sum(shifted, axis=-1, keepdims=True)
    own = jnp.sum(jnp.where(own_lane, shifted, 0.0), axis=-1, keepdims=True) / jnp.where(total > 0.0, total, 1.0)
    for one in g_in:
        one.wait()
    g = dot(draw, g_tile[...])
    deo = (g * own).astype(low)
    deo_ref[...] = deo

    @pl.when(step == 0)
    def _():
        copy_gu.wait()

    gate_up = dot(x, gu[...])

    @pl.when(step == 0)
    def _():
        copy_down.wait()

    gate, up = gate_up[:, :ffw], gate_up[:, ffw:]
    dhid = dot(deo, down[...], 1, 1)
    sig = jax.nn.sigmoid(gate)
    silu = gate * sig
    hidden = (silu * up).astype(low)
    hidden_ref[...] = hidden
    dgate = (dhid * up * (sig + silu * (1.0 - sig))).astype(low)
    dup = (dhid * silu).astype(low)
    dgu_ref[:, :ffw] = dgate
    dgu_ref[:, ffw:] = dup
    out = dot(hidden, down[...]).astype(low).astype(full)
    dlw = jnp.sum(out * g, axis=-1, keepdims=True)
    moe = (out * own).astype(low)
    back = (dot(dgate, gu[:, :ffw], 1, 1) + dot(dup, gu[:, ffw:], 1, 1)).astype(low)
    high = dlw.astype(low)
    rest = (dlw - high.astype(full)).astype(low).astype(full)
    cols = near_ref.shape[1] - width
    lane = lax.broadcasted_iota(jnp.int32, (slots, cols), 1)
    extra = jnp.where(lane == expert, high.astype(full), 0.0)
    extra = jnp.where(lane == experts + expert, rest, extra).astype(low)
    for i, (ref, moe_ref) in enumerate(((near_ref, moe_near_ref), (far_ref, moe_far_ref))):
        lay = draw[:, i * tile : (i + 1) * tile]
        ref[:, :width] = dot(lay, back, 0, 0).astype(low)
        ref[:, width : width + cols] = dot(lay, extra, 0, 0).astype(low)
        moe_ref[...] = dot(lay, moe, 0, 0).astype(low)
    for one in x_out:
        one.wait()


def run_expert(part, part_count, inner, rows, grads, router, w_gate_up, w_down, index, into, cols, most):
    chips, wt_count, share, width = grads[0].shape
    half_rows = chips * inner * share
    tile = min(256, half_rows)
    steps = half_rows // tile
    slots = -(-2 * tile // share * most // 16) * 16
    ffw = w_down.shape[1]
    wide = rows[0].shape[-1]
    widths = [cols, width]
    outs, out_specs = [], []
    for one in widths:
        outs += [shape_of((half_rows, one), low)] * 2
        out_specs += [pl.BlockSpec((tile, one), lambda i: (i, 0))] * 2
    lead_outs = len(outs)
    outs.append(shape_of((2 * half_rows * part_count, width), low))
    out_specs.append(in_any)
    for one in (width, ffw, 2 * ffw, width):
        outs.append(shape_of((part_count * steps * slots, one), low))
        out_specs.append(pl.BlockSpec((slots, one), lambda i: (i + part * steps, 0)))
    ins = [in_smem] + [in_any] * 4 + [pl.BlockSpec(router.shape, lambda i: (0, 0)), in_any, in_any]
    args = [index, *rows, *grads, router, w_gate_up, w_down]
    lead = len(args)
    aliases = {}
    if into is not None:
        for i, array in enumerate(into):
            aliases[len(args)] = lead_outs + i
            ins.append(in_any)
            args.append(array)

    def body(*refs):
        expert_kernel(part, inner, *refs[:lead], *refs[len(args) :])

    results = kernel_call(
        body,
        outs,
        ins,
        args,
        grid=(steps,),
        out_specs=out_specs,
        scratch_shapes=[
            pltpu.VMEM((2 * tile, wide), low),
            pltpu.VMEM((2 * tile, width), low),
            pltpu.VMEM(w_gate_up.shape[1:], low),
            pltpu.VMEM(w_down.shape[1:], low),
            pltpu.SemaphoreType.DMA((6 + 2 * tile // share,)),
        ],
        input_output_aliases=aliases,
    )
    return results[:lead_outs], results[lead_outs:]


def pack_kernel(attn_ref, *refs):
    out_ref, share = refs[-1], refs[0].shape[0]
    wide = refs[0].shape[1]
    for i, ref in enumerate(refs[:-1]):
        out_ref[i * share : (i + 1) * share, :wide] = ref[...]
    rows, cols = out_ref.shape[0], attn_ref.shape[1]
    for i in range(attn_ref.shape[0] // rows):
        out_ref[:, wide + i * cols : wide + (i + 1) * cols] = attn_ref[i * rows : (i + 1) * rows]


def unpack_kernel(*refs):
    in_refs, (rows_ref, attn_ref) = refs[:-2], refs[-2:]
    rows, wide, cols = in_refs[0].shape[0], rows_ref.shape[1], attn_ref.shape[1]
    at = 0
    for i, ref in enumerate(in_refs):
        rows_ref[i * rows : (i + 1) * rows] = ref[:, :wide]
        for j in range((ref.shape[1] - wide) // cols):
            attn_ref[at : at + rows] = ref[:, wide + j * cols : wide + (j + 1) * cols]
            at += rows


def last_kernel(index_ref, x_ref, inv_ref, gain_ref, grad_ref, proj_ref, gains_ref, own_ref, *refs):
    *received, last_ref, message_ref, parts, stack = refs
    total = own_ref[...]
    share, width = total.shape
    for one in received:
        total = total + one[:, :width].astype(full)
    grad = grad_ref[...] + norm_back(total, x_ref[0].astype(full), inv_ref[:share], gain_ref[...])
    last_ref[...] = grad.astype(low)
    parts[index_ref[0]] = gains_ref[...]
    for i, one in enumerate(received):
        for j in range(gains_ref.shape[0] // share):
            cols = slice(width + j * 128, width + (j + 1) * 128)
            parts[index_ref[0] ^ (i + 1), j * share : (j + 1) * share] = one[:, cols].astype(full)
    gains = parts[0]
    for i in range(1, parts.shape[0]):
        gains = gains + parts[i]
    count = 2 * width // 128 + 2 * 1
    stack_split(stack, gains[:count] + gains[count : 2 * count])
    rows = proj_ref.shape[0]
    more = message_ref.shape[0] - rows
    message_ref[:rows] = proj_ref[...]
    message_ref[rows:] = jnp.zeros((more, message_ref.shape[1]), low)
    for j in range(stack.shape[0] // more):
        message_ref[rows:, j * 128 : (j + 1) * 128] = stack[j * more : (j + 1) * more].astype(low)


def join_kernel(*refs):
    out_ref, at = refs[-1], 0
    for ref in refs[:-1]:
        out_ref[at : at + ref.shape[0]] = ref[...]
        at += ref.shape[0]


def join(pieces, after=()):
    rows = sum(one.shape[0] for one in pieces)
    return kernel_call(
        join_kernel,
        shape_of((rows, pieces[0].shape[1]), pieces[0].dtype),
        [in_vmem] * len(pieces),
        list(pieces),
        after,
    )


def cut_kernel(pieces, index_ref, rows_ref, from_ref, *out_refs):
    whole = rows_ref.shape[1]
    cols = out_refs[0].shape[1] - whole
    for k in range(pieces):
        out_refs[k][:, :whole] = rows_ref[...]
        start = pl.multiple_of((index_ref[0] ^ k) * cols, 128)
        out_refs[k][:, whole:] = from_ref[:, pl.ds(start, cols)]


def deal_kernel(pieces, whole, index_ref, *refs):
    in_refs, (own_ref, keep_ref, give_ref) = refs[:pieces], refs[pieces:]
    rows = in_refs[0].shape[0]
    cols = (in_refs[0].shape[1] - whole) // 2
    for i, ref in enumerate(in_refs):
        at = slice(i * rows, (i + 1) * rows)
        own_ref[at] = ref[:, :whole]
        give_ref[at, :whole] = ref[:, :whole]
        keep = pl.multiple_of(whole + index_ref[0] * cols, 128)
        give = pl.multiple_of(whole + (1 - index_ref[0]) * cols, 128)
        keep_ref[at] = ref[:, pl.ds(keep, cols)]
        give_ref[at, whole:] = ref[:, pl.ds(give, cols)]


def deal(core, pieces, whole, **more):
    rows, wide = pieces[0].shape
    cols = (wide - whole) // 2
    total = rows * len(pieces)
    return kernel_call(
        functools.partial(deal_kernel, len(pieces), whole),
        [shape_of((total, whole), low), shape_of((total, cols), low), shape_of((total, whole + cols), low)],
        [in_smem] + [in_vmem] * len(pieces),
        [core, *pieces],
        **more,
    )


def mid_back_kernel(index_ref, sum_ref, rows_ref, mask_ref, router_ref, mid_ref, inv_ref, gain_ref, g_ref, *refs):
    *received, grad_ref, part_ref, message_ref, cols = refs
    total = sum_ref[...]
    for one in received:
        total = total + one[...].astype(full)
    width = grad_ref.shape[1]
    experts = router_ref.shape[0]
    weight_grads = total[:, width : width + experts] + total[:, width + experts : width + 2 * experts]
    chosen = mask_ref[:, :experts].astype(full) > 0.5
    logits = jnp.where(chosen, dot(rows_ref[:, :width], router_ref[...], 1, 1), -1e30)
    shifted = jnp.where(chosen, jnp.exp(logits - jnp.max(logits, axis=-1, keepdims=True)), 0.0)
    routes = shifted / jnp.sum(shifted, axis=-1, keepdims=True)
    logits_grad = routes * (weight_grads - jnp.sum(routes * weight_grads, axis=-1, keepdims=True))
    high, rest = split_low(logits_grad)
    cols[...] = jnp.zeros_like(cols)
    cols[:, :experts] = high.astype(full)
    cols[:, experts : 2 * experts] = rest.astype(full)
    grad = total[:, :width] + dot(high, router_ref[...]) + dot(rest, router_ref[...])
    mid, inverse = mid_ref[...], inv_ref[...]
    part_ref[...] = jnp.sum(grad * mid * inverse, axis=0, keepdims=True)
    grad = g_ref[index_ref[0]].astype(full) + norm_back(grad, mid, inverse, gain_ref[...])
    grad_ref[...] = grad
    message_ref[:, :width] = grad.astype(low)
    message_ref[:, width:] = cols[...].astype(low)


def attend_back_kernel(scale, pieces, index_ref, w_ref, probs_ref, keys_ref, values_ref, q_ref, raw_ref,
                       gain_ref, cos_ref, sin_ref, *refs):
    da_refs = refs[:pieces]
    kv_near_ref, kv_far_ref, dq_ref, part_ref, *message_refs, da_ref, acc = refs[pieces:]
    step = pl.program_id(0)
    tokens, head_dim = cos_ref.shape
    share = da_refs[0].shape[0]
    width = da_ref.shape[1]
    logit_cols = da_refs[0].shape[1] - width

    @pl.when(step == 0)
    def _():
        for i, ref in enumerate(da_refs):
            da_ref[i * share : (i + 1) * share] = ref[:, :width]
            for k, one in enumerate(message_refs):
                one[i * share : (i + 1) * share, :logit_cols] = ref[:, width:]
        for k, one in enumerate(message_refs):
            cols = one.shape[1] - logit_cols
            start = pl.multiple_of((index_ref[0] ^ k) * cols, 128)
            one[:, logit_cols:] = da_ref[:, pl.ds(start, cols)]
        acc[...] = jnp.zeros_like(acc)
        part_ref[...] = jnp.zeros_like(part_ref)

    dattn = dot(da_ref[...], w_ref[...], 1, 1).astype(low)
    heads = dattn.shape[1] // head_dim
    out_grad = jnp.concatenate(
        [dattn[:, h * head_dim : (h + 1) * head_dim] for h in range(heads)], axis=0
    )
    probs_low = probs_ref[...]
    probs = probs_low.astype(full)
    prob_grad = dot(out_grad, values_ref[...], 1, 1)
    inner = jnp.sum(probs * prob_grad, axis=-1, keepdims=True)
    score_grad = (probs * (prob_grad - inner)).astype(low)
    query_grad = (dot(score_grad, keys_ref[...]) * scale).astype(low).astype(full)
    acc[:, :head_dim] += dot(score_grad, q_ref[...], 0, 0)
    acc[:, head_dim:] += dot(probs_low, out_grad, 0, 0)
    gain = gain_ref[...]
    part = part_ref[...]
    for h in range(heads):
        cols = slice(h * head_dim, (h + 1) * head_dim)
        turned = rotate(query_grad[h * tokens : (h + 1) * tokens], cos_ref[...], -sin_ref[...])
        raw = raw_ref[:, cols]
        inverse = rms_scale(raw)
        part = part + jnp.sum(turned * raw * inverse, axis=0, keepdims=True)
        dq_ref[:, cols] = norm_back(turned, raw, inverse, gain).astype(low)
    part_ref[...] = part

    @pl.when(step == pl.num_programs(0) - 1)
    def _():
        near = kv_near_ref.shape[0]
        for ref, at in ((kv_near_ref, 0), (kv_far_ref, near)):
            ref[:, :head_dim] = (acc[at : at + near, :head_dim] * scale).astype(low)
            ref[:, head_dim:] = acc[at : at + near, head_dim:].astype(low)


def stack_rows(stack, at, row):
    for k in range(row.shape[1] // 128):
        stack[at + k : at + k + 1] = row[:, k * 128 : (k + 1) * 128]


def stack_split(stack, values):
    count = values.shape[0]
    high = values.astype(low).astype(full)
    stack[...] = jnp.zeros_like(stack)
    stack[:count] = high
    stack[count : 2 * count] = (values - high).astype(low).astype(full)


def tail_kernel(pieces, moe_part_ref, query_part_ref, dn_ref, dq_ref, raw_ref, kgain_ref, cos_ref, sin_ref, kw_ref, vw_ref, x_ref,
                inv_ref, *refs):
    kv_refs = refs[:pieces]
    own_ref, *rest_refs, proj_ref, gains_ref, values = refs[pieces:]
    total = kv_refs[0][...].astype(full)
    for ref in kv_refs[1:]:
        total = total + ref[...].astype(full)
    head_dim = raw_ref.shape[1]
    query_cols = dq_ref.shape[1]
    turned = rotate(total[:, :head_dim].astype(low).astype(full), cos_ref[...], -sin_ref[...])
    dv = total[:, head_dim:].astype(low)
    raw = raw_ref[...]
    inverse = rms_scale(raw)
    key_part = jnp.sum(turned * raw * inverse, axis=0, keepdims=True)
    dk = norm_back(turned, raw, inverse, kgain_ref[...]).astype(low)
    proj_ref[:, :query_cols] = dq_ref[...]
    proj_ref[:, query_cols : query_cols + head_dim] = dk
    proj_ref[:, query_cols + head_dim :] = dv
    grad = dn_ref[...] + dot(dk, kw_ref[...], 1, 1) + dot(dv, vw_ref[...], 1, 1)
    blocks, share, _ = x_ref.shape
    width = grad.shape[1]
    part = jnp.zeros((1, width), full)
    for i in range(blocks):
        one = grad[i * share : (i + 1) * share]
        x = x_ref[i].astype(full)
        part = part + jnp.sum(one * x * inv_ref[i * share : (i + 1) * share], axis=0, keepdims=True)
        if i == 0:
            own_ref[...] = one
        else:
            rest_refs[i - 1][:, :width] = one.astype(low)
    stack_rows(values, 0, part)
    stack_rows(values, width // 128, moe_part_ref[...])
    stack_rows(values, 2 * width // 128, query_part_ref[...])
    stack_rows(values, (2 * width + head_dim) // 128, key_part)
    stack_split(gains_ref, values[...])
    for ref in rest_refs:
        for j in range(gains_ref.shape[0] // share):
            cols = slice(width + j * 128, width + (j + 1) * 128)
            ref[:, cols] = gains_ref[j * share : (j + 1) * share].astype(low)


def output_kernel(a_near, a_far, b_near, b_far, out_ref):
    rows, cols = out_ref.shape
    far = b_far.shape[1] - cols
    out_ref[...] = dot(a_near[...], b_near[...], 0, 0) + dot(a_far[:, :rows], b_far[:, far:], 0, 0)


def projection_kernel(pieces, index_ref, a_near, a_far, b_near, b_far, query_ref, key_ref, value_ref, *refs):
    *gain_refs, b, parts = refs
    far = a_far.shape[1] - a_near.shape[1]
    each = a_near.shape[0] // pieces
    rows = b_near.shape[0] // pieces
    more = rows - each
    for i, b_ref in enumerate((b_near, b_far)):
        for k in range(pieces):
            at = i * pieces + k
            b[at * each : (at + 1) * each] = b_ref[k * rows : k * rows + each]
            for j in range(parts.shape[1] // more):
                cols = slice(j * 128, (j + 1) * 128)
                parts[index_ref[0] ^ (2 * k + i), j * more : (j + 1) * more] = b_ref[
                    k * rows + each : (k + 1) * rows, cols
                ].astype(full)
    gains = parts[0]
    for i in range(1, 2 * pieces):
        gains = gains + parts[i]
    count = sum(ref.shape[0] for ref in gain_refs)
    gains = gains[:count] + gains[count : 2 * count]
    at = 0
    for ref in gain_refs:
        ref[...] = gains[at : at + ref.shape[0]]
        at += ref.shape[0]
    half = pieces * each
    total = dot(a_near[...], b[:half], 0, 0) + dot(a_far[:, far:], b[half:], 0, 0)
    cols, more = query_ref.shape[1], key_ref.shape[1]
    query_ref[...] = total[:, :cols]
    key_ref[...] = total[:, cols : cols + more]
    value_ref[...] = total[:, cols + more :]


def router_kernel(index_ref, rows_any, near_ref, far_ref, out_ref, rows, grads, sems):
    part_count, groups, inner, share, _ = rows_any.shape
    copies = []
    for p in range(part_count):
        for c in range(groups):
            half = groups // 2
            mask = 2 * (c % half) + c // half
            for w in range(inner):
                to = (index_ref[0] ^ mask) * (part_count * inner) + (index_ref[1] ^ (p * inner + w))
                copy = pltpu.make_async_copy(rows_any.at[p, c, w], rows.at[to], sems.at[len(copies)])
                copy.start()
                copies.append(copy)
                grad_ref = near_ref if c < half else far_ref
                at = ((c % half) * (part_count * inner) + p * inner + w) * share
                grads[to] = grad_ref[at : at + share, : grads.shape[2]]
    for copy in copies:
        copy.wait()
    count = rows.shape[0] * share
    total = dot(grads[...].reshape(count, grads.shape[2]), rows[...].reshape(count, rows.shape[2]), 0, 0)
    experts = out_ref.shape[0]
    out_ref[...] = total[:experts] + total[experts : 2 * experts]


def place_kernel(pieces, index_ref, *refs):
    piece_refs, out_refs = refs[:pieces], refs[pieces:]
    width = out_refs[0].shape[2]
    for i, ref in enumerate(piece_refs):
        for j, out_ref in enumerate(out_refs):
            out_ref[index_ref[0] ^ i] = ref[:, j * width : (j + 1) * width]


def place_rows(index, pieces, width, count, **more):
    share = pieces[0].shape[0]
    return kernel_call(
        functools.partial(place_kernel, len(pieces)),
        [shape_of((len(pieces), share, width), pieces[0].dtype)] * count,
        [in_smem] + [in_vmem] * len(pieces),
        [index.reshape(1), *pieces],
        **more,
    )


def gather_wt(array):
    return [array] + [swap(array, "wt", m) for m in range(1, lax.axis_size("wt"))]


def near_ctx(array):
    return [array] + [swap(array, "ctx", 2 * k) for k in range(1, lax.axis_size("ctx") // 2)]


def far_ctx(arrays):
    return [swap(one, "ctx", 1) for one in arrays]


def split_low(array):
    high = array.astype(low)
    return high, (array - high.astype(full)).astype(low)


def on_device(
    tokens,
    cotangent,
    routes,
    attn_gain,
    query_gain,
    key_gain,
    w_query,
    key_weight,
    value_weight,
    w_output,
    moe_gain,
    w_router,
    w_gate_up,
    w_down,
):
    _, pair_len, width = tokens.shape
    head_dim = query_gain.shape[0]
    query_cols = w_query.shape[1]
    heads = query_cols // head_dim
    share, top_count = routes.shape
    experts = w_router.shape[1]
    ctx_count = lax.axis_size("ctx")
    wt_count = lax.axis_size("wt")
    half = ctx_count // 2
    ctx_index = lax.axis_index("ctx")
    wt_index = lax.axis_index("wt")
    my_expert = ctx_index * wt_count + wt_index
    scale = head_dim ** (-0.5)
    head_step = 2
    parts = 2
    inner = wt_count // parts
    mask_cols = -(-experts // 128) * 128
    extra_cols = -(-2 * experts // 128) * 128
    index = wt_index.reshape(1)
    chip = (ctx_index >> 1).reshape(1)
    core = (ctx_index & 1).reshape(1)
    router = w_router.T

    def plane_swap(blocks):
        return [swap(blocks[k], "ctx", 2 * k) for k in range(1, half)]

    def joined(pieces):
        return jnp.concatenate(pieces, axis=0) if len(pieces) > 1 else pieces[0]

    def both(pieces, after=()):
        near = join(pieces, after)
        return [near, swap(near, "ctx", 1)]


    place = jnp.arange(pair_len, dtype=jnp.int32)
    offsets = ((place // share) ^ wt_index) * share + place % share
    near_masks = 2 * jnp.arange(half, dtype=jnp.int32)
    masks = jnp.concatenate([near_masks, near_masks + 1])
    own_positions = mirrored(ctx_index, offsets, ctx_count, pair_len // 2)
    key_positions = mirrored(
        (ctx_index ^ masks)[:, None], offsets[None, :], ctx_count, pair_len // 2
    ).reshape(1, -1)
    row_positions = jnp.tile(own_positions, head_step).reshape(-1, 1)
    frequency = rope_base ** (-2.0 * jnp.arange(head_dim // 2, dtype=full) / head_dim)
    angles = own_positions.astype(full)[:, None] * frequency[None, :]
    cosine, sine = jnp.cos(angles), jnp.sin(angles)
    cosine = jnp.concatenate([cosine, cosine], axis=1)
    sine = jnp.concatenate([-sine, sine], axis=1)

    expert_ids = jnp.arange(mask_cols, dtype=jnp.int32)
    own_mask = jnp.any(routes[:, :, None] == expert_ids, axis=1).astype(low)
    block_cols = width // ctx_count
    token_rows, normed_one, inverse_one, raw_key, *kv_messages = kernel_call(
        front_kernel,
        [
            shape_of((wt_count, share, width), low),
            shape_of((pair_len, width), low),
            shape_of((pair_len, 1), full),
            shape_of((pair_len, head_dim), full),
        ]
        + [shape_of((pair_len, 2 * head_dim + 2 * block_cols), low)] * half,
        [in_smem] + [in_vmem] * 7,
        [
            jnp.stack([wt_index, ctx_index >> 1]),
            tokens.reshape(wt_count, share, width),
            attn_gain.reshape(1, -1),
            key_weight,
            value_weight,
            key_gain.reshape(1, -1),
            cosine,
            sine,
        ],
    )

    kv_near = [kv_messages[0]] + plane_swap(kv_messages)
    raw_query, queries = kernel_call(
        query_kernel,
        [shape_of((pair_len, query_cols), full), shape_of((heads * pair_len, head_dim), low)],
        [
            pl.BlockSpec((pair_len, width), lambda i: (0, 0)),
            pl.BlockSpec((width, head_step * head_dim), lambda i: (0, i)),
            pl.BlockSpec((1, head_dim), lambda i: (0, 0)),
            pl.BlockSpec((pair_len, head_dim), lambda i: (0, 0)),
            pl.BlockSpec((pair_len, head_dim), lambda i: (0, 0)),
        ],
        [normed_one, w_query, query_gain.reshape(1, -1), cosine, sine],
        grid=(heads // head_step,),
        out_specs=[
            pl.BlockSpec((pair_len, head_step * head_dim), lambda i: (0, i)),
            pl.BlockSpec((head_step * pair_len, head_dim), lambda i: (i, 0)),
        ],
    )

    grad_near = near_ctx(cotangent[0])
    kv_here, normed_keep, kv_give = deal(core, kv_near, 2 * head_dim)
    kv_got = swap(kv_give, "ctx", 1)
    kv_pieces = [kv_here, kv_got]

    total_keys = ctx_count * pair_len
    attn_rows, probs, keys, values, branch_own, *branch_rest = kernel_call(
        functools.partial(attend_kernel, scale, 2),
        [
            shape_of((pair_len, query_cols), low),
            shape_of((heads * pair_len, total_keys), low),
            shape_of((total_keys, head_dim), low),
            shape_of((total_keys, head_dim), low),
            shape_of((share, width), full),
        ]
        + [shape_of((share, width), low)] * (wt_count - 1),
        [
            pl.BlockSpec((head_step * pair_len, 1), lambda i: (0, 0)),
            pl.BlockSpec((1, total_keys), lambda i: (0, 0)),
            pl.BlockSpec((head_step * pair_len, head_dim), lambda i: (i, 0)),
            in_any,
        ]
        + [pl.BlockSpec(one.shape, lambda i: (0, 0)) for one in kv_pieces],
        [row_positions, key_positions, queries, w_output, *kv_pieces],
        grid=(heads // head_step,),
        out_specs=[
            pl.BlockSpec((pair_len, query_cols), lambda i: (0, 0)),
            pl.BlockSpec((head_step * pair_len, total_keys), lambda i: (i, 0)),
            pl.BlockSpec((total_keys, head_dim), lambda i: (0, 0)),
            pl.BlockSpec((total_keys, head_dim), lambda i: (0, 0)),
        ]
        + [pl.BlockSpec((share, width), lambda i: (0, 0))] * wt_count,
        scratch_shapes=[
            pltpu.VMEM((heads // head_step, pair_len, head_step * head_dim), low),
            pltpu.VMEM(w_output.shape, low),
            pltpu.SemaphoreType.DMA,
        ],
    )
    branch_rest, branch_own, attn_rows = fence(branch_rest, branch_own, attn_rows)
    received = [swap(branch_rest[m - 1], "wt", m) for m in range(1, wt_count)]
    mid_rows, inverse_two, message = kernel_call(
        mid_kernel,
        [
            shape_of((share, width), full),
            shape_of((share, 1), full),
            shape_of((share, width + mask_cols), low),
        ],
        [in_vmem] * (3 + wt_count),
        [token_rows, moe_gain.reshape(1, -1), own_mask, branch_own, *received],
    )
    residual_rows = token_rows[0].astype(full)

    first = join([message] + [swap(message, "wt", m) for m in range(1, inner)])
    others = [swap(message, "wt", m) for m in range(inner, wt_count)]
    grads = [one.reshape(half, wt_count, share, width) for one in both(grad_near, first)]
    chunks = pair_len // (inner * share)
    second = kernel_call(
        pack_kernel,
        shape_of((inner * share, width + mask_cols + chunks * query_cols), low),
        [in_vmem] * (1 + inner),
        [attn_rows, *others],
    )
    rows_first = both(near_ctx(first), second)
    near_second = near_ctx(second)
    places = jnp.stack([my_expert, wt_index])
    sums_cols = width + extra_cols
    most = max(2, share * top_count * 5 // (4 * experts) + 1)
    results, into = run_expert(
        0, parts, inner, rows_first, grads, router, w_gate_up, w_down, places, None, sums_cols,
        most,
    )
    results, into, near_second = fence(results, into, near_second)
    rows_second, attn_near = kernel_call(
        unpack_kernel,
        [shape_of((half * inner * share, width + mask_cols), low), shape_of((half * pair_len, query_cols), low)],
        [in_vmem] * half,
        near_second,
    )
    rows_second = [rows_second, swap(rows_second, "ctx", 1)]
    attn_got = swap(attn_near, "ctx", 1)

    def split_parts(near, far_sent):
        cols = near.shape[1]
        total = (near + far_sent).reshape(half, inner * share, cols)
        return [total[k] for k in range(half)]

    def plane_sum(blocks, received):
        total = blocks[0].astype(full)
        for one in received:
            total = total + one.astype(full)
        return total

    def wt_parts(sums):
        return [one[w * share : (w + 1) * share] for one in sums for w in range(inner)]

    back_blocks = [split_parts(results[0], swap(results[1], "ctx", 1))]
    moe_blocks = [split_parts(results[2], swap(results[3], "ctx", 1))]
    rows_second, back_blocks, into = fence(rows_second, back_blocks, into)
    back_received = [plane_swap(back_blocks[0])]
    results, into = run_expert(
        1, parts, inner, rows_second, grads, router, w_gate_up, w_down, places, into, sums_cols,
        most,
    )

    results, into, back_received = fence(results, into, back_received)
    back_blocks.append(split_parts(results[0], swap(results[1], "ctx", 1)))
    back_blocks, moe_far, into = fence(back_blocks, results[3], into)
    rows_all, rows_drawn, hidden, gate_up_grad, expert_grad = into
    back_received.append(plane_swap(back_blocks[1]))
    moe_far = swap(moe_far, "ctx", 1)
    w_gate_up_grad = dot(rows_drawn, gate_up_grad, 0, 0)
    w_down_grad = dot(hidden, expert_grad, 0, 0)
    back_received, moe_far, w_gate_up_grad, w_down_grad, attn_rows = fence(
        back_received, moe_far, w_gate_up_grad, w_down_grad, attn_rows
    )
    moe_blocks.append(split_parts(results[2], moe_far))
    moe_received = [plane_swap(moe_blocks[0])]
    sums = wt_parts([plane_sum(b, r) for b, r in zip(back_blocks, back_received)])
    sums_low = [one.astype(low) for one in sums[1:]]
    received = [swap(one, "wt", m + 1) for m, one in enumerate(sums_low)]
    mid_grad, moe_gain_part, mid_message = kernel_call(
        mid_back_kernel,
        [
            shape_of((share, width), full),
            shape_of((1, width), full),
            shape_of((share, width + extra_cols), low),
        ],
        [in_smem] + [in_vmem] * (7 + wt_count),
        [
            index, sums[0], message, own_mask, router, mid_rows, inverse_two, moe_gain.reshape(1, -1),
            cotangent.reshape(wt_count, share, width), *received,
        ],
        scratch_shapes=[pltpu.VMEM((share, extra_cols), full)],
    )

    mid_pieces = gather_wt(mid_message)
    moe_received.append(plane_swap(moe_blocks[1]))
    mid_pieces, moe_received = fence(mid_pieces, moe_received)

    moe_sums = wt_parts([plane_sum(b, r) for b, r in zip(moe_blocks, moe_received)])
    moe_low = [one.astype(low) for one in moe_sums[1:]]
    moe_low, mid_pieces = fence(moe_low, mid_pieces)
    moe_received = [swap(one, "wt", m + 1) for m, one in enumerate(moe_low)]
    kv_part_near, kv_part_far, query_grad, query_gain_part, *logits_messages, _ = kernel_call(
        functools.partial(attend_back_kernel, scale, wt_count),
        [
            shape_of((total_keys // 2, 2 * head_dim), low),
            shape_of((total_keys // 2, 2 * head_dim), low),
            shape_of((pair_len, query_cols), low),
            shape_of((1, head_dim), full),
        ]
        + [shape_of((pair_len, extra_cols + 2 * block_cols), low)] * half
        + [shape_of((pair_len, width), low)],
        [
            in_smem,
            pl.BlockSpec((head_step * head_dim, width), lambda i: (i, 0)),
            pl.BlockSpec((head_step * pair_len, total_keys), lambda i: (i, 0)),
            pl.BlockSpec((total_keys, head_dim), lambda i: (0, 0)),
            pl.BlockSpec((total_keys, head_dim), lambda i: (0, 0)),
            pl.BlockSpec((head_step * pair_len, head_dim), lambda i: (i, 0)),
            pl.BlockSpec((pair_len, head_step * head_dim), lambda i: (0, i)),
            pl.BlockSpec((1, head_dim), lambda i: (0, 0)),
            pl.BlockSpec((pair_len, head_dim), lambda i: (0, 0)),
            pl.BlockSpec((pair_len, head_dim), lambda i: (0, 0)),
        ]
        + [pl.BlockSpec((share, width + extra_cols), lambda i: (0, 0))] * wt_count,
        [
            chip, w_output, probs, keys, values, queries, raw_query, query_gain.reshape(1, -1),
            cosine, sine, *mid_pieces,
        ],
        grid=(heads // head_step,),
        out_specs=[
            pl.BlockSpec((total_keys // 2, 2 * head_dim), lambda i: (0, 0)),
            pl.BlockSpec((total_keys // 2, 2 * head_dim), lambda i: (0, 0)),
            pl.BlockSpec((pair_len, head_step * head_dim), lambda i: (0, i)),
            pl.BlockSpec((1, head_dim), lambda i: (0, 0)),
        ]
        + [pl.BlockSpec((pair_len, extra_cols + 2 * block_cols), lambda i: (0, 0))] * half
        + [pl.BlockSpec((pair_len, width), lambda i: (0, 0))],
        scratch_shapes=[pltpu.VMEM((total_keys, 2 * head_dim), full)],
    )

    kv_part_near, kv_part_far, query_grad, moe_received, logits_messages = fence(
        kv_part_near, kv_part_far, query_grad, moe_received, logits_messages
    )
    kv_near = (kv_part_near + swap(kv_part_far, "ctx", 1)).reshape(half, pair_len, 2 * head_dim)
    kv_near = [kv_near[k] for k in range(half)]
    out_rows = (mid_rows + plane_sum(moe_sums, moe_received)).astype(low)
    kv_near, query_grad, out_rows = fence(kv_near, query_grad, out_rows)
    kv_received = plane_swap(kv_near)
    out_pieces = gather_wt(out_rows)
    query_term = dot(query_grad, w_query, 1, 1)
    kv_received, query_term = fence(kv_received, query_term)
    gain_rows = 2 * width // 128 + 2 * head_dim // 128
    gain_blocks = -(-2 * gain_rows // share)
    one_own, *tail_results = kernel_call(
        functools.partial(tail_kernel, half),
        [shape_of((share, width), full)]
        + [shape_of((share, width + gain_blocks * 128), low)] * (wt_count - 1)
        + [
            shape_of((pair_len, query_cols + 2 * head_dim), low),
            shape_of((gain_blocks * share, 128), full),
        ],
        [in_vmem] * (12 + half),
        [
            moe_gain_part.reshape(1, -1), query_gain_part, query_term, query_grad, raw_key,
            key_gain.reshape(1, -1), cosine, sine, key_weight, value_weight, token_rows, inverse_one,
            kv_near[0], *kv_received,
        ],
        after=[attn_got, out_pieces],
        through=logits_messages,
        scratch_shapes=[pltpu.VMEM((gain_rows, 128), full)],
    )
    one_rest, (projection_own, gains) = tail_results[: wt_count - 1], tail_results[wt_count - 1 : wt_count + 1]
    logits_messages = tail_results[wt_count + 1 :]
    received = [swap(one, "wt", m + 1) for m, one in enumerate(one_rest)]
    logits_near = [logits_messages[0]] + plane_swap(logits_messages)
    logits_own, mid_keep, logits_give = deal(core, logits_near, extra_cols)
    logits_got = swap(logits_give, "ctx", 1)
    message_rows = pair_len + 16
    last_rows, projection = kernel_call(
        last_kernel,
        [shape_of((share, width), low), shape_of((message_rows, query_cols + 2 * head_dim), low)],
        [in_smem] + [in_vmem] * (6 + wt_count),
        [
            index, token_rows, inverse_one, attn_gain.reshape(1, -1), mid_grad, projection_own,
            gains, one_own, *received,
        ],
        after=logits_near,
        scratch_shapes=[
            pltpu.VMEM((wt_count, gain_blocks * share, 128), full),
            pltpu.VMEM((-(-2 * gain_rows // 16) * 16, 128), full),
        ],
    )

    last_pieces = gather_wt(last_rows)
    projection_near = near_ctx(projection)
    router_grad = kernel_call(
        router_kernel,
        shape_of((experts, width), full),
        [in_smem, in_any, in_vmem, in_vmem],
        [
            jnp.stack([ctx_index, wt_index]),
            rows_all.reshape(parts, ctx_count, inner, share, width),
            logits_own,
            logits_got,
        ],
        scratch_shapes=[
            pltpu.VMEM((ctx_count * wt_count, share, width), low),
            pltpu.VMEM((ctx_count * wt_count, share, extra_cols), low),
            pltpu.SemaphoreType.DMA((ctx_count * wt_count,)),
        ],
    )
    w_output_grad = kernel_call(
        output_kernel,
        shape_of((query_cols, block_cols), full),
        [in_vmem] * 4,
        [attn_near, attn_got, mid_keep, logits_got],
    )
    w_query_grad, w_key_grad, w_value_grad, *gains = kernel_call(
        functools.partial(projection_kernel, half),
        [
            shape_of((block_cols, query_cols), full),
            shape_of((block_cols, head_dim), full),
            shape_of((block_cols, head_dim), full),
        ]
        + [shape_of((size // 128, 128), full) for size in (width, width, head_dim, head_dim)],
        [in_smem] + [in_vmem] * 4,
        [ctx_index.reshape(1), normed_keep, kv_got, *both(projection_near, [last_pieces[1:], w_output_grad, router_grad])],
        scratch_shapes=[
            pltpu.VMEM((total_keys, query_cols + 2 * head_dim), low),
            pltpu.VMEM((ctx_count, -(-2 * gain_rows // 16) * 16, 128), full),
        ],
    )
    attn_gain_grad, moe_gain_grad, query_gain_grad, key_gain_grad = [one.reshape(-1) for one in gains]
    (block_out,) = place_rows(index, out_pieces, width, 1)
    (tokens_grad,) = place_rows(
        index, last_pieces, width, 1, after=[router_grad, w_output_grad, w_query_grad]
    )
    w_router_grad = router_grad.T

    return (
        block_out.reshape(1, pair_len, width),
        tokens_grad.reshape(1, pair_len, width),
        attn_gain_grad,
        query_gain_grad,
        key_gain_grad,
        w_query_grad,
        w_key_grad,
        w_value_grad,
        w_output_grad,
        moe_gain_grad,
        w_router_grad,
        w_gate_up_grad[None],
        w_down_grad[None],
    )


def solution(mesh):
    in_specs = (
        P(None, "ctx", None),
        P(None, "ctx", None),
        P(("ctx", "wt"), None),
        P(),
        P(),
        P(),
        P(None, "wt"),
        P(None, "wt"),
        P(None, "wt"),
        P("wt", None),
        P(),
        P(),
        P(("ctx", "wt"), None, None),
        P(("ctx", "wt"), None, None),
    )
    out_specs = (
        P(None, "ctx", None),
        P(None, "ctx", None),
        P(),
        P(),
        P(),
        P("ctx", "wt"),
        P("ctx", "wt"),
        P("ctx", "wt"),
        P("wt", "ctx"),
        P(),
        P(),
        P(("ctx", "wt"), None, None),
        P(("ctx", "wt"), None, None),
    )
    return jax.shard_map(
        on_device, mesh=mesh, in_specs=in_specs, out_specs=out_specs, check_vma=False
    )
```
